512 devices in a mesh: section: 16 (over x, z_hi), seq: 16 (over z_lo, y), mp: 2 (over core).
Axes of the slice: x: 4, y: 4, z: 16 (z_hi: 4, z_lo: 4; z = z_hi * 4 + z_lo), core: 2. Of those that a mesh axis runs over, the one named last changes fastest.
Arguments:
- query_rows: bfloat16 [16, 2048, 2048], P('section', 'seq', 'mp'), may hold values from -150 to 150
- key_row_matrix: bfloat16 [16, 2048, 1024], P('section', 'seq', 'mp'), may hold values from -13 to 13
- value_row_matrix: bfloat16 [16, 2048, 1024], P('section', 'seq', 'mp'), may hold values from -6 to 6
- out_grad: bfloat16 [16, 2048, 2048], P('section', 'seq', 'mp'), may hold values from -24 to 24
- w_query: bfloat16 [16, 5376, 2048], P('section', 'seq', 'mp'), may hold values from -0.078125 to 0.078125
- key_weight: bfloat16 [16, 5376, 1024], P('section', 'seq', 'mp'), may hold values from -0.078125 to 0.078125
- value_weight: bfloat16 [16, 5376, 1024], P('section', 'seq', 'mp'), may hold values from -0.078125 to 0.078125
- doc_ids: int32 [16, 2048], P('section'), may hold values from 0 to 5, never falling along the last dimension, each value on 1 to 682 neighbouring positions
Outputs:
- upstream: bfloat16 [16, 2048, 5376], P('section', None, ('seq', 'mp'))
The draws below stay inside these ranges and needn't reach their ends.
All inputs are finite; a program needn't handle non-finite values.
Results may differ from the reference program's by a relative error of at most 0.0071.
Values may be sent and summed in bfloat16 or wider, within the bound.
A program may use at most 64 MiB of HBM per device.

```python
import math
import jax
import jax.numpy as jnp
import numpy as np
from jax import lax

MODEL_WIDTH = 5376
QUERY_HEADS = 16
KEY_VALUE_HEADS = 8
HEAD_WIDTH = 128
WINDOW = 512
DOCS = 6
CASCADE_PARTS = 16
BATCH_TOKENS = 2048
DOC_MOST = 682


def make_pair(key):
    key_base = jax.random.fold_in(key, 101)
    key_scale = jax.random.fold_in(key, 102)
    query_base = jax.random.fold_in(key, 103)
    query_scale = jax.random.fold_in(key, 104)
    key_rows_shaped = (CASCADE_PARTS, BATCH_TOKENS, KEY_VALUE_HEADS * HEAD_WIDTH)
    base_keys = jnp.clip(jax.random.normal(key_base, key_rows_shaped, jnp.float32), -4.0, 4.0)
    row_scale = jnp.exp(jax.random.uniform(key_scale, (CASCADE_PARTS, BATCH_TOKENS, 1), jnp.float32, -1.15, 1.15))
    base_queries = jnp.clip(jax.random.normal(query_base, (CASCADE_PARTS, BATCH_TOKENS, QUERY_HEADS * HEAD_WIDTH), jnp.float32), -4.0, 4.0)
    base_queries = base_queries * jnp.exp(jax.random.uniform(query_scale, (CASCADE_PARTS, BATCH_TOKENS, 1), jnp.float32, -1.15, 1.15))
    key_rows_scaled = base_keys * row_scale
    queries = base_queries
    return (queries, key_rows_scaled)


def draw_query_rows(key, part):
    return make_pair(key)[0].astype(jnp.bfloat16)


def draw_key_row_matrix(key, part):
    return make_pair(key)[1].astype(jnp.bfloat16)


def shard_levels(key, extent, split, low, top_value):
    def one(dim, shards_of):
        steps = jax.random.uniform(jax.random.fold_in(jax.random.fold_in(key, 6), dim), (shards_of,), jnp.float32, low / len(split), top_value / len(split))
        return jnp.repeat(jnp.exp(steps), extent[dim] // shards_of).reshape((-1,) + (1,) * (len(extent) - dim - 1))

    gain = one(*split[0])
    for cut in split[1:]:
        gain = gain * one(*cut)
    return gain


def length_profile(count, total, bound, skew):
    portions = [(1 << 20) // math.isqrt(standing ** skew) + 1 for standing in range(2, count + 1)]
    surplus, given = total - bound - (count - 1), [1] * (count - 1)
    while surplus > 0:
        candidates = [i for i in range(count - 1) if given[i] < bound]
        mass, budget = sum([portions[i] for i in candidates]), surplus
        for i in candidates:
            more = min(bound - given[i], max(1, budget * portions[i] // mass), surplus)
            given[i] = given[i] + more
            surplus = surplus - more
    return np.array([bound] + given)


def ragged(rng, count, total, reach, slope):
    if count == 2:
        one = jax.random.randint(rng, (), max(1, total - reach), min(reach, total - 1) + 1)
        return jnp.stack([one, total - one])
    sizes = jnp.asarray(length_profile(count, total, reach, slope), jnp.int32)
    pairs = (count - 1) // 2
    giver, receiver = sizes[1:1 + 2 * pairs:2], sizes[2:2 + 2 * pairs:2]
    room = jnp.minimum(giver - 1, reach - receiver)
    shifted = jax.random.randint(jax.random.fold_in(rng, 1), (pairs,), 0, 1 << 20) % (room + 1)
    sizes = sizes.at[1:1 + 2 * pairs:2].set(giver - shifted).at[2:2 + 2 * pairs:2].set(receiver + shifted)
    return sizes[jax.random.permutation(jax.random.fold_in(rng, 2), count)]


def noise(own_key, extent, spread, bound, split=(), held_as=jnp.bfloat16):
    values = jax.random.normal(own_key, extent, jnp.float32) * spread
    if len(split) > 0:
        values = shard_levels(own_key, extent, split, -0.22, 0.18) * values
    return jnp.clip(values, min=-bound, max=bound).astype(held_as)


def setup_inputs(seed: int = 0) -> dict:
    key_list = jax.random.split(jax.random.key(seed), 9)
    query_rows = draw_query_rows(jax.random.fold_in(key_list[8], 71), 0)
    key_row_matrix = draw_key_row_matrix(jax.random.fold_in(key_list[8], 71), 0)
    value_row_matrix = noise(key_list[2], (CASCADE_PARTS, BATCH_TOKENS, KEY_VALUE_HEADS * HEAD_WIDTH), 1.0, 6.0, ((0, 16), (1, 16), (2, 2)))
    out_grad = noise(key_list[3], (CASCADE_PARTS, BATCH_TOKENS, QUERY_HEADS * HEAD_WIDTH), 4.0, 24.0, ((0, 16), (1, 16), (2, 2)))
    w_query = noise(key_list[4], (CASCADE_PARTS, MODEL_WIDTH, QUERY_HEADS * HEAD_WIDTH), MODEL_WIDTH ** -0.5, 0.078125, ((0, 16), (1, 16), (2, 2)))
    key_weight = noise(key_list[5], (CASCADE_PARTS, MODEL_WIDTH, KEY_VALUE_HEADS * HEAD_WIDTH), MODEL_WIDTH ** -0.5, 0.078125, ((0, 16), (1, 16), (2, 2)))
    value_weight = noise(key_list[6], (CASCADE_PARTS, MODEL_WIDTH, KEY_VALUE_HEADS * HEAD_WIDTH), MODEL_WIDTH ** -0.5, 0.078125, ((0, 16), (1, 16), (2, 2)))
    doc_ids = jax.vmap(lambda own: jnp.searchsorted(jnp.cumsum(ragged(own, DOCS, BATCH_TOKENS, DOC_MOST, 1)), jnp.arange(BATCH_TOKENS), side="right"))(jax.random.split(key_list[7], CASCADE_PARTS)).reshape((CASCADE_PARTS, BATCH_TOKENS)).astype(jnp.int32)
    return dict(query_rows=query_rows, key_row_matrix=key_row_matrix, value_row_matrix=value_row_matrix, out_grad=out_grad, w_query=w_query, key_weight=key_weight, value_weight=value_weight, doc_ids=doc_ids)


def section_backward(query_rows, key_row_matrix, value_row_matrix, out_grad, w_query, key_weight, value_weight, doc_ids):
    group_width = QUERY_HEADS // KEY_VALUE_HEADS
    scaling = 1.0 / math.sqrt(HEAD_WIDTH)
    position = jnp.arange(BATCH_TOKENS, dtype=jnp.int32)
    offset = position[:, None] - position[None, :]
    allowed = (doc_ids[:, None] == doc_ids[None, :]) & (offset >= 0) & (offset < WINDOW)
    query_heads = query_rows.reshape(BATCH_TOKENS, QUERY_HEADS, HEAD_WIDTH).transpose(1, 0, 2)
    key_head_rows = key_row_matrix.reshape(BATCH_TOKENS, KEY_VALUE_HEADS, HEAD_WIDTH).transpose(1, 0, 2)
    value_head_rows = value_row_matrix.reshape(BATCH_TOKENS, KEY_VALUE_HEADS, HEAD_WIDTH).transpose(1, 0, 2)
    grad_heads = out_grad.reshape(BATCH_TOKENS, QUERY_HEADS, HEAD_WIDTH).transpose(1, 0, 2)

    def one_head(head_index):
        query_now = query_heads[head_index]
        key_now = key_head_rows[head_index // group_width]
        value_now = value_head_rows[head_index // group_width]
        grad_now = grad_heads[head_index]
        scores = jnp.dot(query_now, key_now.T, preferred_element_type=jnp.float32) * scaling
        scores = jnp.where(allowed, scores, -jnp.inf)
        row_max = lax.optimization_barrier(jnp.max(scores, axis=1, keepdims=True))
        raised = jnp.exp(scores - row_max)
        weights_full = raised / lax.optimization_barrier(jnp.sum(raised, axis=1, keepdims=True))
        weights_half = weights_full.astype(jnp.bfloat16)
        attended = jnp.dot(weights_half, value_now, preferred_element_type=jnp.float32)
        delta_row = lax.optimization_barrier(jnp.sum(grad_now.astype(jnp.float32) * attended, axis=1))
        grad_weights = jnp.dot(grad_now, value_now.T, preferred_element_type=jnp.float32)
        grad_scores = (weights_full * (grad_weights - delta_row[:, None])).astype(jnp.bfloat16)
        grad_query = (jnp.dot(grad_scores, key_now, preferred_element_type=jnp.float32) * scaling).astype(jnp.bfloat16)
        key_gradient = jnp.dot(grad_scores.T, query_now, preferred_element_type=jnp.float32) * scaling
        value_gradient = jnp.dot(weights_half.T, grad_now, preferred_element_type=jnp.float32)
        return (grad_query, key_gradient, value_gradient)
    grad_query, key_gradient, value_gradient = lax.map(one_head, jnp.arange(QUERY_HEADS, dtype=jnp.int32))
    key_gradient = key_gradient.reshape(KEY_VALUE_HEADS, group_width, BATCH_TOKENS, HEAD_WIDTH).sum(axis=1).astype(jnp.bfloat16)
    value_gradient = value_gradient.reshape(KEY_VALUE_HEADS, group_width, BATCH_TOKENS, HEAD_WIDTH).sum(axis=1).astype(jnp.bfloat16)
    query_cols = grad_query.transpose(1, 0, 2).reshape(BATCH_TOKENS, QUERY_HEADS * HEAD_WIDTH)
    key_columns = key_gradient.transpose(1, 0, 2).reshape(BATCH_TOKENS, KEY_VALUE_HEADS * HEAD_WIDTH)
    value_columns = value_gradient.transpose(1, 0, 2).reshape(BATCH_TOKENS, KEY_VALUE_HEADS * HEAD_WIDTH)
    grad_matrix = jnp.concatenate([query_cols, key_columns, value_columns], axis=1)
    weights_all = jnp.concatenate([w_query, key_weight, value_weight], axis=1)
    product = lax.dot_general(grad_matrix, weights_all, (((1,), (1,)), ((), ())), preferred_element_type=jnp.float32)
    return product.astype(jnp.bfloat16)

def reference(query_rows, key_row_matrix, value_row_matrix, out_grad, w_query, key_weight, value_weight, doc_ids):

    def per_section(section_inputs):
        return section_backward(section_inputs[0], section_inputs[1], section_inputs[2], section_inputs[3], section_inputs[4], section_inputs[5], section_inputs[6], section_inputs[7])
    grad_input = lax.map(per_section, (query_rows, key_row_matrix, value_row_matrix, out_grad, w_query, key_weight, value_weight, doc_ids))
    return jnp.roll(grad_input, -1, axis=0)
```

```python
from functools import reduce
import math

import jax
import jax.numpy as jnp
from jax import lax
from jax.experimental import pallas as pl
from jax.experimental.pallas import tpu as pltpu
from jax.sharding import PartitionSpec as P

HEAD_WIDTH = 128
WINDOW = 512
RING = 4
MESH = pl.DeviceIdType.MESH


def from_behind(shard, axis, by):
    size = lax.axis_size(axis)
    pairs = [(i, i + by) for i in range(size) if 0 <= i + by < size]
    return lax.ppermute(shard, axis, pairs)


NT = (((1,), (1,)), ((), ()))


def spread_kernel(
    grad_query_ref,
    grad_kv_ref,
    w_query_ref,
    key_weight_ref,
    value_weight_ref,
    out_ref,
    held,
    part,
    part_in,
    ready,
    landed,
    own_sem,
    up_send,
    up_recv,
    down_send,
    down_recv,
    right_send,
    right_recv,
    left_send,
    left_recv,
    far_right_send,
    far_right_recv,
    far_left_send,
    far_left_recv,
    core_send,
    core_recv,
    section_send,
    section_recv,
):
    seq_place = lax.axis_index("seq")
    core = lax.axis_index("mp")
    section = lax.axis_index("section")
    section_count = lax.axis_size("section")
    run = seq_place // RING
    turn = lax.rem(seq_place, RING)
    right = run * RING + lax.rem(turn + 1, RING)
    left = run * RING + lax.rem(turn + RING - 1, RING)
    back_section = lax.rem(section + section_count - 1, section_count)
    next_section = lax.rem(section + 1, section_count)
    rows = held.shape[2]
    half = rows // 2
    kv_cols = key_weight_ref.shape[1]
    width = w_query_ref.shape[0] // 2

    barrier = pltpu.get_barrier_semaphore()
    for place in (right, left):
        pl.semaphore_signal(barrier, inc=1, device_id={"seq": place}, device_id_type=MESH)
    pl.semaphore_signal(barrier, inc=1, device_id={"mp": 1 - core}, device_id_type=MESH)
    pl.semaphore_signal(barrier, inc=1, device_id={"section": back_section}, device_id_type=MESH)
    pl.semaphore_signal(barrier, inc=1, device_id={"section": next_section}, device_id_type=MESH)

    @pl.when(run < RING - 1)
    def _():
        pl.semaphore_signal(barrier, inc=1, device_id={"seq": seq_place + RING}, device_id_type=MESH)

    @pl.when(run > 0)
    def _():
        pl.semaphore_signal(barrier, inc=1, device_id={"seq": seq_place - RING}, device_id_type=MESH)

    in_line = (run > 0).astype(jnp.int32) + (run < RING - 1).astype(jnp.int32)
    pl.semaphore_wait(barrier, 5 + in_line)

    def own_copy(piece):
        source = grad_query_ref if piece == 0 else grad_kv_ref
        return pltpu.make_async_copy(source, held.at[piece, seq_place], own_sem.at[piece])

    def shard_copy(piece, owner, to, send, recv, line):
        block = held.at[piece, owner]
        return pltpu.make_async_remote_copy(
            src_ref=block,
            dst_ref=block,
            send_sem=send.at[piece, line],
            recv_sem=recv.at[piece, line],
            device_id={"seq": to},
            device_id_type=MESH,
        )

    def half_copy(piece, owner, start, to, send, recv, line):
        block = held.at[piece, owner, pl.ds(start, half)]
        return pltpu.make_async_remote_copy(
            src_ref=block,
            dst_ref=block,
            send_sem=send.at[piece, line],
            recv_sem=recv.at[piece, line],
            device_id={"seq": to},
            device_id_type=MESH,
        )

    def column(line, step):
        return line * RING + lax.rem(turn + step + RING, RING)

    def up_copy(piece, line):
        return shard_copy(piece, column(line, 0), seq_place + RING, up_send, up_recv, line)

    def down_copy(piece, line):
        return shard_copy(piece, column(line, 0), seq_place - RING, down_send, down_recv, line)

    def right_copy(piece, line, step=0):
        return shard_copy(piece, column(line, step), right, right_send, right_recv, line)

    def left_copy(piece, line, step=0):
        return shard_copy(piece, column(line, step), left, left_send, left_recv, line)

    def far_right_copy(piece, line, step=-1):
        return half_copy(piece, column(line, step), 0, right, far_right_send, far_right_recv, line)

    def far_left_copy(piece, line, step=1):
        return half_copy(piece, column(line, step), half, left, far_left_send, far_left_recv, line)

    def along_ring(piece, line):
        right_copy(piece, line).start()
        left_copy(piece, line).start()

    def from_line(piece, line):
        @pl.when(line < run)
        def _():
            up_copy(piece, line).wait_recv()

            @pl.when(run < RING - 1)
            def _():
                up_copy(piece, line).start()

        @pl.when(line > run)
        def _():
            down_copy(piece, line).wait_recv()

            @pl.when(run > 0)
            def _():
                down_copy(piece, line).start()

        along_ring(piece, line)

    def farther(piece, line):
        right_copy(piece, line, -1).wait_recv()
        far_right_copy(piece, line).start()
        left_copy(piece, line, 1).wait_recv()
        far_left_copy(piece, line).start()

    def last_of(piece, line):
        far_right_copy(piece, line, -2).wait_recv()
        far_left_copy(piece, line, 2).wait_recv()

    def core_copy(line):
        return pltpu.make_async_remote_copy(
            src_ref=part.at[line, 1 - core],
            dst_ref=part_in.at[line],
            send_sem=core_send.at[line],
            recv_sem=core_recv.at[line],
            device_id={"mp": 1 - core},
            device_id_type=MESH,
        )

    def section_copy(line):
        return pltpu.make_async_remote_copy(
            src_ref=ready.at[line],
            dst_ref=landed.at[line],
            send_sem=section_send.at[line],
            recv_sem=section_recv.at[line],
            device_id={"section": back_section},
            device_id_type=MESH,
        )

    def project(line):
        base = line * RING
        query_rows = held[0, pl.ds(base, RING)].reshape(RING * rows, -1)
        kv_rows = held[1, pl.ds(base, RING)].reshape(RING * rows, -1)
        product = lax.dot_general(
            w_query_ref[...], query_rows, NT, preferred_element_type=jnp.float32
        )
        product += lax.dot_general(
            key_weight_ref[...], kv_rows[:, :kv_cols], NT, preferred_element_type=jnp.float32
        )
        product += lax.dot_general(
            value_weight_ref[...], kv_rows[:, kv_cols:], NT, preferred_element_type=jnp.float32
        )
        part[line, 0] = product[:width]
        part[line, 1] = product[width:]
        core_copy(line).start()

    def hand_over(line):
        core_copy(line).wait_recv()
        ready[line] = (part[line, core] + part_in[line]).astype(jnp.bfloat16)
        section_copy(line).start()

    lines = [
        run,
        jnp.where(run == 0, 1, run - 1),
        jnp.where(run == 0, 2, jnp.where(run == 3, 1, run + 1)),
        jnp.where(run < 2, 3, 0),
    ]
    pieces = (0, 1)
    for piece in pieces:
        own_copy(piece).start()
    for piece in pieces:
        own_copy(piece).wait()

        @pl.when(run < RING - 1)
        def _():
            up_copy(piece, run).start()

        @pl.when(run > 0)
        def _():
            down_copy(piece, run).start()

        along_ring(piece, run)
    for order in range(1, RING + 2):
        if order < RING:
            for piece in pieces:
                from_line(piece, lines[order])
        if order <= RING:
            for piece in pieces:
                farther(piece, lines[order - 1])
        if order >= 2:
            for piece in pieces:
                last_of(piece, lines[order - 2])
            project(lines[order - 2])
            hand_over(lines[order - 2])
    for line in range(RING):
        section_copy(line).wait_recv()
        out_ref[line] = landed[line]
    for line in range(RING):
        core_copy(line).wait_send()
        section_copy(line).wait_send()
        for piece in pieces:
            right_copy(piece, line).wait_send()
            left_copy(piece, line).wait_send()
            far_right_copy(piece, line).wait_send()
            far_left_copy(piece, line).wait_send()

            @pl.when((run < RING - 1) & (line <= run))
            def _():
                up_copy(piece, line).wait_send()

            @pl.when((run > 0) & (line >= run))
            def _():
                down_copy(piece, line).wait_send()


def spread_and_project(grad_query, grad_kv, w_query, key_weight, value_weight):
    rows = grad_query.shape[0]
    cols = grad_query.shape[1]
    seq_count = lax.axis_size("seq")
    width = w_query.shape[0] // 2
    span = RING * rows
    dma = pltpu.SemaphoreType.DMA
    pairs = [dma((2, RING))] * 12
    whole = pl.BlockSpec(memory_space=pltpu.VMEM)
    out = pl.pallas_call(
        spread_kernel,
        out_shape=jax.ShapeDtypeStruct((RING, width, span), jnp.bfloat16),
        in_specs=[whole] * 5,
        out_specs=whole,
        scratch_shapes=[
            pltpu.VMEM((2, seq_count, rows, cols), jnp.bfloat16),
            pltpu.VMEM((RING, 2, width, span), jnp.float32),
            pltpu.VMEM((RING, width, span), jnp.float32),
            pltpu.VMEM((RING, width, span), jnp.bfloat16),
            pltpu.VMEM((RING, width, span), jnp.bfloat16),
            dma((2,)),
            *pairs,
            *([dma((RING,))] * 4),
        ],
        compiler_params=pltpu.CompilerParams(collective_id=0, has_side_effects=True),
    )(grad_query, grad_kv, w_query, key_weight, value_weight)
    return jnp.transpose(out, (0, 2, 1)).reshape(seq_count * rows, width)


def per_device(
    query_rows,
    key_row_matrix,
    value_row_matrix,
    out_grad,
    w_query,
    key_weight,
    value_weight,
    doc_ids,
):
    query_here = query_rows[0]
    key_here = key_row_matrix[0]
    value_here = value_row_matrix[0]
    grad_here = out_grad[0]
    documents = doc_ids[0]
    row_count = query_here.shape[0]
    kv_cols = key_here.shape[1]
    kv_heads = kv_cols // HEAD_WIDTH
    group_width = query_here.shape[1] // kv_cols
    scaling = 1.0 / math.sqrt(HEAD_WIDTH)
    seq_count = lax.axis_size("seq")
    seq_place = lax.axis_index("seq")
    reach_now = min((WINDOW - 1) // row_count + 1, seq_count - 1)
    kv_local = jnp.concatenate([key_here, value_here], axis=1)
    rim_blocks = [from_behind(kv_local, "seq", distance) for distance in range(reach_now, 0, -1)]
    kv_blocks = rim_blocks + [kv_local]
    block_total = len(kv_blocks)
    span_rows = block_total * row_count
    first_row = seq_place * row_count
    padded_docs = jnp.concatenate([jnp.full((reach_now * row_count,), -1, jnp.int32), documents])
    key_docs = lax.dynamic_slice_in_dim(padded_docs, first_row, span_rows, 0)
    query_docs = lax.dynamic_slice_in_dim(documents, first_row, row_count, 0)
    query_pos = first_row + jnp.arange(row_count, dtype=jnp.int32)
    key_pos = first_row - reach_now * row_count + jnp.arange(span_rows, dtype=jnp.int32)
    offset = query_pos[:, None] - key_pos[None, :]
    allowed = (query_docs[:, None] == key_docs[None, :]) & (offset >= 0) & (offset < WINDOW)
    query_split = query_here.reshape(row_count, kv_heads, group_width, HEAD_WIDTH)
    grad_split = grad_here.reshape(row_count, kv_heads, group_width, HEAD_WIDTH)
    block_masks = [
        allowed[:, block_index * row_count : (block_index + 1) * row_count]
        for block_index in range(block_total)
    ]
    block_keys = [
        kv_block[:, :kv_cols].reshape(row_count, kv_heads, HEAD_WIDTH) for kv_block in kv_blocks
    ]
    block_values = [
        kv_block[:, kv_cols:].reshape(row_count, kv_heads, HEAD_WIDTH) for kv_block in kv_blocks
    ]

    def score_pair(key_block, mask_now):

        def make_fn():
            product = (
                jnp.einsum(
                    "igrd,jgd->grij", query_split, key_block, preferred_element_type=jnp.float32
                )
                * scaling
            )
            return jnp.where(mask_now[None, None], product, -jnp.inf)

        def empty_fn():
            return jnp.full((kv_heads, group_width, row_count, row_count), -jnp.inf, jnp.float32)

        return (make_fn, empty_fn)

    scores = []
    for block_index in range(block_total):
        make_fn, empty_fn = score_pair(block_keys[block_index], block_masks[block_index])
        scores.append(make_fn())
    row_max = reduce(
        jnp.maximum, [jnp.max(score_now, axis=-1, keepdims=True) for score_now in scores]
    )
    raised = [jnp.exp(score_now - row_max) for score_now in scores]
    row_total = reduce(
        jnp.add, [jnp.sum(raised_now, axis=-1, keepdims=True) for raised_now in raised]
    )
    weights_full = [raised_now / row_total for raised_now in raised]
    weights_half = [weight_now.astype(jnp.bfloat16) for weight_now in weights_full]

    def value_pair(weight_half, value_block):

        def make_fn():
            return jnp.einsum(
                "grij,jgd->igrd", weight_half, value_block, preferred_element_type=jnp.float32
            )

        def empty_fn():
            return jnp.zeros((row_count, kv_heads, group_width, HEAD_WIDTH), jnp.float32)

        return (make_fn, empty_fn)

    attended_terms = []
    for block_index in range(block_total):
        make_fn, empty_fn = value_pair(weights_half[block_index], block_values[block_index])
        attended_terms.append(make_fn())
    attended = reduce(jnp.add, attended_terms)
    delta_row = jnp.transpose(
        jnp.sum(grad_split.astype(jnp.float32) * attended, axis=-1), (1, 2, 0)
    )

    def grad_pair(weight_full, weight_half, key_block, value_block):

        def make_fn():
            grad_weights = jnp.einsum(
                "igrd,jgd->grij", grad_split, value_block, preferred_element_type=jnp.float32
            )
            grad_scores = (weight_full * (grad_weights - delta_row[..., None])).astype(jnp.bfloat16)
            query_term = jnp.einsum(
                "grij,jgd->igrd", grad_scores, key_block, preferred_element_type=jnp.float32
            )
            key_term = (
                jnp.einsum(
                    "grij,igrd->jgd", grad_scores, query_split, preferred_element_type=jnp.float32
                )
                * scaling
            )
            value_term = jnp.einsum(
                "grij,igrd->jgd", weight_half, grad_split, preferred_element_type=jnp.float32
            )
            kv_term = jnp.concatenate(
                [key_term.reshape(row_count, kv_cols), value_term.reshape(row_count, kv_cols)],
                axis=1,
            )
            return (query_term, kv_term)

        def empty_fn():
            return (
                jnp.zeros((row_count, kv_heads, group_width, HEAD_WIDTH), jnp.float32),
                jnp.zeros((row_count, 2 * kv_cols), jnp.float32),
            )

        return (make_fn, empty_fn)

    query_terms = []
    kv_terms = []
    for block_index in range(block_total):
        make_fn, empty_fn = grad_pair(
            weights_full[block_index],
            weights_half[block_index],
            block_keys[block_index],
            block_values[block_index],
        )
        query_term, kv_term = make_fn()
        query_terms.append(query_term)
        kv_terms.append(kv_term)
    query_grad = (
        (reduce(jnp.add, query_terms) * scaling)
        .astype(jnp.bfloat16)
        .reshape(row_count, kv_heads * group_width * HEAD_WIDTH)
    )
    kv_total = kv_terms[-1]
    for distance in range(1, reach_now + 1):
        kv_total = kv_total + from_behind(kv_terms[reach_now - distance], "seq", -distance)
    kv_half = kv_total.astype(jnp.bfloat16)
    upstream = spread_and_project(query_grad, kv_half, w_query[0], key_weight[0], value_weight[0])
    return upstream[None]


def solution(mesh):
    placed = (
        P("section", "seq", "mp"),
        P("section", "seq", "mp"),
        P("section", "seq", "mp"),
        P("section", "seq", "mp"),
        P("section", "seq", "mp"),
        P("section", "seq", "mp"),
        P("section", "seq", "mp"),
        P("section", None),
    )
    return jax.shard_map(
        per_device,
        mesh=mesh,
        in_specs=placed,
        out_specs=P("section", None, ("seq", "mp")),
        check_vma=False,
    )
```

```python
import math

import jax
import jax.numpy as jnp
from jax import lax
from jax.experimental import pallas as pl
from jax.experimental.pallas import tpu as pltpu
from jax.sharding import PartitionSpec as P

HEAD_WIDTH = 128
WINDOW = 512
RING = 4
MESH = pl.DeviceIdType.MESH
NT = (((1,), (1,)), ((), ()))
TN = (((0,), (0,)), ((), ()))


def attention_kernel(
    docs_ref,
    query_ref,
    key_ref,
    value_ref,
    grad_ref,
    query_out,
    kv_out,
    keys,
    values,
    bias,
    sums,
    returned,
    returns_in,
    behind,
    behind_in,
    own_sem,
    halo_send,
    halo_recv,
    back_send,
    back_recv,
    line_send,
    line_recv,
):
    seq_place = lax.axis_index("seq")
    run = seq_place // RING
    turn = lax.rem(seq_place, RING)
    rows = query_ref.shape[0]
    heads = key_ref.shape[1] // HEAD_WIDTH
    scaling = 1.0 / math.sqrt(HEAD_WIDTH)
    near = range(1, RING)

    barrier = pltpu.get_barrier_semaphore()
    for step in near:
        pl.semaphore_signal(
            barrier,
            inc=1,
            device_id={"seq": run * RING + lax.rem(turn + step, RING)},
            device_id_type=MESH,
        )

    @pl.when(run < RING - 1)
    def _():
        pl.semaphore_signal(barrier, inc=1, device_id={"seq": seq_place + RING}, device_id_type=MESH)

    @pl.when(run > 0)
    def _():
        pl.semaphore_signal(barrier, inc=1, device_id={"seq": seq_place - RING}, device_id_type=MESH)

    in_line = (run > 0).astype(jnp.int32) + (run < RING - 1).astype(jnp.int32)
    pl.semaphore_wait(barrier, RING - 1 + in_line)

    sources = (key_ref, value_ref)
    buffers = (keys, values)

    def slot(step):
        return pl.ds((RING - step) * rows, rows)

    def head_of(ref, head):
        return ref.at[:, pl.ds(head * HEAD_WIDTH, HEAD_WIDTH)]

    def own_copy(kind, head):
        return pltpu.make_async_copy(
            head_of(sources[kind], head), buffers[kind].at[head, slot(0)], own_sem.at[kind, head]
        )

    def halo_copy(kind, head, step, relayed):
        if step == RING:
            to = seq_place + RING
        else:
            to = run * RING + lax.rem(turn + step, RING)
        source = buffers[kind].at[head, slot(RING)] if relayed else head_of(sources[kind], head)
        return pltpu.make_async_remote_copy(
            src_ref=source,
            dst_ref=buffers[kind].at[head, slot(step)],
            send_sem=halo_send.at[kind, step - 1, head],
            recv_sem=halo_recv.at[kind, step - 1, head],
            device_id={"seq": to},
            device_id_type=MESH,
        )

    def send_own(head):
        @pl.when(run < RING - 1)
        def _():
            for kind in (0, 1):
                halo_copy(kind, head, RING, False).start()

        for step in near:

            @pl.when(turn + step < RING)
            def _():
                for kind in (0, 1):
                    halo_copy(kind, head, step, False).start()

    def send_relayed(head):
        @pl.when(run > 0)
        def _():
            for kind in (0, 1):
                halo_copy(kind, head, RING, False).wait_recv()
            for step in near:

                @pl.when(turn + step >= RING)
                def _():
                    for kind in (0, 1):
                        halo_copy(kind, head, step, True).start()

    def wait_halo(head):
        for kind in (0, 1):
            own_copy(kind, head).wait()
        for step in near:

            @pl.when(seq_place >= step)
            def _():
                for kind in (0, 1):
                    halo_copy(kind, head, step, False).wait_recv()

    def back_copy(head, step):
        return pltpu.make_async_remote_copy(
            src_ref=returned.at[head, step - 1],
            dst_ref=returns_in.at[head, step - 1],
            send_sem=back_send.at[head, step - 1],
            recv_sem=back_recv.at[head, step - 1],
            device_id={"seq": run * RING + lax.rem(turn + RING - step, RING)},
            device_id_type=MESH,
        )

    def line_copy(head):
        return pltpu.make_async_remote_copy(
            src_ref=behind.at[head],
            dst_ref=behind_in.at[head],
            send_sem=line_send.at[head],
            recv_sem=line_recv.at[head],
            device_id={"seq": seq_place - RING},
            device_id_type=MESH,
        )

    def both(ref, head):
        block = ref[:, 2 * head * HEAD_WIDTH : 2 * (head + 1) * HEAD_WIDTH]
        return jnp.concatenate([block[:, :HEAD_WIDTH], block[:, HEAD_WIDTH:]], axis=0)

    def attend(head):
        query = both(query_ref, head)
        grad = both(grad_ref, head)
        key = keys[head]
        value = values[head]
        scores = lax.dot_general(query, key, NT, preferred_element_type=jnp.float32)
        mask = jnp.concatenate([bias[...], bias[...]], axis=0)
        scores = scores * scaling + mask
        raised = jnp.exp(scores - jnp.max(scores, axis=1, keepdims=True))
        weights = raised * (1.0 / jnp.sum(raised, axis=1, keepdims=True))
        weights_half = weights.astype(jnp.bfloat16)
        attended = jnp.dot(weights_half, value, preferred_element_type=jnp.float32)
        delta = jnp.sum(grad.astype(jnp.float32) * attended, axis=1, keepdims=True)
        grad_weights = lax.dot_general(grad, value, NT, preferred_element_type=jnp.float32)
        grad_scores = (weights * (grad_weights - delta)).astype(jnp.bfloat16)
        grad_query = jnp.dot(grad_scores, key, preferred_element_type=jnp.float32) * scaling
        grad_query = grad_query.astype(jnp.bfloat16)
        first = 2 * head * HEAD_WIDTH
        query_out[:, first : first + HEAD_WIDTH] = grad_query[:rows]
        query_out[:, first + HEAD_WIDTH : first + 2 * HEAD_WIDTH] = grad_query[rows:]
        grads = (
            lax.dot_general(grad_scores, query, TN, preferred_element_type=jnp.float32) * scaling,
            lax.dot_general(weights_half, grad, TN, preferred_element_type=jnp.float32),
        )
        for kind in (0, 1):
            sums[head, 0, kind] = grads[kind][RING * rows :]
            sums[head, 1, kind] = grads[kind][:rows]
            for step in near:
                first = (RING - step) * rows
                returned[head, step - 1, kind] = grads[kind][first : first + rows].astype(jnp.bfloat16)
        for step in near:

            @pl.when(seq_place >= step)
            def _():
                back_copy(head, step).start()

    def collect_behind(head):
        @pl.when(run > 0)
        def _():
            for step in near:

                @pl.when(turn + step >= RING)
                def _():
                    back_copy(head, step).wait_recv()
                    sums[head, 1] += returns_in[head, step - 1].astype(jnp.float32)

            behind[head] = sums[head, 1].astype(jnp.bfloat16)
            line_copy(head).start()

    def collect_own(head):
        for step in near:

            @pl.when(turn + step < RING)
            def _():
                back_copy(head, step).wait_recv()
                sums[head, 0] += returns_in[head, step - 1].astype(jnp.float32)

        @pl.when(run < RING - 1)
        def _():
            line_copy(head).wait_recv()
            sums[head, 0] += behind_in[head].astype(jnp.float32)

        for kind in (0, 1):
            first = (kind * heads + head) * HEAD_WIDTH
            kv_out[:, first : first + HEAD_WIDTH] = sums[head, 0, kind].astype(jnp.bfloat16)

    for head in range(heads):
        for kind in (0, 1):
            own_copy(kind, head).start()
        send_own(head)
        if head >= 1:
            send_relayed(head - 1)
    send_relayed(heads - 1)

    for step in range(1, RING + 1):

        @pl.when(seq_place < step)
        def _():
            for buffer in buffers:
                for head in range(heads):
                    buffer[head, slot(step)] = jnp.zeros((rows, HEAD_WIDTH), jnp.bfloat16)

    first_row = pl.multiple_of(seq_place * rows, rows)
    here = docs_ref[:, pl.ds(first_row, rows)].astype(jnp.float32)
    query_docs = jnp.transpose(jnp.broadcast_to(here, (rows, rows)))
    query_row = lax.broadcasted_iota(jnp.int32, (rows, rows), 0)
    key_row = lax.broadcasted_iota(jnp.int32, (rows, rows), 1)
    for step in range(RING + 1):
        start = pl.multiple_of(jnp.maximum(seq_place - step, 0) * rows, rows)
        there = docs_ref[:, pl.ds(start, rows)].astype(jnp.float32)
        offset = query_row - key_row + step * rows
        allowed = (query_docs == there) & (offset >= 0) & (offset < WINDOW)
        allowed = allowed & (jnp.full((rows, rows), seq_place, jnp.int32) >= step)
        bias[:, (RING - step) * rows : (RING - step + 1) * rows] = jnp.where(
            allowed, 0.0, -jnp.inf
        )

    for head in range(heads):
        wait_halo(head)
        attend(head)
        if head >= 1:
            collect_behind(head - 1)
    collect_behind(heads - 1)
    for head in range(heads):
        collect_own(head)

    for head in range(heads):
        for kind in (0, 1):
            for step in near:

                @pl.when((turn + step < RING) | (run > 0))
                def _():
                    halo_copy(kind, head, step, False).wait_send()

            @pl.when(run < RING - 1)
            def _():
                halo_copy(kind, head, RING, False).wait_send()

        for step in near:

            @pl.when(seq_place >= step)
            def _():
                back_copy(head, step).wait_send()

        @pl.when(run > 0)
        def _():
            line_copy(head).wait_send()


def attention_grads(docs, query, key, value, grad):
    rows = query.shape[0]
    heads = key.shape[1] // HEAD_WIDTH
    dma = pltpu.SemaphoreType.DMA
    whole = pl.BlockSpec(memory_space=pltpu.VMEM)
    tile = (rows, HEAD_WIDTH)
    return pl.pallas_call(
        attention_kernel,
        out_shape=(
            jax.ShapeDtypeStruct(query.shape, jnp.bfloat16),
            jax.ShapeDtypeStruct((rows, 2 * key.shape[1]), jnp.bfloat16),
        ),
        in_specs=[whole] * 5,
        out_specs=(whole, whole),
        scratch_shapes=[
            pltpu.VMEM((heads, (RING + 1) * rows, HEAD_WIDTH), jnp.bfloat16),
            pltpu.VMEM((heads, (RING + 1) * rows, HEAD_WIDTH), jnp.bfloat16),
            pltpu.VMEM((rows, (RING + 1) * rows), jnp.float32),
            pltpu.VMEM((heads, 2, 2) + tile, jnp.float32),
            pltpu.VMEM((heads, RING - 1, 2) + tile, jnp.bfloat16),
            pltpu.VMEM((heads, RING - 1, 2) + tile, jnp.bfloat16),
            pltpu.VMEM((heads, 2) + tile, jnp.bfloat16),
            pltpu.VMEM((heads, 2) + tile, jnp.bfloat16),
            dma((2, heads)),
            dma((2, RING, heads)),
            dma((2, RING, heads)),
            dma((heads, RING - 1)),
            dma((heads, RING - 1)),
            dma((heads,)),
            dma((heads,)),
        ],
        compiler_params=pltpu.CompilerParams(collective_id=1, has_side_effects=True),
    )(docs, query, key, value, grad)


def spread_kernel(
    grad_query_ref,
    grad_kv_ref,
    w_query_ref,
    key_weight_ref,
    value_weight_ref,
    out_ref,
    held,
    part,
    part_in,
    ready,
    landed,
    own_sem,
    up_send,
    up_recv,
    down_send,
    down_recv,
    right_send,
    right_recv,
    left_send,
    left_recv,
    far_right_send,
    far_right_recv,
    far_left_send,
    far_left_recv,
    core_send,
    core_recv,
    section_send,
    section_recv,
):
    seq_place = lax.axis_index("seq")
    core = lax.axis_index("mp")
    section = lax.axis_index("section")
    section_count = lax.axis_size("section")
    run = seq_place // RING
    turn = lax.rem(seq_place, RING)
    right = run * RING + lax.rem(turn + 1, RING)
    left = run * RING + lax.rem(turn + RING - 1, RING)
    back_section = lax.rem(section + section_count - 1, section_count)
    next_section = lax.rem(section + 1, section_count)
    rows = held.shape[2]
    half = rows // 2
    kv_cols = key_weight_ref.shape[1]
    width = w_query_ref.shape[0] // 2

    barrier = pltpu.get_barrier_semaphore()
    for place in (right, left):
        pl.semaphore_signal(barrier, inc=1, device_id={"seq": place}, device_id_type=MESH)
    pl.semaphore_signal(barrier, inc=1, device_id={"mp": 1 - core}, device_id_type=MESH)
    pl.semaphore_signal(barrier, inc=1, device_id={"section": back_section}, device_id_type=MESH)
    pl.semaphore_signal(barrier, inc=1, device_id={"section": next_section}, device_id_type=MESH)

    @pl.when(run < RING - 1)
    def _():
        pl.semaphore_signal(barrier, inc=1, device_id={"seq": seq_place + RING}, device_id_type=MESH)

    @pl.when(run > 0)
    def _():
        pl.semaphore_signal(barrier, inc=1, device_id={"seq": seq_place - RING}, device_id_type=MESH)

    in_line = (run > 0).astype(jnp.int32) + (run < RING - 1).astype(jnp.int32)
    pl.semaphore_wait(barrier, 5 + in_line)

    def own_copy(piece):
        source = grad_query_ref if piece == 0 else grad_kv_ref
        return pltpu.make_async_copy(source, held.at[piece, seq_place], own_sem.at[piece])

    def shard_copy(piece, owner, to, send, recv, line):
        block = held.at[piece, owner]
        return pltpu.make_async_remote_copy(
            src_ref=block,
            dst_ref=block,
            send_sem=send.at[piece, line],
            recv_sem=recv.at[piece, line],
            device_id={"seq": to},
            device_id_type=MESH,
        )

    def half_copy(piece, owner, start, to, send, recv, line):
        block = held.at[piece, owner, pl.ds(start, half)]
        return pltpu.make_async_remote_copy(
            src_ref=block,
            dst_ref=block,
            send_sem=send.at[piece, line],
            recv_sem=recv.at[piece, line],
            device_id={"seq": to},
            device_id_type=MESH,
        )

    def column(line, step):
        return line * RING + lax.rem(turn + step + RING, RING)

    def up_copy(piece, line):
        return shard_copy(piece, column(line, 0), seq_place + RING, up_send, up_recv, line)

    def down_copy(piece, line):
        return shard_copy(piece, column(line, 0), seq_place - RING, down_send, down_recv, line)

    def right_copy(piece, line, step=0):
        return shard_copy(piece, column(line, step), right, right_send, right_recv, line)

    def left_copy(piece, line, step=0):
        return shard_copy(piece, column(line, step), left, left_send, left_recv, line)

    def far_right_copy(piece, line, step=-1):
        return half_copy(piece, column(line, step), 0, right, far_right_send, far_right_recv, line)

    def far_left_copy(piece, line, step=1):
        return half_copy(piece, column(line, step), half, left, far_left_send, far_left_recv, line)

    def along_ring(piece, line):
        right_copy(piece, line).start()
        left_copy(piece, line).start()

    def from_line(piece, line):
        @pl.when(line < run)
        def _():
            up_copy(piece, line).wait_recv()

            @pl.when(run < RING - 1)
            def _():
                up_copy(piece, line).start()

        @pl.when(line > run)
        def _():
            down_copy(piece, line).wait_recv()

            @pl.when(run > 0)
            def _():
                down_copy(piece, line).start()

        along_ring(piece, line)

    def farther(piece, line):
        right_copy(piece, line, -1).wait_recv()
        far_right_copy(piece, line).start()
        left_copy(piece, line, 1).wait_recv()
        far_left_copy(piece, line).start()

    def last_of(piece, line):
        far_right_copy(piece, line, -2).wait_recv()
        far_left_copy(piece, line, 2).wait_recv()

    def core_copy(line):
        return pltpu.make_async_remote_copy(
            src_ref=part.at[line, 1 - core],
            dst_ref=part_in.at[line],
            send_sem=core_send.at[line],
            recv_sem=core_recv.at[line],
            device_id={"mp": 1 - core},
            device_id_type=MESH,
        )

    def section_copy(line):
        return pltpu.make_async_remote_copy(
            src_ref=ready.at[line],
            dst_ref=landed.at[line],
            send_sem=section_send.at[line],
            recv_sem=section_recv.at[line],
            device_id={"section": back_section},
            device_id_type=MESH,
        )

    def project(line):
        base = line * RING
        query_rows = held[0, pl.ds(base, RING)].reshape(RING * rows, -1)
        kv_rows = held[1, pl.ds(base, RING)].reshape(RING * rows, -1)
        product = lax.dot_general(
            w_query_ref[...], query_rows, NT, preferred_element_type=jnp.float32
        )
        product += lax.dot_general(
            key_weight_ref[...], kv_rows[:, :kv_cols], NT, preferred_element_type=jnp.float32
        )
        product += lax.dot_general(
            value_weight_ref[...], kv_rows[:, kv_cols:], NT, preferred_element_type=jnp.float32
        )
        part[line, 0] = product[:width]
        part[line, 1] = product[width:]
        core_copy(line).start()

    def hand_over(line):
        core_copy(line).wait_recv()
        ready[line] = (part[line, core] + part_in[line]).astype(jnp.bfloat16)
        section_copy(line).start()

    lines = [
        run,
        jnp.where(run == 0, 1, run - 1),
        jnp.where(run == 0, 2, jnp.where(run == 3, 1, run + 1)),
        jnp.where(run < 2, 3, 0),
    ]
    pieces = (0, 1)
    for piece in pieces:
        own_copy(piece).start()
    for piece in pieces:
        own_copy(piece).wait()

        @pl.when(run < RING - 1)
        def _():
            up_copy(piece, run).start()

        @pl.when(run > 0)
        def _():
            down_copy(piece, run).start()

        along_ring(piece, run)
    for order in range(1, RING + 2):
        if order < RING:
            for piece in pieces:
                from_line(piece, lines[order])
        if order <= RING:
            for piece in pieces:
                farther(piece, lines[order - 1])
        if order >= 2:
            for piece in pieces:
                last_of(piece, lines[order - 2])
            project(lines[order - 2])
            hand_over(lines[order - 2])
    for line in range(RING):
        section_copy(line).wait_recv()
        out_ref[line] = landed[line]
    for line in range(RING):
        core_copy(line).wait_send()
        section_copy(line).wait_send()
        for piece in pieces:
            right_copy(piece, line).wait_send()
            left_copy(piece, line).wait_send()
            far_right_copy(piece, line).wait_send()
            far_left_copy(piece, line).wait_send()

            @pl.when((run < RING - 1) & (line <= run))
            def _():
                up_copy(piece, line).wait_send()

            @pl.when((run > 0) & (line >= run))
            def _():
                down_copy(piece, line).wait_send()


def spread_and_project(grad_query, grad_kv, w_query, key_weight, value_weight):
    rows = grad_query.shape[0]
    cols = grad_query.shape[1]
    seq_count = lax.axis_size("seq")
    width = w_query.shape[0] // 2
    span = RING * rows
    dma = pltpu.SemaphoreType.DMA
    pairs = [dma((2, RING))] * 12
    whole = pl.BlockSpec(memory_space=pltpu.VMEM)
    out = pl.pallas_call(
        spread_kernel,
        out_shape=jax.ShapeDtypeStruct((RING, width, span), jnp.bfloat16),
        in_specs=[whole] * 5,
        out_specs=whole,
        scratch_shapes=[
            pltpu.VMEM((2, seq_count, rows, cols), jnp.bfloat16),
            pltpu.VMEM((RING, 2, width, span), jnp.float32),
            pltpu.VMEM((RING, width, span), jnp.float32),
            pltpu.VMEM((RING, width, span), jnp.bfloat16),
            pltpu.VMEM((RING, width, span), jnp.bfloat16),
            dma((2,)),
            *pairs,
            *([dma((RING,))] * 4),
        ],
        compiler_params=pltpu.CompilerParams(collective_id=0, has_side_effects=True),
    )(grad_query, grad_kv, w_query, key_weight, value_weight)
    return jnp.transpose(out, (0, 2, 1)).reshape(seq_count * rows, width)


def per_device(
    query_rows,
    key_row_matrix,
    value_row_matrix,
    out_grad,
    w_query,
    key_weight,
    value_weight,
    doc_ids,
):
    grad_query, grad_kv = attention_grads(
        doc_ids, query_rows[0], key_row_matrix[0], value_row_matrix[0], out_grad[0]
    )
    upstream = spread_and_project(grad_query, grad_kv, w_query[0], key_weight[0], value_weight[0])
    return upstream[None]


def solution(mesh):
    placed = (
        P("section", "seq", "mp"),
        P("section", "seq", "mp"),
        P("section", "seq", "mp"),
        P("section", "seq", "mp"),
        P("section", "seq", "mp"),
        P("section", "seq", "mp"),
        P("section", "seq", "mp"),
        P("section", None),
    )
    return jax.shard_map(
        per_device,
        mesh=mesh,
        in_specs=placed,
        out_specs=P("section", None, ("seq", "mp")),
        check_vma=False,
    )
```

```python
import math

import jax
import jax.numpy as jnp
from jax import lax
from jax.experimental import pallas as pl
from jax.experimental.pallas import tpu as pltpu
from jax.sharding import PartitionSpec as P

HEAD_WIDTH = 128
WINDOW = 512
RING = 4
LEG = 6
MESH = pl.DeviceIdType.MESH
NT = (((1,), (1,)), ((), ()))
TN = (((0,), (0,)), ((), ()))
PIECES = 4
PIECE_HEADS = 4
EARLY_WEIGHTS = 2


def signal(semaphore, device):
    pl.semaphore_signal(semaphore, inc=1, device_id=device, device_id_type=MESH)


def cascade_kernel(
    docs_ref,
    query_ref,
    key_ref,
    value_ref,
    grad_ref,
    w_query_ref,
    key_weight_ref,
    value_weight_ref,
    out_ref,
    keys,
    values,
    bias,
    sums,
    returned,
    returns_in,
    behind,
    behind_in,
    held,
    weights_in,
    part,
    part_in,
    ready,
    relayed,
    landed,
    own_sem,
    halo_send,
    halo_recv,
    back_send,
    back_recv,
    line_send,
    line_recv,
    weight_send,
    weight_recv,
    across_send,
    across_recv,
    right_send,
    right_recv,
    left_send,
    left_recv,
    far_right_send,
    far_right_recv,
    far_left_send,
    far_left_recv,
    core_send,
    core_recv,
    section_send,
    section_recv,
    relay_recv,
    forward_send,
):
    seq_place = lax.axis_index("seq")
    core = lax.axis_index("mp")
    section = lax.axis_index("section")
    section_count = lax.axis_size("section")
    run = seq_place // RING
    turn = lax.rem(seq_place, RING)
    column = section // RING
    block = lax.rem(section, RING)
    rows = query_ref.shape[0]
    half = rows // 2
    heads = key_ref.shape[1] // HEAD_WIDTH
    width = w_query_ref.shape[0] // 2
    scaling = 1.0 / math.sqrt(HEAD_WIDTH)
    near = range(1, RING)

    right = run * RING + lax.rem(turn + 1, RING)
    left = run * RING + lax.rem(turn + RING - 1, RING)
    paired_run = run + 1 - 2 * lax.rem(run, 2)
    paired = paired_run * RING + turn
    opposite_run = lax.rem(run + 2, RING)
    opposite = opposite_run * RING + turn
    back_section = lax.rem(section + section_count - 1, section_count)
    next_section = lax.rem(section + 1, section_count)

    depth = RING * RING
    along = block * RING + run
    ahead = lax.rem(along + LEG, depth)
    before = lax.rem(along + depth - LEG, depth)

    def at(col, place):
        return {"section": col * RING + place // RING, "seq": lax.rem(place, RING) * RING + turn}

    turned = block == 0
    from_turned = before < RING
    first_column = lax.rem(column + RING - turned.astype(jnp.int32), RING)
    source_column = lax.rem(column + from_turned.astype(jnp.int32), RING)

    barrier = pltpu.get_barrier_semaphore()
    for step in near:
        signal(barrier, {"seq": run * RING + lax.rem(turn + step, RING)})
    signal(barrier, {"seq": opposite})
    signal(barrier, {"mp": 1 - core})
    for place in (seq_place, paired):
        signal(barrier, {"section": back_section, "seq": place})
        signal(barrier, {"section": next_section, "seq": place})
    signal(barrier, at(column, ahead))
    signal(barrier, at(column, before))

    @pl.when(turned)
    def _():
        signal(barrier, at(first_column, ahead))

    @pl.when(from_turned)
    def _():
        signal(barrier, at(source_column, before))

    @pl.when(run < RING - 1)
    def _():
        signal(barrier, {"seq": seq_place + RING})

    @pl.when(run > 0)
    def _():
        signal(barrier, {"seq": seq_place - RING})

    peers = RING - 1 + 1 + 1 + 4 + 2
    peers = peers + turned.astype(jnp.int32) + from_turned.astype(jnp.int32)
    peers = peers + (run > 0).astype(jnp.int32) + (run < RING - 1).astype(jnp.int32)
    pl.semaphore_wait(barrier, peers)

    sources = (key_ref, value_ref)
    buffers = (keys, values)

    def slot(step):
        return pl.ds((RING - step) * rows, rows)

    def head_of(ref, head):
        return ref.at[:, pl.ds(head * HEAD_WIDTH, HEAD_WIDTH)]

    def own_copy(kind, head):
        return pltpu.make_async_copy(
            head_of(sources[kind], head), buffers[kind].at[head, slot(0)], own_sem.at[kind, head]
        )

    def halo_copy(kind, head, step, relayed):
        if step == RING:
            to = seq_place + RING
        else:
            to = run * RING + lax.rem(turn + step, RING)
        source = buffers[kind].at[head, slot(RING)] if relayed else head_of(sources[kind], head)
        return pltpu.make_async_remote_copy(
            src_ref=source,
            dst_ref=buffers[kind].at[head, slot(step)],
            send_sem=halo_send.at[kind, step - 1, head],
            recv_sem=halo_recv.at[kind, step - 1, head],
            device_id={"seq": to},
            device_id_type=MESH,
        )

    def send_own(head):
        @pl.when(run < RING - 1)
        def _():
            for kind in (0, 1):
                halo_copy(kind, head, RING, False).start()

        for step in near:

            @pl.when(turn + step < RING)
            def _():
                for kind in (0, 1):
                    halo_copy(kind, head, step, False).start()

    def send_relayed(head):
        @pl.when(run > 0)
        def _():
            for kind in (0, 1):
                halo_copy(kind, head, RING, False).wait_recv()
            for step in near:

                @pl.when(turn + step >= RING)
                def _():
                    for kind in (0, 1):
                        halo_copy(kind, head, step, True).start()

    def wait_halo(head):
        for kind in (0, 1):
            own_copy(kind, head).wait()
        for step in near:

            @pl.when(seq_place >= step)
            def _():
                for kind in (0, 1):
                    halo_copy(kind, head, step, False).wait_recv()

    def back_copy(head, step):
        return pltpu.make_async_remote_copy(
            src_ref=returned.at[head, step - 1],
            dst_ref=returns_in.at[head, step - 1],
            send_sem=back_send.at[head, step - 1],
            recv_sem=back_recv.at[head, step - 1],
            device_id={"seq": run * RING + lax.rem(turn + RING - step, RING)},
            device_id_type=MESH,
        )

    def line_copy(head):
        return pltpu.make_async_remote_copy(
            src_ref=behind.at[head],
            dst_ref=behind_in.at[head],
            send_sem=line_send.at[head],
            recv_sem=line_recv.at[head],
            device_id={"seq": seq_place - RING},
            device_id_type=MESH,
        )

    def both(ref, head):
        block = ref[:, 2 * head * HEAD_WIDTH : 2 * (head + 1) * HEAD_WIDTH]
        return jnp.concatenate([block[:, :HEAD_WIDTH], block[:, HEAD_WIDTH:]], axis=0)

    def attend(head):
        query = both(query_ref, head)
        grad = both(grad_ref, head)
        key = keys[head]
        value = values[head]
        scores = lax.dot_general(query, key, NT, preferred_element_type=jnp.float32)
        mask = jnp.concatenate([bias[...], bias[...]], axis=0)
        scores = scores * scaling + mask
        raised = jnp.exp(scores - jnp.max(scores, axis=1, keepdims=True))
        weights = raised * (1.0 / jnp.sum(raised, axis=1, keepdims=True))
        weights_half = weights.astype(jnp.bfloat16)
        attended = jnp.dot(weights_half, value, preferred_element_type=jnp.float32)
        delta = jnp.sum(grad.astype(jnp.float32) * attended, axis=1, keepdims=True)
        grad_weights = lax.dot_general(grad, value, NT, preferred_element_type=jnp.float32)
        grad_scores = (weights * (grad_weights - delta)).astype(jnp.bfloat16)
        grad_query = jnp.dot(grad_scores, key, preferred_element_type=jnp.float32) * scaling
        grad_query = grad_query.astype(jnp.bfloat16)
        piece, place = divmod(2 * head, PIECE_HEADS)
        first = place * HEAD_WIDTH
        held[piece, 0, turn, :, first : first + HEAD_WIDTH] = grad_query[:rows]
        held[piece, 0, turn, :, first + HEAD_WIDTH : first + 2 * HEAD_WIDTH] = grad_query[rows:]
        grads = (
            lax.dot_general(grad_scores, query, TN, preferred_element_type=jnp.float32) * scaling,
            lax.dot_general(weights_half, grad, TN, preferred_element_type=jnp.float32),
        )
        for kind in (0, 1):
            sums[head, 0, kind] = grads[kind][RING * rows :]
            sums[head, 1, kind] = grads[kind][:rows]
            for step in near:
                first = (RING - step) * rows
                returned[head, step - 1, kind] = grads[kind][first : first + rows].astype(jnp.bfloat16)
        for step in near:

            @pl.when(seq_place >= step)
            def _():
                back_copy(head, step).start()

    def collect_behind(head):
        @pl.when(run > 0)
        def _():
            for step in near:

                @pl.when(turn + step >= RING)
                def _():
                    back_copy(head, step).wait_recv()
                    sums[head, 1] += returns_in[head, step - 1].astype(jnp.float32)

            behind[head] = sums[head, 1].astype(jnp.bfloat16)
            line_copy(head).start()

    def collect_own(head):
        for step in near:

            @pl.when(turn + step < RING)
            def _():
                back_copy(head, step).wait_recv()
                sums[head, 0] += returns_in[head, step - 1].astype(jnp.float32)

        @pl.when(run < RING - 1)
        def _():
            line_copy(head).wait_recv()
            sums[head, 0] += behind_in[head].astype(jnp.float32)

        for kind in (0, 1):
            first = head * HEAD_WIDTH
            held[2 + kind, 0, turn, :, first : first + HEAD_WIDTH] = sums[head, 0, kind].astype(
                jnp.bfloat16
            )


    def weight_piece(piece):
        span = pl.ds(piece * PIECE_HEADS * HEAD_WIDTH, PIECE_HEADS * HEAD_WIDTH)
        return (
            w_query_ref.at[:, span] if piece < 2 else (key_weight_ref, value_weight_ref)[piece - 2]
        )

    def weight_copy(piece):
        return pltpu.make_async_remote_copy(
            src_ref=weight_piece(piece),
            dst_ref=weights_in.at[piece],
            send_sem=weight_send.at[piece],
            recv_sem=weight_recv.at[piece],
            device_id={"seq": paired},
            device_id_type=MESH,
        )

    def across_copy(piece):
        return pltpu.make_async_remote_copy(
            src_ref=held.at[piece, 0, turn],
            dst_ref=held.at[piece, 1, turn],
            send_sem=across_send.at[piece],
            recv_sem=across_recv.at[piece],
            device_id={"seq": opposite},
            device_id_type=MESH,
        )

    def ring_copy(shard, to, send, recv):
        return pltpu.make_async_remote_copy(
            src_ref=shard,
            dst_ref=shard,
            send_sem=send,
            recv_sem=recv,
            device_id={"seq": to},
            device_id_type=MESH,
        )

    def shard_of(piece, line, step):
        return held.at[piece, line, lax.rem(turn + step + RING, RING)]

    def half_of(piece, line, step, start):
        return held.at[piece, line, lax.rem(turn + step + RING, RING), pl.ds(start, half)]

    def right_copy(piece, line, step=0):
        return ring_copy(
            shard_of(piece, line, step), right, right_send.at[piece, line], right_recv.at[piece, line]
        )

    def left_copy(piece, line, step=0):
        return ring_copy(
            shard_of(piece, line, step), left, left_send.at[piece, line], left_recv.at[piece, line]
        )

    def far_right_copy(piece, line, step=-1):
        return ring_copy(
            half_of(piece, line, step, 0),
            right,
            far_right_send.at[piece, line],
            far_right_recv.at[piece, line],
        )

    def far_left_copy(piece, line, step=1):
        return ring_copy(
            half_of(piece, line, step, half),
            left,
            far_left_send.at[piece, line],
            far_left_recv.at[piece, line],
        )

    def along_ring(piece, line):
        right_copy(piece, line).start()
        left_copy(piece, line).start()

    def spread(piece):
        across_copy(piece).start()
        along_ring(piece, 0)

    def from_across(piece):
        across_copy(piece).wait_recv()
        along_ring(piece, 1)

    def farther(piece, line):
        right_copy(piece, line, -1).wait_recv()
        far_right_copy(piece, line).start()
        left_copy(piece, line, 1).wait_recv()
        far_left_copy(piece, line).start()

    def last_of(piece, line):
        far_right_copy(piece, line, -2).wait_recv()
        far_left_copy(piece, line, 2).wait_recv()

    def core_copy(unit):
        return pltpu.make_async_remote_copy(
            src_ref=part.at[unit, 1 - core],
            dst_ref=part_in.at[unit],
            send_sem=core_send.at[unit],
            recv_sem=core_recv.at[unit],
            device_id={"mp": 1 - core},
            device_id_type=MESH,
        )

    def section_copy(unit):
        line, owner = divmod(unit, 2)
        row = opposite_run if line else run
        return pltpu.make_async_remote_copy(
            src_ref=ready.at[unit],
            dst_ref=landed.at[row],
            send_sem=section_send.at[unit],
            recv_sem=section_recv.at[row],
            device_id={"section": back_section, "seq": paired if owner else seq_place},
            device_id_type=MESH,
        )

    def relay_copy():
        return pltpu.make_async_remote_copy(
            src_ref=ready.at[0],
            dst_ref=relayed,
            send_sem=section_send.at[0],
            recv_sem=relay_recv.at[0],
            device_id=at(first_column, ahead),
            device_id_type=MESH,
        )

    def forward_copy():
        return pltpu.make_async_remote_copy(
            src_ref=relayed,
            dst_ref=landed.at[opposite_run],
            send_sem=forward_send.at[0],
            recv_sem=section_recv.at[opposite_run],
            device_id=at(column, ahead),
            device_id_type=MESH,
        )

    def land(row):
        pltpu.make_async_remote_copy(
            src_ref=landed.at[row],
            dst_ref=landed.at[row],
            send_sem=forward_send.at[0],
            recv_sem=section_recv.at[row],
            device_id={"section": back_section},
            device_id_type=MESH,
        ).wait_recv()
        start = row * RING * rows
        out_ref[pl.ds(pl.multiple_of(start, RING * rows), RING * rows), :] = jnp.transpose(landed[row])

    def project(unit):
        line, owner = divmod(unit, 2)
        product = None
        for piece in range(PIECES):
            weight = weights_in[piece] if owner else weight_piece(piece)[...]
            shards = held[piece, line].reshape(RING * rows, -1)
            term = lax.dot_general(weight, shards, NT, preferred_element_type=jnp.float32)
            product = term if product is None else product + term
        part[unit, 0] = product[:width]
        part[unit, 1] = product[width:]
        core_copy(unit).start()

    def hand_over(unit):
        core_copy(unit).wait_recv()
        ready[unit] = (part[unit, core] + part_in[unit]).astype(jnp.bfloat16)
        if unit == 0:
            relay_copy().start()
        else:
            section_copy(unit).start()

    for head in range(heads):
        for kind in (0, 1):
            own_copy(kind, head).start()
        send_own(head)
        if head >= 1:
            send_relayed(head - 1)
    for piece in range(EARLY_WEIGHTS):
        weight_copy(piece).start()
    send_relayed(heads - 1)

    for step in range(1, RING + 1):

        @pl.when(seq_place < step)
        def _():
            for buffer in buffers:
                for head in range(heads):
                    buffer[head, slot(step)] = jnp.zeros((rows, HEAD_WIDTH), jnp.bfloat16)

    first_row = pl.multiple_of(seq_place * rows, rows)
    here = docs_ref[:, pl.ds(first_row, rows)].astype(jnp.float32)
    query_docs = jnp.transpose(jnp.broadcast_to(here, (rows, rows)))
    query_row = lax.broadcasted_iota(jnp.int32, (rows, rows), 0)
    key_row = lax.broadcasted_iota(jnp.int32, (rows, rows), 1)
    for step in range(RING + 1):
        start = pl.multiple_of(jnp.maximum(seq_place - step, 0) * rows, rows)
        there = docs_ref[:, pl.ds(start, rows)].astype(jnp.float32)
        offset = query_row - key_row + step * rows
        allowed = (query_docs == there) & (offset >= 0) & (offset < WINDOW)
        allowed = allowed & (jnp.full((rows, rows), seq_place, jnp.int32) >= step)
        bias[:, (RING - step) * rows : (RING - step + 1) * rows] = jnp.where(
            allowed, 0.0, -jnp.inf
        )

    for head in range(heads):
        wait_halo(head)
        attend(head)
        if head >= 1:
            collect_behind(head - 1)
        if head % 2:
            spread(head // 2)
    collect_behind(heads - 1)
    for piece in range(EARLY_WEIGHTS, PIECES):
        weight_copy(piece).start()
    farther(0, 0)
    from_across(0)
    for head in range(heads):
        collect_own(head)
    for piece in (2, 3):
        spread(piece)
    farther(1, 0)
    from_across(1)
    farther(0, 1)
    for piece in (2, 3):
        farther(piece, 0)
    for piece in range(PIECES):
        last_of(piece, 0)
    project(0)
    farther(1, 1)
    for piece in (2, 3):
        from_across(piece)
    hand_over(0)
    for piece in range(PIECES):
        weight_copy(piece).wait_recv()
    project(1)
    for piece in (2, 3):
        farther(piece, 1)
    hand_over(1)
    for piece in range(PIECES):
        last_of(piece, 1)
    project(2)
    project(3)
    hand_over(2)
    hand_over(3)
    relay_copy().wait_recv()
    forward_copy().start()
    for row in (lax.rem(run + 1, RING), opposite_run, lax.rem(run + 3, RING), run):
        land(row)

    for unit in range(4):
        core_copy(unit).wait_send()
        section_copy(unit).wait_send()
    forward_copy().wait_send()
    for piece in range(PIECES):
        weight_copy(piece).wait_send()
        across_copy(piece).wait_send()
        for line in (0, 1):
            right_copy(piece, line).wait_send()
            left_copy(piece, line).wait_send()
            far_right_copy(piece, line).wait_send()
            far_left_copy(piece, line).wait_send()
    for head in range(heads):
        for kind in (0, 1):
            for step in near:

                @pl.when((turn + step < RING) | (run > 0))
                def _():
                    halo_copy(kind, head, step, False).wait_send()

            @pl.when(run < RING - 1)
            def _():
                halo_copy(kind, head, RING, False).wait_send()

        for step in near:

            @pl.when(seq_place >= step)
            def _():
                back_copy(head, step).wait_send()

        @pl.when(run > 0)
        def _():
            line_copy(head).wait_send()


def cascade(docs, query, key, value, grad, w_query, key_weight, value_weight):
    rows = query.shape[0]
    heads = key.shape[1] // HEAD_WIDTH
    seq_count = lax.axis_size("seq")
    width = w_query.shape[0] // 2
    span = RING * rows
    cols = PIECE_HEADS * HEAD_WIDTH
    dma = pltpu.SemaphoreType.DMA
    whole = pl.BlockSpec(memory_space=pltpu.VMEM)
    tile = (rows, HEAD_WIDTH)
    return pl.pallas_call(
        cascade_kernel,
        out_shape=jax.ShapeDtypeStruct((seq_count * rows, width), jnp.bfloat16),
        in_specs=[whole] * 8,
        out_specs=whole,
        scratch_shapes=[
            pltpu.VMEM((heads, (RING + 1) * rows, HEAD_WIDTH), jnp.bfloat16),
            pltpu.VMEM((heads, (RING + 1) * rows, HEAD_WIDTH), jnp.bfloat16),
            pltpu.VMEM((rows, (RING + 1) * rows), jnp.float32),
            pltpu.VMEM((heads, 2, 2) + tile, jnp.float32),
            pltpu.VMEM((heads, RING - 1, 2) + tile, jnp.bfloat16),
            pltpu.VMEM((heads, RING - 1, 2) + tile, jnp.bfloat16),
            pltpu.VMEM((heads, 2) + tile, jnp.bfloat16),
            pltpu.VMEM((heads, 2) + tile, jnp.bfloat16),
            pltpu.VMEM((PIECES, 2, RING, rows, cols), jnp.bfloat16),
            pltpu.VMEM((PIECES, 2 * width, cols), jnp.bfloat16),
            pltpu.VMEM((4, 2, width, span), jnp.float32),
            pltpu.VMEM((4, width, span), jnp.float32),
            pltpu.VMEM((4, width, span), jnp.bfloat16),
            pltpu.VMEM((width, span), jnp.bfloat16),
            pltpu.VMEM((RING, width, span), jnp.bfloat16),
            dma((2, heads)),
            dma((2, RING, heads)),
            dma((2, RING, heads)),
            dma((heads, RING - 1)),
            dma((heads, RING - 1)),
            dma((heads,)),
            dma((heads,)),
            *([dma((PIECES,))] * 4),
            *([dma((PIECES, 2))] * 8),
            *([dma((4,))] * 4),
            *([dma((1,))] * 2),
        ],
        compiler_params=pltpu.CompilerParams(collective_id=0, has_side_effects=True),
    )(docs, query, key, value, grad, w_query, key_weight, value_weight)


def per_device(
    query_rows,
    key_row_matrix,
    value_row_matrix,
    out_grad,
    w_query,
    key_weight,
    value_weight,
    doc_ids,
):
    upstream = cascade(
        doc_ids,
        query_rows[0],
        key_row_matrix[0],
        value_row_matrix[0],
        out_grad[0],
        w_query[0],
        key_weight[0],
        value_weight[0],
    )
    return upstream[None]


def solution(mesh):
    placed = (
        P("section", "seq", "mp"),
        P("section", "seq", "mp"),
        P("section", "seq", "mp"),
        P("section", "seq", "mp"),
        P("section", "seq", "mp"),
        P("section", "seq", "mp"),
        P("section", "seq", "mp"),
        P("section", None),
    )
    return jax.shard_map(
        per_device,
        mesh=mesh,
        in_specs=placed,
        out_specs=P("section", None, ("seq", "mp")),
        check_vma=False,
    )
```

```python
import math

import jax
import jax.numpy as jnp
from jax import lax
from jax.experimental import pallas as pl
from jax.experimental.pallas import tpu as pltpu
from jax.sharding import PartitionSpec as P

HEAD_WIDTH = 128
WINDOW = 512
RING = 4
LEG = 6
MESH = pl.DeviceIdType.MESH
NT = (((1,), (1,)), ((), ()))
TN = (((0,), (0,)), ((), ()))
PIECES = 2
EARLY_WEIGHTS = 2


def signal(semaphore, device):
    pl.semaphore_signal(semaphore, inc=1, device_id=device, device_id_type=MESH)


def cascade_kernel(
    docs_ref,
    query_ref,
    key_ref,
    value_ref,
    grad_ref,
    w_query_ref,
    key_weight_ref,
    value_weight_ref,
    out_ref,
    keys,
    values,
    queries,
    grads,
    bias,
    sums,
    behind,
    behind_in,
    weights,
    weights_in,
    held,
    part,
    part_in,
    ready,
    relayed,
    landed,
    own_sem,
    own_weight_sem,
    swap_send,
    swap_recv,
    halo_send,
    halo_recv,
    line_send,
    line_recv,
    weight_send,
    weight_recv,
    across_send,
    across_recv,
    right_send,
    right_recv,
    left_send,
    left_recv,
    far_right_send,
    far_right_recv,
    far_left_send,
    far_left_recv,
    core_send,
    core_recv,
    section_send,
    section_recv,
    relay_recv,
    forward_send,
):
    seq_place = lax.axis_index("seq")
    core = lax.axis_index("mp")
    section = lax.axis_index("section")
    section_count = lax.axis_size("section")
    run = seq_place // RING
    turn = lax.rem(seq_place, RING)
    column = section // RING
    block = lax.rem(section, RING)
    rows = query_ref.shape[0]
    span = RING * rows
    half = span // 2
    width = w_query_ref.shape[0] // 2
    scaling = 1.0 / math.sqrt(HEAD_WIDTH)
    near = range(1, RING)

    right = run * RING + lax.rem(turn + 1, RING)
    left = run * RING + lax.rem(turn + RING - 1, RING)
    paired_run = run + 1 - 2 * lax.rem(run, 2)
    paired = paired_run * RING + turn
    opposite_run = lax.rem(run + 2, RING)
    opposite = opposite_run * RING + turn
    back_section = lax.rem(section + section_count - 1, section_count)
    next_section = lax.rem(section + 1, section_count)

    depth = RING * RING
    along = block * RING + run
    ahead = lax.rem(along + LEG, depth)
    before = lax.rem(along + depth - LEG, depth)

    def at(col, place):
        return {"section": col * RING + place // RING, "seq": lax.rem(place, RING) * RING + turn}

    turned = block == 0
    from_turned = before < RING
    first_column = lax.rem(column + RING - turned.astype(jnp.int32), RING)
    source_column = lax.rem(column + from_turned.astype(jnp.int32), RING)

    barrier = pltpu.get_barrier_semaphore()
    for step in near:
        signal(barrier, {"seq": run * RING + lax.rem(turn + step, RING)})
    signal(barrier, {"seq": opposite})
    signal(barrier, {"mp": 1 - core})
    for place in (seq_place, paired):
        signal(barrier, {"section": back_section, "seq": place})
        signal(barrier, {"section": next_section, "seq": place})
    signal(barrier, at(column, ahead))
    signal(barrier, at(column, before))

    @pl.when(turned)
    def _():
        signal(barrier, at(first_column, ahead))

    @pl.when(from_turned)
    def _():
        signal(barrier, at(source_column, before))

    @pl.when(run < RING - 1)
    def _():
        signal(barrier, {"seq": seq_place + RING})

    @pl.when(run > 0)
    def _():
        signal(barrier, {"seq": seq_place - RING})

    peers = RING - 1 + 1 + 1 + 4 + 2
    peers = peers + turned.astype(jnp.int32) + from_turned.astype(jnp.int32)
    peers = peers + (run > 0).astype(jnp.int32) + (run < RING - 1).astype(jnp.int32)
    pl.semaphore_wait(barrier, peers)

    sources = (key_ref, value_ref, query_ref, grad_ref)
    buffers = (keys, values, queries, grads)

    def block_rows(place, first=0):
        return pl.ds(pl.multiple_of(first + place * rows, rows), rows)

    def head_cols(kind, head):
        wide = buffers[kind].shape[1]
        return sources[kind].at[:, pl.ds(pl.multiple_of(head * wide, HEAD_WIDTH), wide)]

    def home(kind):
        return span if kind < 2 else 0

    def own_copy(kind):
        return pltpu.make_async_copy(
            head_cols(kind, turn), buffers[kind].at[block_rows(turn, home(kind))], own_sem.at[kind]
        )

    def swap_copy(kind, step):
        to = lax.rem(turn + step, RING)
        return pltpu.make_async_remote_copy(
            src_ref=head_cols(kind, to),
            dst_ref=buffers[kind].at[block_rows(turn, home(kind))],
            send_sem=swap_send.at[kind, step - 1],
            recv_sem=swap_recv.at[kind, step - 1],
            device_id={"seq": run * RING + to},
            device_id_type=MESH,
        )

    def halo_copy(kind, step):
        place = lax.rem(turn + RING - step, RING)
        return pltpu.make_async_remote_copy(
            src_ref=buffers[kind].at[block_rows(place, span)] if step else head_cols(kind, turn),
            dst_ref=buffers[kind].at[block_rows(place)],
            send_sem=halo_send.at[kind, step],
            recv_sem=halo_recv.at[kind, step],
            device_id={"seq": seq_place + RING},
            device_id_type=MESH,
        )

    def line_copy(place):
        return pltpu.make_async_remote_copy(
            src_ref=behind.at[place],
            dst_ref=behind_in.at[place],
            send_sem=line_send.at[place],
            recv_sem=line_recv.at[place],
            device_id={"seq": seq_place - RING},
            device_id_type=MESH,
        )

    def own_weight_copies(head):
        wide = 2 * HEAD_WIDTH
        query_cols = pl.ds(head * wide, wide)
        kv_span = pl.ds(head * HEAD_WIDTH, HEAD_WIDTH)
        return [
            pltpu.make_async_copy(source, target, own_weight_sem.at[head, index])
            for index, (source, target) in enumerate(
                (
                    (w_query_ref.at[:, query_cols], weights.at[head, :, pl.ds(0, wide)]),
                    (key_weight_ref.at[:, kv_span], weights.at[head, :, pl.ds(wide, HEAD_WIDTH)]),
                    (
                        value_weight_ref.at[:, kv_span],
                        weights.at[head, :, pl.ds(wide + HEAD_WIDTH, HEAD_WIDTH)],
                    ),
                )
            )
        ]

    def weight_copy(head):
        return pltpu.make_async_remote_copy(
            src_ref=weights.at[head],
            dst_ref=weights_in.at[head],
            send_sem=weight_send.at[head],
            recv_sem=weight_recv.at[head],
            device_id={"seq": paired},
            device_id_type=MESH,
        )

    def both(ref, place):
        block = ref[place * rows : (place + 1) * rows]
        return jnp.concatenate([block[:, :HEAD_WIDTH], block[:, HEAD_WIDTH:]], axis=0)

    def attend(place):
        query = both(queries, place)
        grad = both(grads, place)
        reach = slice(place * rows, place * rows + span + rows)
        key = keys[reach]
        value = values[reach]
        scores = lax.dot_general(query, key, NT, preferred_element_type=jnp.float32)
        mask = jnp.concatenate([bias[place], bias[place]], axis=0)
        scores = scores * scaling + mask
        raised = jnp.exp(scores - jnp.max(scores, axis=1, keepdims=True))
        weights_full = raised * (1.0 / jnp.sum(raised, axis=1, keepdims=True))
        weights_half = weights_full.astype(jnp.bfloat16)
        attended = jnp.dot(weights_half, value, preferred_element_type=jnp.float32)
        delta = jnp.sum(grad.astype(jnp.float32) * attended, axis=1, keepdims=True)
        grad_weights = lax.dot_general(grad, value, NT, preferred_element_type=jnp.float32)
        grad_scores = (weights_full * (grad_weights - delta)).astype(jnp.bfloat16)
        grad_query = jnp.dot(grad_scores, key, preferred_element_type=jnp.float32) * scaling
        grad_query = grad_query.astype(jnp.bfloat16)
        here = slice(place * rows, (place + 1) * rows)
        held[0, 0, turn, here, :HEAD_WIDTH] = grad_query[:rows]
        held[0, 0, turn, here, HEAD_WIDTH:] = grad_query[rows:]
        terms = (
            lax.dot_general(grad_scores, query, TN, preferred_element_type=jnp.float32) * scaling,
            lax.dot_general(weights_half, grad, TN, preferred_element_type=jnp.float32),
        )
        for kind in (0, 1):
            if place == 0:
                sums[kind, reach] = terms[kind]
            else:
                sums[kind, place * rows : place * rows + span] += terms[kind][:span]
                sums[kind, place * rows + span : place * rows + span + rows] = terms[kind][span:]

        @pl.when(run > 0)
        def _():
            behind[place] = sums[:, here].astype(jnp.bfloat16)
            line_copy(place).start()

    def collect(place):
        @pl.when(run < RING - 1)
        def _():
            line_copy(place).wait_recv()
            there = slice(span + place * rows, span + (place + 1) * rows)
            sums[:, there] += behind_in[place].astype(jnp.float32)

    def across_copy(piece):
        return pltpu.make_async_remote_copy(
            src_ref=held.at[piece, 0, turn],
            dst_ref=held.at[piece, 1, turn],
            send_sem=across_send.at[piece],
            recv_sem=across_recv.at[piece],
            device_id={"seq": opposite},
            device_id_type=MESH,
        )

    def ring_copy(shard, to, send, recv):
        return pltpu.make_async_remote_copy(
            src_ref=shard,
            dst_ref=shard,
            send_sem=send,
            recv_sem=recv,
            device_id={"seq": to},
            device_id_type=MESH,
        )

    def shard_of(piece, line, step):
        return held.at[piece, line, lax.rem(turn + step + RING, RING)]

    def half_of(piece, line, step, start):
        return held.at[piece, line, lax.rem(turn + step + RING, RING), pl.ds(start, half)]

    def right_copy(piece, line, step=0):
        return ring_copy(
            shard_of(piece, line, step), right, right_send.at[piece, line], right_recv.at[piece, line]
        )

    def left_copy(piece, line, step=0):
        return ring_copy(
            shard_of(piece, line, step), left, left_send.at[piece, line], left_recv.at[piece, line]
        )

    def far_right_copy(piece, line, step=-1):
        return ring_copy(
            half_of(piece, line, step, 0),
            right,
            far_right_send.at[piece, line],
            far_right_recv.at[piece, line],
        )

    def far_left_copy(piece, line, step=1):
        return ring_copy(
            half_of(piece, line, step, half),
            left,
            far_left_send.at[piece, line],
            far_left_recv.at[piece, line],
        )

    def along_ring(piece, line):
        right_copy(piece, line).start()
        left_copy(piece, line).start()

    def spread(piece):
        across_copy(piece).start()
        along_ring(piece, 0)

    def from_across(piece):
        across_copy(piece).wait_recv()
        along_ring(piece, 1)

    def farther(piece, line):
        right_copy(piece, line, -1).wait_recv()
        far_right_copy(piece, line).start()
        left_copy(piece, line, 1).wait_recv()
        far_left_copy(piece, line).start()

    def last_of(piece, line):
        far_right_copy(piece, line, -2).wait_recv()
        far_left_copy(piece, line, 2).wait_recv()

    def core_copy(unit):
        return pltpu.make_async_remote_copy(
            src_ref=part.at[unit, 1 - core],
            dst_ref=part_in.at[unit],
            send_sem=core_send.at[unit],
            recv_sem=core_recv.at[unit],
            device_id={"mp": 1 - core},
            device_id_type=MESH,
        )

    def section_copy(unit):
        line, owner = divmod(unit, 2)
        row = opposite_run if line else run
        return pltpu.make_async_remote_copy(
            src_ref=ready.at[unit],
            dst_ref=landed.at[row],
            send_sem=section_send.at[unit],
            recv_sem=section_recv.at[row],
            device_id={"section": back_section, "seq": paired if owner else seq_place},
            device_id_type=MESH,
        )

    def relay_copy():
        return pltpu.make_async_remote_copy(
            src_ref=ready.at[0],
            dst_ref=relayed,
            send_sem=section_send.at[0],
            recv_sem=relay_recv.at[0],
            device_id=at(first_column, ahead),
            device_id_type=MESH,
        )

    def forward_copy():
        return pltpu.make_async_remote_copy(
            src_ref=relayed,
            dst_ref=landed.at[opposite_run],
            send_sem=forward_send.at[0],
            recv_sem=section_recv.at[opposite_run],
            device_id=at(column, ahead),
            device_id_type=MESH,
        )

    def land(row):
        pltpu.make_async_remote_copy(
            src_ref=landed.at[row],
            dst_ref=landed.at[row],
            send_sem=forward_send.at[0],
            recv_sem=section_recv.at[row],
            device_id={"section": back_section},
            device_id_type=MESH,
        ).wait_recv()
        out_ref[pl.ds(pl.multiple_of(row * span, span), span), :] = jnp.transpose(landed[row])

    def project(unit):
        line, owner = divmod(unit, 2)
        source = weights_in if owner else weights
        product = None
        for head in range(RING):
            for piece in range(PIECES):
                weight = source[head, :, piece * 2 * HEAD_WIDTH : (piece + 1) * 2 * HEAD_WIDTH]
                term = lax.dot_general(
                    weight, held[piece, line, head], NT, preferred_element_type=jnp.float32
                )
                product = term if product is None else product + term
        part[unit, 0] = product[:width]
        part[unit, 1] = product[width:]
        core_copy(unit).start()

    def hand_over(unit):
        core_copy(unit).wait_recv()
        ready[unit] = (part[unit, core] + part_in[unit]).astype(jnp.bfloat16)
        if unit == 0:
            relay_copy().start()
        else:
            section_copy(unit).start()

    order = (1, 3, 2)
    for step in order:
        for kind in (0, 1):
            swap_copy(kind, step).start()

    @pl.when(run < RING - 1)
    def _():
        for kind in (0, 1):
            halo_copy(kind, 0).start()

    for kind in range(4):
        own_copy(kind).start()
    for step in order:
        for kind in (2, 3):
            swap_copy(kind, step).start()
    for head in range(RING):
        for copy in own_weight_copies(head):
            copy.start()

    query_row = lax.broadcasted_iota(jnp.int32, (rows, rows), 0)
    key_row = lax.broadcasted_iota(jnp.int32, (rows, rows), 1)

    def block_docs(place):
        start = pl.multiple_of(jnp.maximum(place, 0) * rows, rows)
        return docs_ref[:, pl.ds(start, rows)].astype(jnp.float32)

    for place in range(RING):
        query_place = run * RING + place
        query_docs = jnp.transpose(jnp.broadcast_to(block_docs(query_place), (rows, rows)))
        for step in range(RING + 1):
            offset = query_row - key_row + step * rows
            allowed = (query_docs == block_docs(query_place - step)) & (offset >= 0)
            allowed = allowed & (offset < WINDOW)
            allowed = allowed & (jnp.full((rows, rows), query_place, jnp.int32) >= step)
            first = (RING - step) * rows
            bias[place, :, first : first + rows] = jnp.where(allowed, 0.0, -jnp.inf)

    @pl.when(run == 0)
    def _():
        for buffer in (keys, values):
            buffer[:span] = jnp.zeros((span, HEAD_WIDTH), jnp.bfloat16)

    for step in order:
        for kind in (0, 1):
            swap_copy(kind, step).wait_recv()

        @pl.when(run < RING - 1)
        def _():
            for kind in (0, 1):
                halo_copy(kind, step).start()

    for head in range(RING):
        for copy in own_weight_copies(head):
            copy.wait()
    for head in range(EARLY_WEIGHTS):
        weight_copy(head).start()
    for kind in range(4):
        own_copy(kind).wait()
    for step in order:
        for kind in (2, 3):
            swap_copy(kind, step).wait_recv()

    @pl.when(run > 0)
    def _():
        for step in range(RING):
            for kind in (0, 1):
                halo_copy(kind, step).wait_recv()

    for place in range(RING):
        attend(place)
    spread(0)
    for head in range(EARLY_WEIGHTS, RING):
        weight_copy(head).start()
    for place in range(RING):
        collect(place)
    for kind in (0, 1):
        first = kind * HEAD_WIDTH
        held[1, 0, turn, :, first : first + HEAD_WIDTH] = sums[kind, span:].astype(jnp.bfloat16)
    spread(1)
    farther(0, 0)
    from_across(0)
    farther(1, 0)
    for piece in range(PIECES):
        last_of(piece, 0)
    project(0)
    farther(0, 1)
    from_across(1)
    hand_over(0)
    for head in range(RING):
        weight_copy(head).wait_recv()
    project(1)
    farther(1, 1)
    hand_over(1)
    for piece in range(PIECES):
        last_of(piece, 1)
    project(2)
    project(3)
    hand_over(2)
    hand_over(3)
    relay_copy().wait_recv()
    forward_copy().start()
    for row in (lax.rem(run + 1, RING), opposite_run, lax.rem(run + 3, RING), run):
        land(row)

    for unit in range(4):
        core_copy(unit).wait_send()
        section_copy(unit).wait_send()
    forward_copy().wait_send()
    for piece in range(PIECES):
        across_copy(piece).wait_send()
        for line in (0, 1):
            right_copy(piece, line).wait_send()
            left_copy(piece, line).wait_send()
            far_right_copy(piece, line).wait_send()
            far_left_copy(piece, line).wait_send()
    for head in range(RING):
        weight_copy(head).wait_send()
    for kind in range(4):
        for step in near:
            swap_copy(kind, step).wait_send()

    @pl.when(run < RING - 1)
    def _():
        for kind in (0, 1):
            for step in range(RING):
                halo_copy(kind, step).wait_send()

    @pl.when(run > 0)
    def _():
        for place in range(RING):
            line_copy(place).wait_send()


def cascade(docs, query, key, value, grad, w_query, key_weight, value_weight):
    rows = query.shape[0]
    seq_count = lax.axis_size("seq")
    width = w_query.shape[0] // 2
    span = RING * rows
    wide = 2 * HEAD_WIDTH
    dma = pltpu.SemaphoreType.DMA
    whole = pl.BlockSpec(memory_space=pltpu.VMEM)
    stay = pl.BlockSpec(memory_space=pl.ANY)
    return pl.pallas_call(
        cascade_kernel,
        out_shape=jax.ShapeDtypeStruct((seq_count * rows, width), jnp.bfloat16),
        in_specs=[whole] + [stay] * 7,
        out_specs=whole,
        scratch_shapes=[
            pltpu.VMEM((2 * span, HEAD_WIDTH), jnp.bfloat16),
            pltpu.VMEM((2 * span, HEAD_WIDTH), jnp.bfloat16),
            pltpu.VMEM((span, wide), jnp.bfloat16),
            pltpu.VMEM((span, wide), jnp.bfloat16),
            pltpu.VMEM((RING, rows, span + rows), jnp.float32),
            pltpu.VMEM((2, 2 * span, HEAD_WIDTH), jnp.float32),
            pltpu.VMEM((RING, 2, rows, HEAD_WIDTH), jnp.bfloat16),
            pltpu.VMEM((RING, 2, rows, HEAD_WIDTH), jnp.bfloat16),
            pltpu.VMEM((RING, 2 * width, 2 * wide), jnp.bfloat16),
            pltpu.VMEM((RING, 2 * width, 2 * wide), jnp.bfloat16),
            pltpu.VMEM((PIECES, 2, RING, span, wide), jnp.bfloat16),
            pltpu.VMEM((4, 2, width, span), jnp.float32),
            pltpu.VMEM((4, width, span), jnp.float32),
            pltpu.VMEM((4, width, span), jnp.bfloat16),
            pltpu.VMEM((width, span), jnp.bfloat16),
            pltpu.VMEM((RING, width, span), jnp.bfloat16),
            dma((4,)),
            dma((RING, 3)),
            dma((4, RING - 1)),
            dma((4, RING - 1)),
            dma((2, RING)),
            dma((2, RING)),
            *([dma((RING,))] * 4),
            *([dma((PIECES,))] * 2),
            *([dma((PIECES, 2))] * 8),
            *([dma((4,))] * 4),
            *([dma((1,))] * 2),
        ],
        compiler_params=pltpu.CompilerParams(collective_id=0, has_side_effects=True),
    )(docs, query, key, value, grad, w_query, key_weight, value_weight)


def per_device(
    query_rows,
    key_row_matrix,
    value_row_matrix,
    out_grad,
    w_query,
    key_weight,
    value_weight,
    doc_ids,
):
    upstream = cascade(
        doc_ids,
        query_rows[0],
        key_row_matrix[0],
        value_row_matrix[0],
        out_grad[0],
        w_query[0],
        key_weight[0],
        value_weight[0],
    )
    return upstream[None]


def solution(mesh):
    placed = (
        P("section", "seq", "mp"),
        P("section", "seq", "mp"),
        P("section", "seq", "mp"),
        P("section", "seq", "mp"),
        P("section", "seq", "mp"),
        P("section", "seq", "mp"),
        P("section", "seq", "mp"),
        P("section", None),
    )
    return jax.shard_map(
        per_device,
        mesh=mesh,
        in_specs=placed,
        out_specs=P("section", None, ("seq", "mp")),
        check_vma=False,
    )
```

```python
import math

import jax
import jax.numpy as jnp
from jax import lax
from jax.experimental import pallas as pl
from jax.experimental.pallas import tpu as pltpu
from jax.sharding import PartitionSpec as P

HEAD_WIDTH = 128
WINDOW = 512
RING = 4
LEG = 6
MESH = pl.DeviceIdType.MESH
NT = (((1,), (1,)), ((), ()))
TN = (((0,), (0,)), ((), ()))
PIECES = 2
EARLY_EVEN = 4
EARLY_ODD = 2


def signal(semaphore, device):
    pl.semaphore_signal(semaphore, inc=1, device_id=device, device_id_type=MESH)


def cascade_kernel(
    docs_ref,
    query_ref,
    key_ref,
    value_ref,
    grad_ref,
    w_query_ref,
    key_weight_ref,
    value_weight_ref,
    out_ref,
    keys,
    values,
    queries,
    grads,
    bias,
    sums,
    behind,
    behind_in,
    weights,
    weights_in,
    held,
    part,
    part_in,
    ready,
    relayed,
    landed,
    own_sem,
    own_weight_sem,
    swap_send,
    swap_recv,
    halo_send,
    halo_recv,
    line_send,
    line_recv,
    weight_send,
    weight_recv,
    across_send,
    across_recv,
    right_send,
    right_recv,
    left_send,
    left_recv,
    far_right_send,
    far_right_recv,
    far_left_send,
    far_left_recv,
    core_send,
    core_recv,
    section_send,
    section_recv,
    relay_recv,
    forward_send,
):
    seq_place = lax.axis_index("seq")
    core = lax.axis_index("mp")
    section = lax.axis_index("section")
    section_count = lax.axis_size("section")
    run = seq_place // RING
    turn = lax.rem(seq_place, RING)
    column = section // RING
    block = lax.rem(section, RING)
    rows = query_ref.shape[0]
    span = RING * rows
    half = span // 2
    width = w_query_ref.shape[0] // 2
    scaling = 1.0 / math.sqrt(HEAD_WIDTH)
    near = range(1, RING)

    right = run * RING + lax.rem(turn + 1, RING)
    left = run * RING + lax.rem(turn + RING - 1, RING)
    paired_run = run + 1 - 2 * lax.rem(run, 2)
    paired = paired_run * RING + turn
    opposite_run = lax.rem(run + 2, RING)
    opposite = opposite_run * RING + turn
    back_section = lax.rem(section + section_count - 1, section_count)
    next_section = lax.rem(section + 1, section_count)

    depth = RING * RING
    along = block * RING + run
    odd = lax.rem(run, 2) == 1
    ahead = lax.rem(along + LEG, depth)
    before = lax.rem(along + depth - LEG, depth)
    after_relay = lax.rem(along + LEG - 1, depth)
    before_relay = lax.rem(along + depth - LEG + 1, depth)

    def at(col, place):
        return {"section": col * RING + place // RING, "seq": lax.rem(place, RING) * RING + turn}

    first_column = lax.rem(column + RING - (block == 0).astype(jnp.int32), RING)
    source_column = lax.rem(column + (before < RING).astype(jnp.int32), RING)

    barrier = pltpu.get_barrier_semaphore()
    for step in near:
        signal(barrier, {"seq": run * RING + lax.rem(turn + step, RING)})
    signal(barrier, {"seq": opposite})
    signal(barrier, {"mp": 1 - core})
    for place in (seq_place, paired):
        signal(barrier, {"section": back_section, "seq": place})
        signal(barrier, {"section": next_section, "seq": place})

    @pl.when(odd)
    def _():
        signal(barrier, at(first_column, ahead))
        signal(barrier, at(source_column, before))
        signal(barrier, at(column, after_relay))

    @pl.when(jnp.logical_not(odd))
    def _():
        signal(barrier, at(column, before_relay))

    @pl.when(run < RING - 1)
    def _():
        signal(barrier, {"seq": seq_place + RING})

    @pl.when(run > 0)
    def _():
        signal(barrier, {"seq": seq_place - RING})

    peers = RING - 1 + 1 + 1 + 4 + 1 + 2 * odd.astype(jnp.int32)
    peers = peers + (run > 0).astype(jnp.int32) + (run < RING - 1).astype(jnp.int32)

    sources = (key_ref, value_ref, query_ref, grad_ref)
    buffers = (keys, values, queries, grads)

    def block_rows(place, first=0):
        return pl.ds(pl.multiple_of(first + place * rows, rows), rows)

    def head_cols(kind, head):
        wide = buffers[kind].shape[1]
        return sources[kind].at[:, pl.ds(pl.multiple_of(head * wide, HEAD_WIDTH), wide)]

    def home(kind):
        return span if kind < 2 else 0

    def own_copy(kind):
        return pltpu.make_async_copy(
            head_cols(kind, turn), buffers[kind].at[block_rows(turn, home(kind))], own_sem.at[kind]
        )

    def swap_copy(kind, step):
        to = lax.rem(turn + step, RING)
        return pltpu.make_async_remote_copy(
            src_ref=head_cols(kind, to),
            dst_ref=buffers[kind].at[block_rows(turn, home(kind))],
            send_sem=swap_send.at[kind, step - 1],
            recv_sem=swap_recv.at[kind, step - 1],
            device_id={"seq": run * RING + to},
            device_id_type=MESH,
        )

    def halo_copy(kind, step):
        place = lax.rem(turn + RING - step, RING)
        return pltpu.make_async_remote_copy(
            src_ref=buffers[kind].at[block_rows(place, span)] if step else head_cols(kind, turn),
            dst_ref=buffers[kind].at[block_rows(place)],
            send_sem=halo_send.at[kind, step],
            recv_sem=halo_recv.at[kind, step],
            device_id={"seq": seq_place + RING},
            device_id_type=MESH,
        )

    def line_copy(place):
        return pltpu.make_async_remote_copy(
            src_ref=behind.at[place],
            dst_ref=behind_in.at[place],
            send_sem=line_send.at[place],
            recv_sem=line_recv.at[place],
            device_id={"seq": seq_place - RING},
            device_id_type=MESH,
        )

    def own_weight_copies(head):
        wide = 2 * HEAD_WIDTH
        query_cols = pl.ds(head * wide, wide)
        kv_span = pl.ds(head * HEAD_WIDTH, HEAD_WIDTH)
        return [
            pltpu.make_async_copy(source, target, own_weight_sem.at[head, index])
            for index, (source, target) in enumerate(
                (
                    (w_query_ref.at[:, query_cols], weights.at[head, :, pl.ds(0, wide)]),
                    (key_weight_ref.at[:, kv_span], weights.at[head, :, pl.ds(wide, HEAD_WIDTH)]),
                    (
                        value_weight_ref.at[:, kv_span],
                        weights.at[head, :, pl.ds(wide + HEAD_WIDTH, HEAD_WIDTH)],
                    ),
                )
            )
        ]

    def weight_copy(head):
        return pltpu.make_async_remote_copy(
            src_ref=weights.at[head],
            dst_ref=weights_in.at[head],
            send_sem=weight_send.at[head],
            recv_sem=weight_recv.at[head],
            device_id={"seq": paired},
            device_id_type=MESH,
        )

    def both(ref, place):
        block = ref[place * rows : (place + 1) * rows]
        return jnp.concatenate([block[:, :HEAD_WIDTH], block[:, HEAD_WIDTH:]], axis=0)

    def attend(place):
        query = both(queries, place)
        grad = both(grads, place)
        reach = slice(place * rows, place * rows + span + rows)
        key = keys[reach]
        value = values[reach]
        scores = lax.dot_general(query, key, NT, preferred_element_type=jnp.float32)
        mask = jnp.concatenate([bias[place], bias[place]], axis=0)
        scores = scores * scaling + mask
        raised = jnp.exp(scores - jnp.max(scores, axis=1, keepdims=True))
        weights_full = raised * (1.0 / jnp.sum(raised, axis=1, keepdims=True))
        weights_half = weights_full.astype(jnp.bfloat16)
        attended = jnp.dot(weights_half, value, preferred_element_type=jnp.float32)
        delta = jnp.sum(grad.astype(jnp.float32) * attended, axis=1, keepdims=True)
        grad_weights = lax.dot_general(grad, value, NT, preferred_element_type=jnp.float32)
        grad_scores = (weights_full * (grad_weights - delta)).astype(jnp.bfloat16)
        grad_query = jnp.dot(grad_scores, key, preferred_element_type=jnp.float32) * scaling
        grad_query = grad_query.astype(jnp.bfloat16)
        here = slice(place * rows, (place + 1) * rows)
        held[0, 0, turn, here, :HEAD_WIDTH] = grad_query[:rows]
        held[0, 0, turn, here, HEAD_WIDTH:] = grad_query[rows:]
        terms = (
            lax.dot_general(grad_scores, query, TN, preferred_element_type=jnp.float32) * scaling,
            lax.dot_general(weights_half, grad, TN, preferred_element_type=jnp.float32),
        )
        for kind in (0, 1):
            if place == 0:
                sums[kind, reach] = terms[kind]
            else:
                sums[kind, place * rows : place * rows + span] += terms[kind][:span]
                sums[kind, place * rows + span : place * rows + span + rows] = terms[kind][span:]

        @pl.when(run > 0)
        def _():
            behind[place] = sums[:, here].astype(jnp.bfloat16)
            line_copy(place).start()

    def collect(place):
        @pl.when(run < RING - 1)
        def _():
            line_copy(place).wait_recv()
            there = slice(span + place * rows, span + (place + 1) * rows)
            sums[:, there] += behind_in[place].astype(jnp.float32)

    def across_copy(piece):
        return pltpu.make_async_remote_copy(
            src_ref=held.at[piece, 0, turn],
            dst_ref=held.at[piece, 1, turn],
            send_sem=across_send.at[piece],
            recv_sem=across_recv.at[piece],
            device_id={"seq": opposite},
            device_id_type=MESH,
        )

    def ring_copy(shard, to, send, recv):
        return pltpu.make_async_remote_copy(
            src_ref=shard,
            dst_ref=shard,
            send_sem=send,
            recv_sem=recv,
            device_id={"seq": to},
            device_id_type=MESH,
        )

    def shard_of(piece, line, step):
        return held.at[piece, line, lax.rem(turn + step + RING, RING)]

    def half_of(piece, line, step, start):
        return held.at[piece, line, lax.rem(turn + step + RING, RING), pl.ds(start, half)]

    def right_copy(piece, line, step=0):
        return ring_copy(
            shard_of(piece, line, step), right, right_send.at[piece, line], right_recv.at[piece, line]
        )

    def left_copy(piece, line, step=0):
        return ring_copy(
            shard_of(piece, line, step), left, left_send.at[piece, line], left_recv.at[piece, line]
        )

    def far_right_copy(piece, line, step=-1):
        return ring_copy(
            half_of(piece, line, step, 0),
            right,
            far_right_send.at[piece, line],
            far_right_recv.at[piece, line],
        )

    def far_left_copy(piece, line, step=1):
        return ring_copy(
            half_of(piece, line, step, half),
            left,
            far_left_send.at[piece, line],
            far_left_recv.at[piece, line],
        )

    def along_ring(piece, line):
        right_copy(piece, line).start()
        left_copy(piece, line).start()

    def spread(piece):
        across_copy(piece).start()
        along_ring(piece, 0)

    def from_across(piece):
        across_copy(piece).wait_recv()
        along_ring(piece, 1)

    def farther(piece, line):
        right_copy(piece, line, -1).wait_recv()
        far_right_copy(piece, line).start()
        left_copy(piece, line, 1).wait_recv()
        far_left_copy(piece, line).start()

    def last_of(piece, line):
        far_right_copy(piece, line, -2).wait_recv()
        far_left_copy(piece, line, 2).wait_recv()

    def core_copy(unit):
        return pltpu.make_async_remote_copy(
            src_ref=part.at[unit, 1 - core],
            dst_ref=part_in.at[unit],
            send_sem=core_send.at[unit],
            recv_sem=core_recv.at[unit],
            device_id={"mp": 1 - core},
            device_id_type=MESH,
        )

    def section_copy(unit):
        line, owner = divmod(unit, 2)
        row = opposite_run if line else run
        return pltpu.make_async_remote_copy(
            src_ref=ready.at[unit],
            dst_ref=landed.at[row],
            send_sem=section_send.at[unit],
            recv_sem=section_recv.at[row],
            device_id={"section": back_section, "seq": paired if owner else seq_place},
            device_id_type=MESH,
        )

    def relay_copy(unit):
        return pltpu.make_async_remote_copy(
            src_ref=ready.at[unit],
            dst_ref=relayed.at[unit // 2],
            send_sem=section_send.at[unit],
            recv_sem=relay_recv.at[unit // 2],
            device_id=at(first_column, ahead),
            device_id_type=MESH,
        )

    def forward_copy(unit):
        row = run if unit // 2 else opposite_run
        return pltpu.make_async_remote_copy(
            src_ref=relayed.at[unit // 2],
            dst_ref=landed.at[row],
            send_sem=forward_send.at[unit // 2],
            recv_sem=section_recv.at[row],
            device_id=at(column, after_relay),
            device_id_type=MESH,
        )

    def forward(unit):
        @pl.when(odd)
        def _():
            relay_copy(unit).wait_recv()
            forward_copy(unit).start()

    def land(row):
        pltpu.make_async_remote_copy(
            src_ref=landed.at[row],
            dst_ref=landed.at[row],
            send_sem=forward_send.at[0],
            recv_sem=section_recv.at[row],
            device_id={"section": back_section},
            device_id_type=MESH,
        ).wait_recv()
        out_ref[pl.ds(pl.multiple_of(row * span, span), span), :] = jnp.transpose(landed[row])

    def project(unit):
        line, owner = divmod(unit, 2)
        source = weights_in if owner else weights
        product = None
        for head in range(RING):
            for piece in range(PIECES):
                weight = source[head, :, piece * 2 * HEAD_WIDTH : (piece + 1) * 2 * HEAD_WIDTH]
                term = lax.dot_general(
                    weight, held[piece, line, head], NT, preferred_element_type=jnp.float32
                )
                product = term if product is None else product + term
        part[unit, 0] = product[:width]
        part[unit, 1] = product[width:]
        core_copy(unit).start()

    def hand_over(unit):
        core_copy(unit).wait_recv()
        ready[unit] = (part[unit, core] + part_in[unit]).astype(jnp.bfloat16)
        if unit % 2 == 0:
            section_copy(unit).start()
        else:

            @pl.when(odd)
            def _():
                relay_copy(unit).start()

            @pl.when(jnp.logical_not(odd))
            def _():
                section_copy(unit).start()

    for head in range(RING):
        for copy in own_weight_copies(head):
            copy.start()
    for kind in range(4):
        own_copy(kind).start()
    pl.semaphore_wait(barrier, peers)
    order = (1, 3, 2)
    for step in order:
        for kind in (0, 1):
            swap_copy(kind, step).start()

    @pl.when(run < RING - 1)
    def _():
        for kind in (0, 1):
            halo_copy(kind, 0).start()

    for step in order:
        for kind in (2, 3):
            swap_copy(kind, step).start()

    @pl.when(odd)
    def _():
        for head in range(EARLY_ODD):
            for copy in own_weight_copies(head):
                copy.wait()
            weight_copy(head).start()

    query_row = lax.broadcasted_iota(jnp.int32, (rows, rows), 0)
    key_row = lax.broadcasted_iota(jnp.int32, (rows, rows), 1)

    def block_docs(place):
        start = pl.multiple_of(jnp.maximum(place, 0) * rows, rows)
        return docs_ref[:, pl.ds(start, rows)].astype(jnp.float32)

    for place in range(RING):
        query_place = run * RING + place
        query_docs = jnp.transpose(jnp.broadcast_to(block_docs(query_place), (rows, rows)))
        for step in range(RING + 1):
            offset = query_row - key_row + step * rows
            allowed = (query_docs == block_docs(query_place - step)) & (offset >= 0)
            allowed = allowed & (offset < WINDOW)
            allowed = allowed & (jnp.full((rows, rows), query_place, jnp.int32) >= step)
            first = (RING - step) * rows
            bias[place, :, first : first + rows] = jnp.where(allowed, 0.0, -jnp.inf)

    @pl.when(run == 0)
    def _():
        for buffer in (keys, values):
            buffer[:span] = jnp.zeros((span, HEAD_WIDTH), jnp.bfloat16)

    for step in order:
        for kind in (0, 1):
            swap_copy(kind, step).wait_recv()

        @pl.when(run < RING - 1)
        def _():
            for kind in (0, 1):
                halo_copy(kind, step).start()

    @pl.when(jnp.logical_not(odd))
    def _():
        for head in range(EARLY_EVEN):
            for copy in own_weight_copies(head):
                copy.wait()
            weight_copy(head).start()

    for kind in range(4):
        own_copy(kind).wait()
    for step in order:
        for kind in (2, 3):
            swap_copy(kind, step).wait_recv()

    @pl.when(run > 0)
    def _():
        for step in range(RING):
            for kind in (0, 1):
                halo_copy(kind, step).wait_recv()

    for place in range(RING):
        attend(place)
    spread(0)
    for place in range(RING):
        collect(place)
    for kind in (0, 1):
        first = kind * HEAD_WIDTH
        held[1, 0, turn, :, first : first + HEAD_WIDTH] = sums[kind, span:].astype(jnp.bfloat16)
    spread(1)

    @pl.when(odd)
    def _():
        for head in range(EARLY_ODD, RING):
            for copy in own_weight_copies(head):
                copy.wait()
            weight_copy(head).start()

    @pl.when(jnp.logical_not(odd))
    def _():
        for head in range(EARLY_EVEN, RING):
            for copy in own_weight_copies(head):
                copy.wait()
            weight_copy(head).start()


    farther(0, 0)
    from_across(0)
    farther(1, 0)
    for piece in range(PIECES):
        last_of(piece, 0)
    project(0)
    farther(0, 1)
    from_across(1)
    hand_over(0)
    for head in range(RING):
        weight_copy(head).wait_recv()
    project(1)
    farther(1, 1)
    hand_over(1)
    for piece in range(PIECES):
        last_of(piece, 1)
    project(2)
    hand_over(2)
    project(3)
    hand_over(3)
    forward(1)
    forward(3)
    for row in (run, opposite_run, paired_run, lax.rem(paired_run + 2, RING)):
        land(row)

    for unit in range(4):
        core_copy(unit).wait_send()
        section_copy(unit).wait_send()

    @pl.when(odd)
    def _():
        for unit in (1, 3):
            forward_copy(unit).wait_send()

    for piece in range(PIECES):
        across_copy(piece).wait_send()
        for line in (0, 1):
            right_copy(piece, line).wait_send()
            left_copy(piece, line).wait_send()
            far_right_copy(piece, line).wait_send()
            far_left_copy(piece, line).wait_send()
    for head in range(RING):
        weight_copy(head).wait_send()
    for kind in range(4):
        for step in near:
            swap_copy(kind, step).wait_send()

    @pl.when(run < RING - 1)
    def _():
        for kind in (0, 1):
            for step in range(RING):
                halo_copy(kind, step).wait_send()

    @pl.when(run > 0)
    def _():
        for place in range(RING):
            line_copy(place).wait_send()


def cascade(docs, query, key, value, grad, w_query, key_weight, value_weight):
    rows = query.shape[0]
    seq_count = lax.axis_size("seq")
    width = w_query.shape[0] // 2
    span = RING * rows
    wide = 2 * HEAD_WIDTH
    dma = pltpu.SemaphoreType.DMA
    whole = pl.BlockSpec(memory_space=pltpu.VMEM)
    stay = pl.BlockSpec(memory_space=pl.ANY)
    return pl.pallas_call(
        cascade_kernel,
        out_shape=jax.ShapeDtypeStruct((seq_count * rows, width), jnp.bfloat16),
        in_specs=[whole] + [stay] * 7,
        out_specs=whole,
        scratch_shapes=[
            pltpu.VMEM((2 * span, HEAD_WIDTH), jnp.bfloat16),
            pltpu.VMEM((2 * span, HEAD_WIDTH), jnp.bfloat16),
            pltpu.VMEM((span, wide), jnp.bfloat16),
            pltpu.VMEM((span, wide), jnp.bfloat16),
            pltpu.VMEM((RING, rows, span + rows), jnp.float32),
            pltpu.VMEM((2, 2 * span, HEAD_WIDTH), jnp.float32),
            pltpu.VMEM((RING, 2, rows, HEAD_WIDTH), jnp.bfloat16),
            pltpu.VMEM((RING, 2, rows, HEAD_WIDTH), jnp.bfloat16),
            pltpu.VMEM((RING, 2 * width, 2 * wide), jnp.bfloat16),
            pltpu.VMEM((RING, 2 * width, 2 * wide), jnp.bfloat16),
            pltpu.VMEM((PIECES, 2, RING, span, wide), jnp.bfloat16),
            pltpu.VMEM((4, 2, width, span), jnp.float32),
            pltpu.VMEM((4, width, span), jnp.float32),
            pltpu.VMEM((4, width, span), jnp.bfloat16),
            pltpu.VMEM((2, width, span), jnp.bfloat16),
            pltpu.VMEM((RING, width, span), jnp.bfloat16),
            dma((4,)),
            dma((RING, 3)),
            dma((4, RING - 1)),
            dma((4, RING - 1)),
            dma((2, RING)),
            dma((2, RING)),
            *([dma((RING,))] * 4),
            *([dma((PIECES,))] * 2),
            *([dma((PIECES, 2))] * 8),
            *([dma((4,))] * 4),
            *([dma((2,))] * 2),
        ],
        compiler_params=pltpu.CompilerParams(collective_id=0, has_side_effects=True),
    )(docs, query, key, value, grad, w_query, key_weight, value_weight)


def per_device(
    query_rows,
    key_row_matrix,
    value_row_matrix,
    out_grad,
    w_query,
    key_weight,
    value_weight,
    doc_ids,
):
    upstream = cascade(
        doc_ids,
        query_rows[0],
        key_row_matrix[0],
        value_row_matrix[0],
        out_grad[0],
        w_query[0],
        key_weight[0],
        value_weight[0],
    )
    return upstream[None]


def solution(mesh):
    placed = (
        P("section", "seq", "mp"),
        P("section", "seq", "mp"),
        P("section", "seq", "mp"),
        P("section", "seq", "mp"),
        P("section", "seq", "mp"),
        P("section", "seq", "mp"),
        P("section", "seq", "mp"),
        P("section", None),
    )
    return jax.shard_map(
        per_device,
        mesh=mesh,
        in_specs=placed,
        out_specs=P("section", None, ("seq", "mp")),
        check_vma=False,
    )
```

```python
import math

import jax
import jax.numpy as jnp
from jax import lax
from jax.experimental import pallas as pl
from jax.experimental.pallas import tpu as pltpu
from jax.sharding import PartitionSpec as P

HEAD_WIDTH = 128
WINDOW = 512
RING = 4
LEG = 6
MESH = pl.DeviceIdType.MESH
NT = (((1,), (1,)), ((), ()))
TN = (((0,), (0,)), ((), ()))
PIECES = 2
EARLY_EVEN = 4
EARLY_ODD = 2


def signal(semaphore, device):
    pl.semaphore_signal(semaphore, inc=1, device_id=device, device_id_type=MESH)


def cascade_kernel(
    docs_ref,
    query_ref,
    key_ref,
    value_ref,
    grad_ref,
    w_query_ref,
    key_weight_ref,
    value_weight_ref,
    out_ref,
    keys,
    values,
    queries,
    grads,
    bias,
    sums,
    behind,
    behind_in,
    weights,
    weights_in,
    held,
    part,
    part_in,
    ready,
    relayed,
    landed,
    own_sem,
    own_weight_sem,
    swap_send,
    swap_recv,
    halo_send,
    halo_recv,
    line_send,
    line_recv,
    weight_send,
    weight_recv,
    across_send,
    across_recv,
    right_send,
    right_recv,
    left_send,
    left_recv,
    far_right_send,
    far_right_recv,
    far_left_send,
    far_left_recv,
    core_send,
    core_recv,
    section_send,
    section_recv,
    relay_recv,
    forward_send,
):
    seq_place = lax.axis_index("seq")
    core = lax.axis_index("mp")
    section = lax.axis_index("section")
    section_count = lax.axis_size("section")
    run = seq_place // RING
    turn = lax.rem(seq_place, RING)
    column = section // RING
    block = lax.rem(section, RING)
    rows = query_ref.shape[0]
    span = RING * rows
    half = span // 2
    width = w_query_ref.shape[0] // 2
    scaling = 1.0 / math.sqrt(HEAD_WIDTH)
    near = range(1, RING)

    right = run * RING + lax.rem(turn + 1, RING)
    left = run * RING + lax.rem(turn + RING - 1, RING)
    paired_run = run + 1 - 2 * lax.rem(run, 2)
    paired = paired_run * RING + turn
    opposite_run = lax.rem(run + 2, RING)
    opposite = opposite_run * RING + turn
    back_section = lax.rem(section + section_count - 1, section_count)
    next_section = lax.rem(section + 1, section_count)

    depth = RING * RING
    along = block * RING + run
    odd = lax.rem(run, 2) == 1
    ahead = lax.rem(along + LEG, depth)
    before = lax.rem(along + depth - LEG, depth)
    after_relay = lax.rem(along + LEG - 1, depth)
    before_relay = lax.rem(along + depth - LEG + 1, depth)

    def at(col, place):
        return {"section": col * RING + place // RING, "seq": lax.rem(place, RING) * RING + turn}

    first_column = lax.rem(column + RING - (block == 0).astype(jnp.int32), RING)
    source_column = lax.rem(column + (before < RING).astype(jnp.int32), RING)

    barrier = pltpu.get_barrier_semaphore()
    for step in near:
        signal(barrier, {"seq": run * RING + lax.rem(turn + step, RING)})
    signal(barrier, {"seq": opposite})
    signal(barrier, {"mp": 1 - core})
    for place in (seq_place, paired):
        signal(barrier, {"section": back_section, "seq": place})
        signal(barrier, {"section": next_section, "seq": place})

    @pl.when(odd)
    def _():
        signal(barrier, at(first_column, ahead))
        signal(barrier, at(source_column, before))
        signal(barrier, at(column, after_relay))

    @pl.when(jnp.logical_not(odd))
    def _():
        signal(barrier, at(column, before_relay))

    @pl.when(run < RING - 1)
    def _():
        signal(barrier, {"seq": seq_place + RING})

    @pl.when(run > 0)
    def _():
        signal(barrier, {"seq": seq_place - RING})

    peers = RING - 1 + 1 + 1 + 4 + 1 + 2 * odd.astype(jnp.int32)
    peers = peers + (run > 0).astype(jnp.int32) + (run < RING - 1).astype(jnp.int32)

    sources = (key_ref, value_ref, query_ref, grad_ref)
    buffers = (keys, values, queries, grads)

    def block_rows(place, first=0):
        return pl.ds(pl.multiple_of(first + place * rows, rows), rows)

    def head_cols(kind, head):
        wide = buffers[kind].shape[1]
        return sources[kind].at[:, pl.ds(pl.multiple_of(head * wide, HEAD_WIDTH), wide)]

    def home(kind):
        return span if kind < 2 else 0

    def own_copy(kind):
        return pltpu.make_async_copy(
            head_cols(kind, turn), buffers[kind].at[block_rows(turn, home(kind))], own_sem.at[kind]
        )

    def swap_copy(kind, step):
        to = lax.rem(turn + step, RING)
        return pltpu.make_async_remote_copy(
            src_ref=head_cols(kind, to),
            dst_ref=buffers[kind].at[block_rows(turn, home(kind))],
            send_sem=swap_send.at[kind, step - 1],
            recv_sem=swap_recv.at[kind, step - 1],
            device_id={"seq": run * RING + to},
            device_id_type=MESH,
        )

    def halo_copy(kind, step):
        place = lax.rem(turn + RING - step, RING)
        return pltpu.make_async_remote_copy(
            src_ref=buffers[kind].at[block_rows(place, span)] if step else head_cols(kind, turn),
            dst_ref=buffers[kind].at[block_rows(place)],
            send_sem=halo_send.at[kind, step],
            recv_sem=halo_recv.at[kind, step],
            device_id={"seq": seq_place + RING},
            device_id_type=MESH,
        )

    def line_copy(place):
        return pltpu.make_async_remote_copy(
            src_ref=behind.at[place],
            dst_ref=behind_in.at[place],
            send_sem=line_send.at[place],
            recv_sem=line_recv.at[place],
            device_id={"seq": seq_place - RING},
            device_id_type=MESH,
        )

    def own_weight_copies(head):
        wide = 2 * HEAD_WIDTH
        query_cols = pl.ds(head * wide, wide)
        kv_span = pl.ds(head * HEAD_WIDTH, HEAD_WIDTH)
        return [
            pltpu.make_async_copy(source, target, own_weight_sem.at[head, index])
            for index, (source, target) in enumerate(
                (
                    (w_query_ref.at[:, query_cols], weights.at[head, :, pl.ds(0, wide)]),
                    (key_weight_ref.at[:, kv_span], weights.at[head, :, pl.ds(wide, HEAD_WIDTH)]),
                    (
                        value_weight_ref.at[:, kv_span],
                        weights.at[head, :, pl.ds(wide + HEAD_WIDTH, HEAD_WIDTH)],
                    ),
                )
            )
        ]

    def weight_copy(head):
        return pltpu.make_async_remote_copy(
            src_ref=weights.at[head],
            dst_ref=weights_in.at[head],
            send_sem=weight_send.at[head],
            recv_sem=weight_recv.at[head],
            device_id={"seq": paired},
            device_id_type=MESH,
        )

    def both(ref, place):
        block = ref[place * rows : (place + 1) * rows]
        return jnp.concatenate([block[:, :HEAD_WIDTH], block[:, HEAD_WIDTH:]], axis=0)

    def attend(place):
        query = both(queries, place)
        grad = both(grads, place)
        reach = slice(place * rows, place * rows + span + rows)
        key = keys[reach]
        value = values[reach]
        scores = lax.dot_general(query, key, NT, preferred_element_type=jnp.float32)
        mask = jnp.concatenate([bias[place], bias[place]], axis=0)
        scores = scores * scaling + mask
        raised = jnp.exp(scores - jnp.max(scores, axis=1, keepdims=True))
        weights_full = raised * (1.0 / jnp.sum(raised, axis=1, keepdims=True))
        weights_half = weights_full.astype(jnp.bfloat16)
        attended = jnp.dot(weights_half, value, preferred_element_type=jnp.float32)
        delta = jnp.sum(grad.astype(jnp.float32) * attended, axis=1, keepdims=True)
        grad_weights = lax.dot_general(grad, value, NT, preferred_element_type=jnp.float32)
        grad_scores = (weights_full * (grad_weights - delta)).astype(jnp.bfloat16)
        grad_query = jnp.dot(grad_scores, key, preferred_element_type=jnp.float32) * scaling
        grad_query = grad_query.astype(jnp.bfloat16)
        here = slice(place * rows, (place + 1) * rows)
        held[0, 0, turn, here, :HEAD_WIDTH] = grad_query[:rows]
        held[0, 0, turn, here, HEAD_WIDTH:] = grad_query[rows:]
        terms = (
            lax.dot_general(grad_scores, query, TN, preferred_element_type=jnp.float32) * scaling,
            lax.dot_general(weights_half, grad, TN, preferred_element_type=jnp.float32),
        )
        for kind in (0, 1):
            if place == 0:
                sums[kind, reach] = terms[kind]
            else:
                sums[kind, place * rows : place * rows + span] += terms[kind][:span]
                sums[kind, place * rows + span : place * rows + span + rows] = terms[kind][span:]

        @pl.when(run > 0)
        def _():
            behind[place] = sums[:, here].astype(jnp.bfloat16)
            line_copy(place).start()

    def collect(place):
        @pl.when(run < RING - 1)
        def _():
            line_copy(place).wait_recv()
            there = slice(span + place * rows, span + (place + 1) * rows)
            sums[:, there] += behind_in[place].astype(jnp.float32)

    def across_copy(piece):
        return pltpu.make_async_remote_copy(
            src_ref=held.at[piece, 0, turn],
            dst_ref=held.at[piece, 1, turn],
            send_sem=across_send.at[piece],
            recv_sem=across_recv.at[piece],
            device_id={"seq": opposite},
            device_id_type=MESH,
        )

    def ring_copy(shard, to, send, recv):
        return pltpu.make_async_remote_copy(
            src_ref=shard,
            dst_ref=shard,
            send_sem=send,
            recv_sem=recv,
            device_id={"seq": to},
            device_id_type=MESH,
        )

    def shard_of(piece, line, step):
        return held.at[piece, line, lax.rem(turn + step + RING, RING)]

    def half_of(piece, line, step, start):
        return held.at[piece, line, lax.rem(turn + step + RING, RING), pl.ds(start, half)]

    def right_copy(piece, line, step=0):
        return ring_copy(
            shard_of(piece, line, step), right, right_send.at[piece, line], right_recv.at[piece, line]
        )

    def left_copy(piece, line, step=0):
        return ring_copy(
            shard_of(piece, line, step), left, left_send.at[piece, line], left_recv.at[piece, line]
        )

    def far_right_copy(piece, line, step=-1):
        return ring_copy(
            half_of(piece, line, step, 0),
            right,
            far_right_send.at[piece, line],
            far_right_recv.at[piece, line],
        )

    def far_left_copy(piece, line, step=1):
        return ring_copy(
            half_of(piece, line, step, half),
            left,
            far_left_send.at[piece, line],
            far_left_recv.at[piece, line],
        )

    def along_ring(piece, line):
        right_copy(piece, line).start()
        left_copy(piece, line).start()

    def spread(piece):
        across_copy(piece).start()
        along_ring(piece, 0)

    def from_across(piece):
        across_copy(piece).wait_recv()
        along_ring(piece, 1)

    def farther(piece, line):
        right_copy(piece, line, -1).wait_recv()
        far_right_copy(piece, line).start()
        left_copy(piece, line, 1).wait_recv()
        far_left_copy(piece, line).start()

    def last_of(piece, line):
        far_right_copy(piece, line, -2).wait_recv()
        far_left_copy(piece, line, 2).wait_recv()

    def core_copy(unit):
        return pltpu.make_async_remote_copy(
            src_ref=part.at[unit, 1 - core],
            dst_ref=part_in.at[unit],
            send_sem=core_send.at[unit],
            recv_sem=core_recv.at[unit],
            device_id={"mp": 1 - core},
            device_id_type=MESH,
        )

    def section_copy(unit):
        line, owner = divmod(unit, 2)
        row = opposite_run if line else run
        return pltpu.make_async_remote_copy(
            src_ref=ready.at[unit],
            dst_ref=landed.at[row],
            send_sem=section_send.at[unit],
            recv_sem=section_recv.at[row],
            device_id={"section": back_section, "seq": paired if owner else seq_place},
            device_id_type=MESH,
        )

    def goes_up(unit, origin):
        return (origin == 3) | ((origin == 1) & (unit == 1))

    def relay_copy(unit):
        return pltpu.make_async_remote_copy(
            src_ref=ready.at[unit],
            dst_ref=relayed.at[unit // 2],
            send_sem=section_send.at[unit],
            recv_sem=relay_recv.at[unit // 2],
            device_id=at(first_column, ahead),
            device_id_type=MESH,
        )

    def forward_copy(unit):
        row = run if unit // 2 else opposite_run
        return pltpu.make_async_remote_copy(
            src_ref=relayed.at[unit // 2],
            dst_ref=landed.at[row],
            send_sem=forward_send.at[unit // 2],
            recv_sem=section_recv.at[row],
            device_id=at(column, after_relay),
            device_id_type=MESH,
        )

    def forward(unit):
        @pl.when(goes_up(unit, opposite_run))
        def _():
            relay_copy(unit).wait_recv()
            forward_copy(unit).start()

    def land(row):
        pltpu.make_async_remote_copy(
            src_ref=landed.at[row],
            dst_ref=landed.at[row],
            send_sem=forward_send.at[0],
            recv_sem=section_recv.at[row],
            device_id={"section": back_section},
            device_id_type=MESH,
        ).wait_recv()
        out_ref[pl.ds(pl.multiple_of(row * span, span), span), :] = jnp.transpose(landed[row])

    def project(unit):
        line, owner = divmod(unit, 2)
        source = weights_in if owner else weights
        product = None
        for head in range(RING):
            for piece in range(PIECES):
                weight = source[head, :, piece * 2 * HEAD_WIDTH : (piece + 1) * 2 * HEAD_WIDTH]
                term = lax.dot_general(
                    weight, held[piece, line, head], NT, preferred_element_type=jnp.float32
                )
                product = term if product is None else product + term
        part[unit, 0] = product[:width]
        part[unit, 1] = product[width:]
        core_copy(unit).start()

    def hand_over(unit):
        core_copy(unit).wait_recv()
        ready[unit] = (part[unit, core] + part_in[unit]).astype(jnp.bfloat16)
        if unit % 2 == 0:
            section_copy(unit).start()
        else:

            @pl.when(goes_up(unit, run))
            def _():
                relay_copy(unit).start()

            @pl.when(jnp.logical_not(goes_up(unit, run)))
            def _():
                section_copy(unit).start()

    for head in range(RING):
        for copy in own_weight_copies(head):
            copy.start()
    for kind in range(4):
        own_copy(kind).start()
    pl.semaphore_wait(barrier, peers)
    order = (1, 3, 2)
    for step in order:
        for kind in (0, 1):
            swap_copy(kind, step).start()

    @pl.when(run < RING - 1)
    def _():
        for kind in (0, 1):
            halo_copy(kind, 0).start()

    for step in order:
        for kind in (2, 3):
            swap_copy(kind, step).start()

    @pl.when(odd)
    def _():
        for head in range(EARLY_ODD):
            for copy in own_weight_copies(head):
                copy.wait()
            weight_copy(head).start()

    query_row = lax.broadcasted_iota(jnp.int32, (rows, rows), 0)
    key_row = lax.broadcasted_iota(jnp.int32, (rows, rows), 1)

    def block_docs(place):
        start = pl.multiple_of(jnp.maximum(place, 0) * rows, rows)
        return docs_ref[:, pl.ds(start, rows)].astype(jnp.float32)

    for place in range(RING):
        query_place = run * RING + place
        query_docs = jnp.transpose(jnp.broadcast_to(block_docs(query_place), (rows, rows)))
        for step in range(RING + 1):
            offset = query_row - key_row + step * rows
            allowed = (query_docs == block_docs(query_place - step)) & (offset >= 0)
            allowed = allowed & (offset < WINDOW)
            allowed = allowed & (jnp.full((rows, rows), query_place, jnp.int32) >= step)
            first = (RING - step) * rows
            bias[place, :, first : first + rows] = jnp.where(allowed, 0.0, -jnp.inf)

    @pl.when(run == 0)
    def _():
        for buffer in (keys, values):
            buffer[:span] = jnp.zeros((span, HEAD_WIDTH), jnp.bfloat16)

    for step in order:
        for kind in (0, 1):
            swap_copy(kind, step).wait_recv()

        @pl.when(run < RING - 1)
        def _():
            for kind in (0, 1):
                halo_copy(kind, step).start()

    @pl.when(jnp.logical_not(odd))
    def _():
        for head in range(EARLY_EVEN):
            for copy in own_weight_copies(head):
                copy.wait()
            weight_copy(head).start()

    for kind in range(4):
        own_copy(kind).wait()
    for step in order:
        for kind in (2, 3):
            swap_copy(kind, step).wait_recv()

    @pl.when(run > 0)
    def _():
        for step in range(RING):
            for kind in (0, 1):
                halo_copy(kind, step).wait_recv()

    for place in range(RING):
        attend(place)
    spread(0)
    for place in range(RING):
        collect(place)
    for kind in (0, 1):
        first = kind * HEAD_WIDTH
        held[1, 0, turn, :, first : first + HEAD_WIDTH] = sums[kind, span:].astype(jnp.bfloat16)
    spread(1)

    @pl.when(odd)
    def _():
        for head in range(EARLY_ODD, RING):
            for copy in own_weight_copies(head):
                copy.wait()
            weight_copy(head).start()

    @pl.when(jnp.logical_not(odd))
    def _():
        for head in range(EARLY_EVEN, RING):
            for copy in own_weight_copies(head):
                copy.wait()
            weight_copy(head).start()


    farther(0, 0)
    from_across(0)
    farther(1, 0)
    for piece in range(PIECES):
        last_of(piece, 0)
    project(0)
    farther(0, 1)
    from_across(1)
    hand_over(0)
    for head in range(RING):
        weight_copy(head).wait_recv()
    project(1)
    farther(1, 1)
    hand_over(1)
    for piece in range(PIECES):
        last_of(piece, 1)
    project(3)
    project(2)
    hand_over(3)
    hand_over(2)
    forward(1)
    forward(3)
    for row in (run, opposite_run, paired_run, lax.rem(paired_run + 2, RING)):
        land(row)

    for unit in range(4):
        core_copy(unit).wait_send()
        section_copy(unit).wait_send()

    for unit in (1, 3):

        @pl.when(goes_up(unit, opposite_run))
        def _():
            forward_copy(unit).wait_send()

    for piece in range(PIECES):
        across_copy(piece).wait_send()
        for line in (0, 1):
            right_copy(piece, line).wait_send()
            left_copy(piece, line).wait_send()
            far_right_copy(piece, line).wait_send()
            far_left_copy(piece, line).wait_send()
    for head in range(RING):
        weight_copy(head).wait_send()
    for kind in range(4):
        for step in near:
            swap_copy(kind, step).wait_send()

    @pl.when(run < RING - 1)
    def _():
        for kind in (0, 1):
            for step in range(RING):
                halo_copy(kind, step).wait_send()

    @pl.when(run > 0)
    def _():
        for place in range(RING):
            line_copy(place).wait_send()


def cascade(docs, query, key, value, grad, w_query, key_weight, value_weight):
    rows = query.shape[0]
    seq_count = lax.axis_size("seq")
    width = w_query.shape[0] // 2
    span = RING * rows
    wide = 2 * HEAD_WIDTH
    dma = pltpu.SemaphoreType.DMA
    whole = pl.BlockSpec(memory_space=pltpu.VMEM)
    stay = pl.BlockSpec(memory_space=pl.ANY)
    return pl.pallas_call(
        cascade_kernel,
        out_shape=jax.ShapeDtypeStruct((seq_count * rows, width), jnp.bfloat16),
        in_specs=[whole] + [stay] * 7,
        out_specs=whole,
        scratch_shapes=[
            pltpu.VMEM((2 * span, HEAD_WIDTH), jnp.bfloat16),
            pltpu.VMEM((2 * span, HEAD_WIDTH), jnp.bfloat16),
            pltpu.VMEM((span, wide), jnp.bfloat16),
            pltpu.VMEM((span, wide), jnp.bfloat16),
            pltpu.VMEM((RING, rows, span + rows), jnp.float32),
            pltpu.VMEM((2, 2 * span, HEAD_WIDTH), jnp.float32),
            pltpu.VMEM((RING, 2, rows, HEAD_WIDTH), jnp.bfloat16),
            pltpu.VMEM((RING, 2, rows, HEAD_WIDTH), jnp.bfloat16),
            pltpu.VMEM((RING, 2 * width, 2 * wide), jnp.bfloat16),
            pltpu.VMEM((RING, 2 * width, 2 * wide), jnp.bfloat16),
            pltpu.VMEM((PIECES, 2, RING, span, wide), jnp.bfloat16),
            pltpu.VMEM((4, 2, width, span), jnp.float32),
            pltpu.VMEM((4, width, span), jnp.float32),
            pltpu.VMEM((4, width, span), jnp.bfloat16),
            pltpu.VMEM((2, width, span), jnp.bfloat16),
            pltpu.VMEM((RING, width, span), jnp.bfloat16),
            dma((4,)),
            dma((RING, 3)),
            dma((4, RING - 1)),
            dma((4, RING - 1)),
            dma((2, RING)),
            dma((2, RING)),
            *([dma((RING,))] * 4),
            *([dma((PIECES,))] * 2),
            *([dma((PIECES, 2))] * 8),
            *([dma((4,))] * 4),
            *([dma((2,))] * 2),
        ],
        compiler_params=pltpu.CompilerParams(collective_id=0, has_side_effects=True),
    )(docs, query, key, value, grad, w_query, key_weight, value_weight)


def per_device(
    query_rows,
    key_row_matrix,
    value_row_matrix,
    out_grad,
    w_query,
    key_weight,
    value_weight,
    doc_ids,
):
    upstream = cascade(
        doc_ids,
        query_rows[0],
        key_row_matrix[0],
        value_row_matrix[0],
        out_grad[0],
        w_query[0],
        key_weight[0],
        value_weight[0],
    )
    return upstream[None]


def solution(mesh):
    placed = (
        P("section", "seq", "mp"),
        P("section", "seq", "mp"),
        P("section", "seq", "mp"),
        P("section", "seq", "mp"),
        P("section", "seq", "mp"),
        P("section", "seq", "mp"),
        P("section", "seq", "mp"),
        P("section", None),
    )
    return jax.shard_map(
        per_device,
        mesh=mesh,
        in_specs=placed,
        out_specs=P("section", None, ("seq", "mp")),
        check_vma=False,
    )
```

```python
import math

import jax
import jax.numpy as jnp
from jax import lax
from jax.experimental import pallas as pl
from jax.experimental.pallas import tpu as pltpu
from jax.sharding import PartitionSpec as P

HEAD_WIDTH = 128
WINDOW = 512
RING = 4
LEG = 6
MESH = pl.DeviceIdType.MESH
NT = (((1,), (1,)), ((), ()))
TN = (((0,), (0,)), ((), ()))
PIECES = 2
EARLY_EVEN = 4
EARLY_ODD = 2


def signal(semaphore, device):
    pl.semaphore_signal(semaphore, inc=1, device_id=device, device_id_type=MESH)


def cascade_kernel(
    docs_ref,
    query_ref,
    key_ref,
    value_ref,
    grad_ref,
    w_query_ref,
    key_weight_ref,
    value_weight_ref,
    out_ref,
    keys,
    values,
    queries,
    grads,
    bias,
    sums,
    behind,
    behind_in,
    weights,
    weights_in,
    held,
    part,
    part_in,
    ready,
    relayed,
    landed,
    own_sem,
    own_weight_sem,
    swap_send,
    swap_recv,
    halo_send,
    halo_recv,
    line_send,
    line_recv,
    weight_send,
    weight_recv,
    across_send,
    across_recv,
    right_send,
    right_recv,
    left_send,
    left_recv,
    far_right_send,
    far_right_recv,
    far_left_send,
    far_left_recv,
    core_send,
    core_recv,
    section_send,
    section_recv,
    relay_recv,
    forward_send,
):
    seq_place = lax.axis_index("seq")
    core = lax.axis_index("mp")
    section = lax.axis_index("section")
    section_count = lax.axis_size("section")
    run = seq_place // RING
    turn = lax.rem(seq_place, RING)
    column = section // RING
    block = lax.rem(section, RING)
    rows = query_ref.shape[0]
    span = RING * rows
    half = span // 2
    width = w_query_ref.shape[0] // 2
    scaling = 1.0 / math.sqrt(HEAD_WIDTH)
    near = range(1, RING)

    right = run * RING + lax.rem(turn + 1, RING)
    left = run * RING + lax.rem(turn + RING - 1, RING)
    paired_run = run + 1 - 2 * lax.rem(run, 2)
    paired = paired_run * RING + turn
    opposite_run = lax.rem(run + 2, RING)
    opposite = opposite_run * RING + turn
    back_section = lax.rem(section + section_count - 1, section_count)
    next_section = lax.rem(section + 1, section_count)

    depth = RING * RING
    along = block * RING + run
    odd = lax.rem(run, 2) == 1
    ahead = lax.rem(along + LEG, depth)
    before = lax.rem(along + depth - LEG, depth)
    after_relay = lax.rem(along + LEG - 1, depth)
    before_relay = lax.rem(along + depth - LEG + 1, depth)

    def at(col, place):
        return {"section": col * RING + place // RING, "seq": lax.rem(place, RING) * RING + turn}

    first_column = lax.rem(column + RING - (block == 0).astype(jnp.int32), RING)
    source_column = lax.rem(column + (before < RING).astype(jnp.int32), RING)

    barrier = pltpu.get_barrier_semaphore()
    for step in near:
        signal(barrier, {"seq": run * RING + lax.rem(turn + step, RING)})
    signal(barrier, {"seq": opposite})
    signal(barrier, {"mp": 1 - core})
    for place in (seq_place, paired):
        signal(barrier, {"section": back_section, "seq": place})
        signal(barrier, {"section": next_section, "seq": place})

    @pl.when(odd)
    def _():
        signal(barrier, at(first_column, ahead))
        signal(barrier, at(source_column, before))
        signal(barrier, at(column, after_relay))

    @pl.when(jnp.logical_not(odd))
    def _():
        signal(barrier, at(column, before_relay))

    @pl.when(run < RING - 1)
    def _():
        signal(barrier, {"seq": seq_place + RING})

    @pl.when(run > 0)
    def _():
        signal(barrier, {"seq": seq_place - RING})

    peers = RING - 1 + 1 + 1 + 4 + 1 + 2 * odd.astype(jnp.int32)
    peers = peers + (run > 0).astype(jnp.int32) + (run < RING - 1).astype(jnp.int32)

    sources = (key_ref, value_ref, query_ref, grad_ref)
    buffers = (keys, values, queries, grads)

    def block_rows(place, first=0):
        return pl.ds(pl.multiple_of(first + place * rows, rows), rows)

    def head_cols(kind, head):
        wide = buffers[kind].shape[1]
        return sources[kind].at[:, pl.ds(pl.multiple_of(head * wide, HEAD_WIDTH), wide)]

    def home(kind):
        return span if kind < 2 else 0

    def own_copy(kind):
        return pltpu.make_async_copy(
            head_cols(kind, turn), buffers[kind].at[block_rows(turn, home(kind))], own_sem.at[kind]
        )

    def swap_copy(kind, step):
        to = lax.rem(turn + step, RING)
        return pltpu.make_async_remote_copy(
            src_ref=head_cols(kind, to),
            dst_ref=buffers[kind].at[block_rows(turn, home(kind))],
            send_sem=swap_send.at[kind, step - 1],
            recv_sem=swap_recv.at[kind, step - 1],
            device_id={"seq": run * RING + to},
            device_id_type=MESH,
        )

    def halo_copy(kind, step):
        place = lax.rem(turn + RING - step, RING)
        return pltpu.make_async_remote_copy(
            src_ref=buffers[kind].at[block_rows(place, span)] if step else head_cols(kind, turn),
            dst_ref=buffers[kind].at[block_rows(place)],
            send_sem=halo_send.at[kind, step],
            recv_sem=halo_recv.at[kind, step],
            device_id={"seq": seq_place + RING},
            device_id_type=MESH,
        )

    def line_copy(place):
        return pltpu.make_async_remote_copy(
            src_ref=behind.at[place],
            dst_ref=behind_in.at[place],
            send_sem=line_send.at[place],
            recv_sem=line_recv.at[place],
            device_id={"seq": seq_place - RING},
            device_id_type=MESH,
        )

    def own_weight_copies(head):
        wide = 2 * HEAD_WIDTH
        query_cols = pl.ds(head * wide, wide)
        kv_span = pl.ds(head * HEAD_WIDTH, HEAD_WIDTH)
        return [
            pltpu.make_async_copy(source, target, own_weight_sem.at[head, index])
            for index, (source, target) in enumerate(
                (
                    (w_query_ref.at[:, query_cols], weights.at[head, :, pl.ds(0, wide)]),
                    (key_weight_ref.at[:, kv_span], weights.at[head, :, pl.ds(wide, HEAD_WIDTH)]),
                    (
                        value_weight_ref.at[:, kv_span],
                        weights.at[head, :, pl.ds(wide + HEAD_WIDTH, HEAD_WIDTH)],
                    ),
                )
            )
        ]

    def weight_copy(head):
        return pltpu.make_async_remote_copy(
            src_ref=weights.at[head],
            dst_ref=weights_in.at[head],
            send_sem=weight_send.at[head],
            recv_sem=weight_recv.at[head],
            device_id={"seq": paired},
            device_id_type=MESH,
        )

    def both(ref, place):
        block = ref[place * rows : (place + 1) * rows]
        return jnp.concatenate([block[:, :HEAD_WIDTH], block[:, HEAD_WIDTH:]], axis=0)

    def attend(place):
        query = both(queries, place)
        grad = both(grads, place)
        reach = slice(place * rows, place * rows + span + rows)
        key = keys[reach]
        value = values[reach]
        scores = lax.dot_general(query, key, NT, preferred_element_type=jnp.float32)
        mask = jnp.concatenate([bias[place], bias[place]], axis=0)
        scores = scores * scaling + mask
        raised = jnp.exp(scores - jnp.max(scores, axis=1, keepdims=True))
        weights_full = raised * (1.0 / jnp.sum(raised, axis=1, keepdims=True))
        weights_half = weights_full.astype(jnp.bfloat16)
        attended = jnp.dot(weights_half, value, preferred_element_type=jnp.float32)
        delta = jnp.sum(grad.astype(jnp.float32) * attended, axis=1, keepdims=True)
        grad_weights = lax.dot_general(grad, value, NT, preferred_element_type=jnp.float32)
        grad_scores = (weights_full * (grad_weights - delta)).astype(jnp.bfloat16)
        grad_query = jnp.dot(grad_scores, key, preferred_element_type=jnp.float32) * scaling
        grad_query = grad_query.astype(jnp.bfloat16)
        here = slice(place * rows, (place + 1) * rows)
        held[0, 0, turn, here, :HEAD_WIDTH] = grad_query[:rows]
        held[0, 0, turn, here, HEAD_WIDTH:] = grad_query[rows:]
        terms = (
            lax.dot_general(grad_scores, query, TN, preferred_element_type=jnp.float32) * scaling,
            lax.dot_general(weights_half, grad, TN, preferred_element_type=jnp.float32),
        )
        for kind in (0, 1):
            if place == 0:
                sums[kind, reach] = terms[kind]
            else:
                sums[kind, place * rows : place * rows + span] += terms[kind][:span]
                sums[kind, place * rows + span : place * rows + span + rows] = terms[kind][span:]

        @pl.when(run > 0)
        def _():
            behind[place] = sums[:, here].astype(jnp.bfloat16)
            line_copy(place).start()

    def collect(place):
        @pl.when(run < RING - 1)
        def _():
            line_copy(place).wait_recv()
            there = slice(span + place * rows, span + (place + 1) * rows)
            sums[:, there] += behind_in[place].astype(jnp.float32)

    def across_copy(piece):
        return pltpu.make_async_remote_copy(
            src_ref=held.at[piece, 0, turn],
            dst_ref=held.at[piece, 1, turn],
            send_sem=across_send.at[piece],
            recv_sem=across_recv.at[piece],
            device_id={"seq": opposite},
            device_id_type=MESH,
        )

    def ring_copy(shard, to, send, recv):
        return pltpu.make_async_remote_copy(
            src_ref=shard,
            dst_ref=shard,
            send_sem=send,
            recv_sem=recv,
            device_id={"seq": to},
            device_id_type=MESH,
        )

    def shard_of(piece, line, step):
        return held.at[piece, line, lax.rem(turn + step + RING, RING)]

    def half_of(piece, line, step, start):
        return held.at[piece, line, lax.rem(turn + step + RING, RING), pl.ds(start, half)]

    def right_copy(piece, line, step=0):
        return ring_copy(
            shard_of(piece, line, step), right, right_send.at[piece, line], right_recv.at[piece, line]
        )

    def left_copy(piece, line, step=0):
        return ring_copy(
            shard_of(piece, line, step), left, left_send.at[piece, line], left_recv.at[piece, line]
        )

    def far_right_copy(piece, line, step=-1):
        return ring_copy(
            half_of(piece, line, step, 0),
            right,
            far_right_send.at[piece, line],
            far_right_recv.at[piece, line],
        )

    def far_left_copy(piece, line, step=1):
        return ring_copy(
            half_of(piece, line, step, half),
            left,
            far_left_send.at[piece, line],
            far_left_recv.at[piece, line],
        )

    def along_ring(piece, line):
        right_copy(piece, line).start()
        left_copy(piece, line).start()

    def spread(piece):
        across_copy(piece).start()
        along_ring(piece, 0)

    def from_across(piece):
        across_copy(piece).wait_recv()
        along_ring(piece, 1)

    def farther(piece, line):
        right_copy(piece, line, -1).wait_recv()
        far_right_copy(piece, line).start()
        left_copy(piece, line, 1).wait_recv()
        far_left_copy(piece, line).start()

    def last_of(piece, line):
        far_right_copy(piece, line, -2).wait_recv()
        far_left_copy(piece, line, 2).wait_recv()

    def core_copy(unit):
        return pltpu.make_async_remote_copy(
            src_ref=part.at[unit, 1 - core],
            dst_ref=part_in.at[unit],
            send_sem=core_send.at[unit],
            recv_sem=core_recv.at[unit],
            device_id={"mp": 1 - core},
            device_id_type=MESH,
        )

    def section_copy(unit):
        line, owner = divmod(unit, 2)
        row = opposite_run if line else run
        return pltpu.make_async_remote_copy(
            src_ref=ready.at[unit],
            dst_ref=landed.at[row],
            send_sem=section_send.at[unit],
            recv_sem=section_recv.at[row],
            device_id={"section": back_section, "seq": paired if owner else seq_place},
            device_id_type=MESH,
        )

    def goes_up(unit, origin):
        return (origin == 3) | ((origin == 1) & (unit == 1))

    def relay_copy(unit):
        return pltpu.make_async_remote_copy(
            src_ref=ready.at[unit],
            dst_ref=relayed.at[unit // 2],
            send_sem=section_send.at[unit],
            recv_sem=relay_recv.at[unit // 2],
            device_id=at(first_column, ahead),
            device_id_type=MESH,
        )

    def forward_copy(unit):
        row = run if unit // 2 else opposite_run
        return pltpu.make_async_remote_copy(
            src_ref=relayed.at[unit // 2],
            dst_ref=landed.at[row],
            send_sem=forward_send.at[unit // 2],
            recv_sem=section_recv.at[row],
            device_id=at(column, after_relay),
            device_id_type=MESH,
        )

    def forward(unit):
        @pl.when(goes_up(unit, opposite_run))
        def _():
            relay_copy(unit).wait_recv()
            forward_copy(unit).start()

    def land(row):
        pltpu.make_async_remote_copy(
            src_ref=landed.at[row],
            dst_ref=landed.at[row],
            send_sem=forward_send.at[0],
            recv_sem=section_recv.at[row],
            device_id={"section": back_section},
            device_id_type=MESH,
        ).wait_recv()
        out_ref[pl.ds(pl.multiple_of(row * span, span), span), :] = jnp.transpose(landed[row])

    def project(unit):
        line, owner = divmod(unit, 2)
        source = weights_in if owner else weights
        product = None
        for head in range(RING):
            for piece in range(PIECES):
                weight = source[head, :, piece * 2 * HEAD_WIDTH : (piece + 1) * 2 * HEAD_WIDTH]
                term = lax.dot_general(
                    weight, held[piece, line, head], NT, preferred_element_type=jnp.float32
                )
                product = term if product is None else product + term
        part[unit, 0] = product[:width]
        part[unit, 1] = product[width:]
        core_copy(unit).start()

    def hand_over(unit):
        core_copy(unit).wait_recv()
        ready[unit] = (part[unit, core] + part_in[unit]).astype(jnp.bfloat16)
        if unit % 2 == 0:
            section_copy(unit).start()
        else:

            @pl.when(goes_up(unit, run))
            def _():
                relay_copy(unit).start()

            @pl.when(jnp.logical_not(goes_up(unit, run)))
            def _():
                section_copy(unit).start()

    for head in range(RING):
        for copy in own_weight_copies(head):
            copy.start()
    for kind in range(4):
        own_copy(kind).start()
    pl.semaphore_wait(barrier, peers)
    order = (1, 3, 2)
    for step in order:
        for kind in (0, 1):
            swap_copy(kind, step).start()

    @pl.when(run < RING - 1)
    def _():
        for kind in (0, 1):
            halo_copy(kind, 0).start()

    for step in order:
        for kind in (2, 3):
            swap_copy(kind, step).start()

    @pl.when(odd)
    def _():
        for head in range(EARLY_ODD):
            for copy in own_weight_copies(head):
                copy.wait()
            weight_copy(head).start()

    query_row = lax.broadcasted_iota(jnp.int32, (rows, rows), 0)
    key_row = lax.broadcasted_iota(jnp.int32, (rows, rows), 1)

    def block_docs(place):
        start = pl.multiple_of(jnp.maximum(place, 0) * rows, rows)
        return docs_ref[:, pl.ds(start, rows)].astype(jnp.float32)

    for place in range(RING):
        query_place = run * RING + place
        query_docs = jnp.transpose(jnp.broadcast_to(block_docs(query_place), (rows, rows)))
        for step in range(RING + 1):
            offset = query_row - key_row + step * rows
            allowed = (query_docs == block_docs(query_place - step)) & (offset >= 0)
            allowed = allowed & (offset < WINDOW)
            allowed = allowed & (jnp.full((rows, rows), query_place, jnp.int32) >= step)
            first = (RING - step) * rows
            bias[place, :, first : first + rows] = jnp.where(allowed, 0.0, -jnp.inf)

    @pl.when(run == 0)
    def _():
        for buffer in (keys, values):
            buffer[:span] = jnp.zeros((span, HEAD_WIDTH), jnp.bfloat16)

    for step in order:
        for kind in (0, 1):
            swap_copy(kind, step).wait_recv()

        @pl.when(run < RING - 1)
        def _():
            for kind in (0, 1):
                halo_copy(kind, step).start()

    @pl.when(jnp.logical_not(odd))
    def _():
        for head in range(EARLY_EVEN):
            for copy in own_weight_copies(head):
                copy.wait()
            weight_copy(head).start()

    for kind in range(4):
        own_copy(kind).wait()
    for step in order:
        for kind in (2, 3):
            swap_copy(kind, step).wait_recv()

    @pl.when(run > 0)
    def _():
        for step in range(RING):
            for kind in (0, 1):
                halo_copy(kind, step).wait_recv()

    for place in range(RING):
        attend(place)
    spread(0)
    for place in range(RING):
        collect(place)
    for kind in (0, 1):
        first = kind * HEAD_WIDTH
        held[1, 0, turn, :, first : first + HEAD_WIDTH] = sums[kind, span:].astype(jnp.bfloat16)
    spread(1)

    @pl.when(odd)
    def _():
        for head in range(EARLY_ODD, RING):
            for copy in own_weight_copies(head):
                copy.wait()
            weight_copy(head).start()

    @pl.when(jnp.logical_not(odd))
    def _():
        for head in range(EARLY_EVEN, RING):
            for copy in own_weight_copies(head):
                copy.wait()
            weight_copy(head).start()


    farther(0, 0)
    from_across(0)
    farther(1, 0)
    for piece in range(PIECES):
        last_of(piece, 0)
    project(0)
    farther(0, 1)
    from_across(1)
    hand_over(0)
    for head in range(RING):
        weight_copy(head).wait_recv()
    project(1)
    farther(1, 1)
    hand_over(1)
    for piece in range(PIECES):
        last_of(piece, 1)
    project(2)
    hand_over(2)
    project(3)
    hand_over(3)
    forward(1)
    forward(3)
    for row in (run, opposite_run, paired_run, lax.rem(paired_run + 2, RING)):
        land(row)

    for unit in range(4):
        core_copy(unit).wait_send()
        section_copy(unit).wait_send()

    for unit in (1, 3):

        @pl.when(goes_up(unit, opposite_run))
        def _():
            forward_copy(unit).wait_send()

    for piece in range(PIECES):
        across_copy(piece).wait_send()
        for line in (0, 1):
            right_copy(piece, line).wait_send()
            left_copy(piece, line).wait_send()
            far_right_copy(piece, line).wait_send()
            far_left_copy(piece, line).wait_send()
    for head in range(RING):
        weight_copy(head).wait_send()
    for kind in range(4):
        for step in near:
            swap_copy(kind, step).wait_send()

    @pl.when(run < RING - 1)
    def _():
        for kind in (0, 1):
            for step in range(RING):
                halo_copy(kind, step).wait_send()

    @pl.when(run > 0)
    def _():
        for place in range(RING):
            line_copy(place).wait_send()


def cascade(docs, query, key, value, grad, w_query, key_weight, value_weight):
    rows = query.shape[0]
    seq_count = lax.axis_size("seq")
    width = w_query.shape[0] // 2
    span = RING * rows
    wide = 2 * HEAD_WIDTH
    dma = pltpu.SemaphoreType.DMA
    whole = pl.BlockSpec(memory_space=pltpu.VMEM)
    stay = pl.BlockSpec(memory_space=pl.ANY)
    return pl.pallas_call(
        cascade_kernel,
        out_shape=jax.ShapeDtypeStruct((seq_count * rows, width), jnp.bfloat16),
        in_specs=[whole] + [stay] * 7,
        out_specs=whole,
        scratch_shapes=[
            pltpu.VMEM((2 * span, HEAD_WIDTH), jnp.bfloat16),
            pltpu.VMEM((2 * span, HEAD_WIDTH), jnp.bfloat16),
            pltpu.VMEM((span, wide), jnp.bfloat16),
            pltpu.VMEM((span, wide), jnp.bfloat16),
            pltpu.VMEM((RING, rows, span + rows), jnp.float32),
            pltpu.VMEM((2, 2 * span, HEAD_WIDTH), jnp.float32),
            pltpu.VMEM((RING, 2, rows, HEAD_WIDTH), jnp.bfloat16),
            pltpu.VMEM((RING, 2, rows, HEAD_WIDTH), jnp.bfloat16),
            pltpu.VMEM((RING, 2 * width, 2 * wide), jnp.bfloat16),
            pltpu.VMEM((RING, 2 * width, 2 * wide), jnp.bfloat16),
            pltpu.VMEM((PIECES, 2, RING, span, wide), jnp.bfloat16),
            pltpu.VMEM((4, 2, width, span), jnp.float32),
            pltpu.VMEM((4, width, span), jnp.float32),
            pltpu.VMEM((4, width, span), jnp.bfloat16),
            pltpu.VMEM((2, width, span), jnp.bfloat16),
            pltpu.VMEM((RING, width, span), jnp.bfloat16),
            dma((4,)),
            dma((RING, 3)),
            dma((4, RING - 1)),
            dma((4, RING - 1)),
            dma((2, RING)),
            dma((2, RING)),
            *([dma((RING,))] * 4),
            *([dma((PIECES,))] * 2),
            *([dma((PIECES, 2))] * 8),
            *([dma((4,))] * 4),
            *([dma((2,))] * 2),
        ],
        compiler_params=pltpu.CompilerParams(collective_id=0, has_side_effects=True),
    )(docs, query, key, value, grad, w_query, key_weight, value_weight)


def per_device(
    query_rows,
    key_row_matrix,
    value_row_matrix,
    out_grad,
    w_query,
    key_weight,
    value_weight,
    doc_ids,
):
    upstream = cascade(
        doc_ids,
        query_rows[0],
        key_row_matrix[0],
        value_row_matrix[0],
        out_grad[0],
        w_query[0],
        key_weight[0],
        value_weight[0],
    )
    return upstream[None]


def solution(mesh):
    placed = (
        P("section", "seq", "mp"),
        P("section", "seq", "mp"),
        P("section", "seq", "mp"),
        P("section", "seq", "mp"),
        P("section", "seq", "mp"),
        P("section", "seq", "mp"),
        P("section", "seq", "mp"),
        P("section", None),
    )
    return jax.shard_map(
        per_device,
        mesh=mesh,
        in_specs=placed,
        out_specs=P("section", None, ("seq", "mp")),
        check_vma=False,
    )
```

```python
import math

import jax
import jax.numpy as jnp
from jax import lax
from jax.experimental import pallas as pl
from jax.experimental.pallas import tpu as pltpu
from jax.sharding import PartitionSpec as P

HEAD_WIDTH = 128
WINDOW = 512
RING = 4
LEG = 6
MESH = pl.DeviceIdType.MESH
NT = (((1,), (1,)), ((), ()))
TN = (((0,), (0,)), ((), ()))
PIECES = 2
EARLY_EVEN = 4
EARLY_ODD = 2


def signal(semaphore, device):
    pl.semaphore_signal(semaphore, inc=1, device_id=device, device_id_type=MESH)


def cascade_kernel(
    docs_ref,
    query_ref,
    key_ref,
    value_ref,
    grad_ref,
    w_query_ref,
    key_weight_ref,
    value_weight_ref,
    out_ref,
    keys,
    values,
    queries,
    grads,
    bias,
    sums,
    behind,
    behind_in,
    weights,
    weights_in,
    held,
    part,
    part_in,
    ready,
    relayed,
    landed,
    own_sem,
    own_weight_sem,
    swap_send,
    swap_recv,
    halo_send,
    halo_recv,
    line_send,
    line_recv,
    weight_send,
    weight_recv,
    across_send,
    across_recv,
    right_send,
    right_recv,
    left_send,
    left_recv,
    far_right_send,
    far_right_recv,
    far_left_send,
    far_left_recv,
    core_send,
    core_recv,
    section_send,
    section_recv,
    relay_recv,
    forward_send,
):
    seq_place = lax.axis_index("seq")
    core = lax.axis_index("mp")
    section = lax.axis_index("section")
    section_count = lax.axis_size("section")
    run = seq_place // RING
    turn = lax.rem(seq_place, RING)
    column = section // RING
    block = lax.rem(section, RING)
    rows = query_ref.shape[0]
    span = RING * rows
    half = span // 2
    width = w_query_ref.shape[0] // 2
    scaling = 1.0 / math.sqrt(HEAD_WIDTH)
    near = range(1, RING)

    right = run * RING + lax.rem(turn + 1, RING)
    left = run * RING + lax.rem(turn + RING - 1, RING)
    paired_run = run + 1 - 2 * lax.rem(run, 2)
    paired = paired_run * RING + turn
    opposite_run = lax.rem(run + 2, RING)
    opposite = opposite_run * RING + turn
    back_section = lax.rem(section + section_count - 1, section_count)
    next_section = lax.rem(section + 1, section_count)

    depth = RING * RING
    along = block * RING + run
    odd = lax.rem(run, 2) == 1
    ahead = lax.rem(along + LEG, depth)
    before = lax.rem(along + depth - LEG, depth)
    after_relay = lax.rem(along + LEG - 1, depth)
    before_relay = lax.rem(along + depth - LEG + 1, depth)

    def at(col, place):
        return {"section": col * RING + place // RING, "seq": lax.rem(place, RING) * RING + turn}

    first_column = lax.rem(column + RING - (block == 0).astype(jnp.int32), RING)
    source_column = lax.rem(column + (before < RING).astype(jnp.int32), RING)

    barrier = pltpu.get_barrier_semaphore()
    for step in near:
        signal(barrier, {"seq": run * RING + lax.rem(turn + step, RING)})
    signal(barrier, {"seq": opposite})
    signal(barrier, {"mp": 1 - core})
    for place in (seq_place, paired):
        signal(barrier, {"section": back_section, "seq": place})
        signal(barrier, {"section": next_section, "seq": place})

    @pl.when(odd)
    def _():
        signal(barrier, at(first_column, ahead))
        signal(barrier, at(source_column, before))
        signal(barrier, at(column, after_relay))

    @pl.when(jnp.logical_not(odd))
    def _():
        signal(barrier, at(column, before_relay))

    @pl.when(run < RING - 1)
    def _():
        signal(barrier, {"seq": seq_place + RING})

    @pl.when(run > 0)
    def _():
        signal(barrier, {"seq": seq_place - RING})

    peers = RING - 1 + 1 + 1 + 4 + 1 + 2 * odd.astype(jnp.int32)
    peers = peers + (run > 0).astype(jnp.int32) + (run < RING - 1).astype(jnp.int32)

    sources = (key_ref, value_ref, query_ref, grad_ref)
    buffers = (keys, values, queries, grads)

    def block_rows(place, first=0):
        return pl.ds(pl.multiple_of(first + place * rows, rows), rows)

    def head_cols(kind, head):
        wide = buffers[kind].shape[1]
        return sources[kind].at[:, pl.ds(pl.multiple_of(head * wide, HEAD_WIDTH), wide)]

    def home(kind):
        return span if kind < 2 else 0

    def own_copy(kind):
        return pltpu.make_async_copy(
            head_cols(kind, turn), buffers[kind].at[block_rows(turn, home(kind))], own_sem.at[kind]
        )

    def swap_copy(kind, step):
        to = lax.rem(turn + step, RING)
        return pltpu.make_async_remote_copy(
            src_ref=head_cols(kind, to),
            dst_ref=buffers[kind].at[block_rows(turn, home(kind))],
            send_sem=swap_send.at[kind, step - 1],
            recv_sem=swap_recv.at[kind, step - 1],
            device_id={"seq": run * RING + to},
            device_id_type=MESH,
        )

    def halo_copy(kind, step):
        place = lax.rem(turn + RING - step, RING)
        return pltpu.make_async_remote_copy(
            src_ref=buffers[kind].at[block_rows(place, span)] if step else head_cols(kind, turn),
            dst_ref=buffers[kind].at[block_rows(place)],
            send_sem=halo_send.at[kind, step],
            recv_sem=halo_recv.at[kind, step],
            device_id={"seq": seq_place + RING},
            device_id_type=MESH,
        )

    def line_copy(place):
        return pltpu.make_async_remote_copy(
            src_ref=behind.at[place],
            dst_ref=behind_in.at[place],
            send_sem=line_send.at[place],
            recv_sem=line_recv.at[place],
            device_id={"seq": seq_place - RING},
            device_id_type=MESH,
        )

    def own_weight_copies(head):
        wide = 2 * HEAD_WIDTH
        query_cols = pl.ds(head * wide, wide)
        kv_span = pl.ds(head * HEAD_WIDTH, HEAD_WIDTH)
        return [
            pltpu.make_async_copy(source, target, own_weight_sem.at[head, index])
            for index, (source, target) in enumerate(
                (
                    (w_query_ref.at[:, query_cols], weights.at[head, :, pl.ds(0, wide)]),
                    (key_weight_ref.at[:, kv_span], weights.at[head, :, pl.ds(wide, HEAD_WIDTH)]),
                    (
                        value_weight_ref.at[:, kv_span],
                        weights.at[head, :, pl.ds(wide + HEAD_WIDTH, HEAD_WIDTH)],
                    ),
                )
            )
        ]

    def weight_copy(head):
        return pltpu.make_async_remote_copy(
            src_ref=weights.at[head],
            dst_ref=weights_in.at[head],
            send_sem=weight_send.at[head],
            recv_sem=weight_recv.at[head],
            device_id={"seq": paired},
            device_id_type=MESH,
        )

    def both(ref, place):
        block = ref[place * rows : (place + 1) * rows]
        return jnp.concatenate([block[:, :HEAD_WIDTH], block[:, HEAD_WIDTH:]], axis=0)

    def attend(place):
        query = both(queries, place)
        grad = both(grads, place)
        reach = slice(place * rows, place * rows + span + rows)
        key = keys[reach]
        value = values[reach]
        scores = lax.dot_general(query, key, NT, preferred_element_type=jnp.float32)
        mask = jnp.concatenate([bias[place], bias[place]], axis=0)
        scores = scores * scaling + mask
        raised = jnp.exp(scores - jnp.max(scores, axis=1, keepdims=True))
        weights_full = raised * (1.0 / jnp.sum(raised, axis=1, keepdims=True))
        weights_half = weights_full.astype(jnp.bfloat16)
        attended = jnp.dot(weights_half, value, preferred_element_type=jnp.float32)
        delta = jnp.sum(grad.astype(jnp.float32) * attended, axis=1, keepdims=True)
        grad_weights = lax.dot_general(grad, value, NT, preferred_element_type=jnp.float32)
        grad_scores = (weights_full * (grad_weights - delta)).astype(jnp.bfloat16)
        grad_query = jnp.dot(grad_scores, key, preferred_element_type=jnp.float32) * scaling
        grad_query = grad_query.astype(jnp.bfloat16)
        here = slice(place * rows, (place + 1) * rows)
        held[0, 0, turn, here, :HEAD_WIDTH] = grad_query[:rows]
        held[0, 0, turn, here, HEAD_WIDTH:] = grad_query[rows:]
        terms = (
            lax.dot_general(grad_scores, query, TN, preferred_element_type=jnp.float32) * scaling,
            lax.dot_general(weights_half, grad, TN, preferred_element_type=jnp.float32),
        )
        for kind in (0, 1):
            if place == 0:
                sums[kind, reach] = terms[kind]
            else:
                sums[kind, place * rows : place * rows + span] += terms[kind][:span]
                sums[kind, place * rows + span : place * rows + span + rows] = terms[kind][span:]

        @pl.when(run > 0)
        def _():
            behind[place] = sums[:, here].astype(jnp.bfloat16)
            line_copy(place).start()

    def collect(place):
        @pl.when(run < RING - 1)
        def _():
            line_copy(place).wait_recv()
            there = slice(span + place * rows, span + (place + 1) * rows)
            sums[:, there] += behind_in[place].astype(jnp.float32)

    def across_copy(piece):
        return pltpu.make_async_remote_copy(
            src_ref=held.at[piece, 0, turn],
            dst_ref=held.at[piece, 1, turn],
            send_sem=across_send.at[piece],
            recv_sem=across_recv.at[piece],
            device_id={"seq": opposite},
            device_id_type=MESH,
        )

    def ring_copy(shard, to, send, recv):
        return pltpu.make_async_remote_copy(
            src_ref=shard,
            dst_ref=shard,
            send_sem=send,
            recv_sem=recv,
            device_id={"seq": to},
            device_id_type=MESH,
        )

    def shard_of(piece, line, step):
        return held.at[piece, line, lax.rem(turn + step + RING, RING)]

    def half_of(piece, line, step, start):
        return held.at[piece, line, lax.rem(turn + step + RING, RING), pl.ds(start, half)]

    def right_copy(piece, line, step=0):
        return ring_copy(
            shard_of(piece, line, step), right, right_send.at[piece, line], right_recv.at[piece, line]
        )

    def left_copy(piece, line, step=0):
        return ring_copy(
            shard_of(piece, line, step), left, left_send.at[piece, line], left_recv.at[piece, line]
        )

    def far_right_copy(piece, line, step=-1):
        return ring_copy(
            half_of(piece, line, step, 0),
            right,
            far_right_send.at[piece, line],
            far_right_recv.at[piece, line],
        )

    def far_left_copy(piece, line, step=1):
        return ring_copy(
            half_of(piece, line, step, half),
            left,
            far_left_send.at[piece, line],
            far_left_recv.at[piece, line],
        )

    def along_ring(piece, line):
        right_copy(piece, line).start()
        left_copy(piece, line).start()

    def spread(piece):
        across_copy(piece).start()
        along_ring(piece, 0)

    def from_across(piece):
        across_copy(piece).wait_recv()
        along_ring(piece, 1)

    def farther(piece, line):
        right_copy(piece, line, -1).wait_recv()
        far_right_copy(piece, line).start()
        left_copy(piece, line, 1).wait_recv()
        far_left_copy(piece, line).start()

    def last_of(piece, line):
        far_right_copy(piece, line, -2).wait_recv()
        far_left_copy(piece, line, 2).wait_recv()

    def core_copy(unit):
        return pltpu.make_async_remote_copy(
            src_ref=part.at[unit, 1 - core],
            dst_ref=part_in.at[unit],
            send_sem=core_send.at[unit],
            recv_sem=core_recv.at[unit],
            device_id={"mp": 1 - core},
            device_id_type=MESH,
        )

    def section_copy(unit):
        line, owner = divmod(unit, 2)
        row = opposite_run if line else run
        return pltpu.make_async_remote_copy(
            src_ref=ready.at[unit],
            dst_ref=landed.at[row],
            send_sem=section_send.at[unit],
            recv_sem=section_recv.at[row],
            device_id={"section": back_section, "seq": paired if owner else seq_place},
            device_id_type=MESH,
        )

    def goes_up(unit, origin):
        return (origin == 3) | ((origin == 1) & (unit == 1))

    def relay_copy(unit):
        return pltpu.make_async_remote_copy(
            src_ref=ready.at[unit],
            dst_ref=relayed.at[unit // 2],
            send_sem=section_send.at[unit],
            recv_sem=relay_recv.at[unit // 2],
            device_id=at(first_column, ahead),
            device_id_type=MESH,
        )

    def forward_copy(unit):
        row = run if unit // 2 else opposite_run
        return pltpu.make_async_remote_copy(
            src_ref=relayed.at[unit // 2],
            dst_ref=landed.at[row],
            send_sem=forward_send.at[unit // 2],
            recv_sem=section_recv.at[row],
            device_id=at(column, after_relay),
            device_id_type=MESH,
        )

    def forward(unit):
        @pl.when(goes_up(unit, opposite_run))
        def _():
            relay_copy(unit).wait_recv()
            forward_copy(unit).start()

    def land(row):
        pltpu.make_async_remote_copy(
            src_ref=landed.at[row],
            dst_ref=landed.at[row],
            send_sem=forward_send.at[0],
            recv_sem=section_recv.at[row],
            device_id={"section": back_section},
            device_id_type=MESH,
        ).wait_recv()
        out_ref[pl.ds(pl.multiple_of(row * span, span), span), :] = jnp.transpose(landed[row])

    def project(unit):
        line, owner = divmod(unit, 2)
        source = weights_in if owner else weights
        product = None
        for head in range(RING):
            for piece in range(PIECES):
                weight = source[head, :, piece * 2 * HEAD_WIDTH : (piece + 1) * 2 * HEAD_WIDTH]
                term = lax.dot_general(
                    weight, held[piece, line, head], NT, preferred_element_type=jnp.float32
                )
                product = term if product is None else product + term
        part[unit, 0] = product[:width]
        part[unit, 1] = product[width:]
        core_copy(unit).start()

    def hand_over(unit):
        core_copy(unit).wait_recv()
        ready[unit] = (part[unit, core] + part_in[unit]).astype(jnp.bfloat16)
        if unit % 2 == 0:
            section_copy(unit).start()
        else:

            @pl.when(goes_up(unit, run))
            def _():
                relay_copy(unit).start()

            @pl.when(jnp.logical_not(goes_up(unit, run)))
            def _():
                section_copy(unit).start()

    for head in range(RING):
        for copy in own_weight_copies(head):
            copy.start()
    for kind in range(4):
        own_copy(kind).start()
    pl.semaphore_wait(barrier, peers)
    order = (1, 3, 2)
    for step in order:
        for kind in (0, 1):
            swap_copy(kind, step).start()

    @pl.when(run < RING - 1)
    def _():
        for kind in (0, 1):
            halo_copy(kind, 0).start()

    for step in order:
        for kind in (2, 3):
            swap_copy(kind, step).start()

    @pl.when(odd)
    def _():
        for head in range(EARLY_ODD):
            for copy in own_weight_copies(head):
                copy.wait()
            weight_copy(head).start()

    query_row = lax.broadcasted_iota(jnp.int32, (rows, rows), 0)
    key_row = lax.broadcasted_iota(jnp.int32, (rows, rows), 1)

    def block_docs(place):
        start = pl.multiple_of(jnp.maximum(place, 0) * rows, rows)
        return docs_ref[:, pl.ds(start, rows)].astype(jnp.float32)

    for place in range(RING):
        query_place = run * RING + place
        query_docs = jnp.transpose(jnp.broadcast_to(block_docs(query_place), (rows, rows)))
        for step in range(RING + 1):
            offset = query_row - key_row + step * rows
            allowed = (query_docs == block_docs(query_place - step)) & (offset >= 0)
            allowed = allowed & (offset < WINDOW)
            allowed = allowed & (jnp.full((rows, rows), query_place, jnp.int32) >= step)
            first = (RING - step) * rows
            bias[place, :, first : first + rows] = jnp.where(allowed, 0.0, -jnp.inf)

    @pl.when(run == 0)
    def _():
        for buffer in (keys, values):
            buffer[:span] = jnp.zeros((span, HEAD_WIDTH), jnp.bfloat16)

    for step in order:
        for kind in (0, 1):
            swap_copy(kind, step).wait_recv()

        @pl.when(run < RING - 1)
        def _():
            for kind in (0, 1):
                halo_copy(kind, step).start()

    @pl.when(jnp.logical_not(odd))
    def _():
        for head in range(EARLY_EVEN):
            for copy in own_weight_copies(head):
                copy.wait()
            weight_copy(head).start()

    for kind in range(4):
        own_copy(kind).wait()
    for step in order:
        for kind in (2, 3):
            swap_copy(kind, step).wait_recv()

    @pl.when(run > 0)
    def _():
        for step in range(RING):
            for kind in (0, 1):
                halo_copy(kind, step).wait_recv()

    for place in range(RING):
        attend(place)
    spread(0)
    for place in range(RING):
        collect(place)
    for kind in (0, 1):
        first = kind * HEAD_WIDTH
        held[1, 0, turn, :, first : first + HEAD_WIDTH] = sums[kind, span:].astype(jnp.bfloat16)
    spread(1)

    @pl.when(odd)
    def _():
        for head in range(EARLY_ODD, RING):
            for copy in own_weight_copies(head):
                copy.wait()
            weight_copy(head).start()

    @pl.when(jnp.logical_not(odd))
    def _():
        for head in range(EARLY_EVEN, RING):
            for copy in own_weight_copies(head):
                copy.wait()
            weight_copy(head).start()


    farther(0, 0)
    from_across(0)
    farther(1, 0)
    for piece in range(PIECES):
        last_of(piece, 0)
    farther(0, 1)
    project(0)
    from_across(1)
    hand_over(0)
    for head in range(RING):
        weight_copy(head).wait_recv()
    project(1)
    farther(1, 1)
    hand_over(1)
    for piece in range(PIECES):
        last_of(piece, 1)
    project(2)
    hand_over(2)
    project(3)
    hand_over(3)
    forward(1)
    forward(3)
    for row in (run, opposite_run, paired_run, lax.rem(paired_run + 2, RING)):
        land(row)

    for unit in range(4):
        core_copy(unit).wait_send()
        section_copy(unit).wait_send()

    for unit in (1, 3):

        @pl.when(goes_up(unit, opposite_run))
        def _():
            forward_copy(unit).wait_send()

    for piece in range(PIECES):
        across_copy(piece).wait_send()
        for line in (0, 1):
            right_copy(piece, line).wait_send()
            left_copy(piece, line).wait_send()
            far_right_copy(piece, line).wait_send()
            far_left_copy(piece, line).wait_send()
    for head in range(RING):
        weight_copy(head).wait_send()
    for kind in range(4):
        for step in near:
            swap_copy(kind, step).wait_send()

    @pl.when(run < RING - 1)
    def _():
        for kind in (0, 1):
            for step in range(RING):
                halo_copy(kind, step).wait_send()

    @pl.when(run > 0)
    def _():
        for place in range(RING):
            line_copy(place).wait_send()


def cascade(docs, query, key, value, grad, w_query, key_weight, value_weight):
    rows = query.shape[0]
    seq_count = lax.axis_size("seq")
    width = w_query.shape[0] // 2
    span = RING * rows
    wide = 2 * HEAD_WIDTH
    dma = pltpu.SemaphoreType.DMA
    whole = pl.BlockSpec(memory_space=pltpu.VMEM)
    stay = pl.BlockSpec(memory_space=pl.ANY)
    return pl.pallas_call(
        cascade_kernel,
        out_shape=jax.ShapeDtypeStruct((seq_count * rows, width), jnp.bfloat16),
        in_specs=[whole] + [stay] * 7,
        out_specs=whole,
        scratch_shapes=[
            pltpu.VMEM((2 * span, HEAD_WIDTH), jnp.bfloat16),
            pltpu.VMEM((2 * span, HEAD_WIDTH), jnp.bfloat16),
            pltpu.VMEM((span, wide), jnp.bfloat16),
            pltpu.VMEM((span, wide), jnp.bfloat16),
            pltpu.VMEM((RING, rows, span + rows), jnp.float32),
            pltpu.VMEM((2, 2 * span, HEAD_WIDTH), jnp.float32),
            pltpu.VMEM((RING, 2, rows, HEAD_WIDTH), jnp.bfloat16),
            pltpu.VMEM((RING, 2, rows, HEAD_WIDTH), jnp.bfloat16),
            pltpu.VMEM((RING, 2 * width, 2 * wide), jnp.bfloat16),
            pltpu.VMEM((RING, 2 * width, 2 * wide), jnp.bfloat16),
            pltpu.VMEM((PIECES, 2, RING, span, wide), jnp.bfloat16),
            pltpu.VMEM((4, 2, width, span), jnp.float32),
            pltpu.VMEM((4, width, span), jnp.float32),
            pltpu.VMEM((4, width, span), jnp.bfloat16),
            pltpu.VMEM((2, width, span), jnp.bfloat16),
            pltpu.VMEM((RING, width, span), jnp.bfloat16),
            dma((4,)),
            dma((RING, 3)),
            dma((4, RING - 1)),
            dma((4, RING - 1)),
            dma((2, RING)),
            dma((2, RING)),
            *([dma((RING,))] * 4),
            *([dma((PIECES,))] * 2),
            *([dma((PIECES, 2))] * 8),
            *([dma((4,))] * 4),
            *([dma((2,))] * 2),
        ],
        compiler_params=pltpu.CompilerParams(collective_id=0, has_side_effects=True),
    )(docs, query, key, value, grad, w_query, key_weight, value_weight)


def per_device(
    query_rows,
    key_row_matrix,
    value_row_matrix,
    out_grad,
    w_query,
    key_weight,
    value_weight,
    doc_ids,
):
    upstream = cascade(
        doc_ids,
        query_rows[0],
        key_row_matrix[0],
        value_row_matrix[0],
        out_grad[0],
        w_query[0],
        key_weight[0],
        value_weight[0],
    )
    return upstream[None]


def solution(mesh):
    placed = (
        P("section", "seq", "mp"),
        P("section", "seq", "mp"),
        P("section", "seq", "mp"),
        P("section", "seq", "mp"),
        P("section", "seq", "mp"),
        P("section", "seq", "mp"),
        P("section", "seq", "mp"),
        P("section", None),
    )
    return jax.shard_map(
        per_device,
        mesh=mesh,
        in_specs=placed,
        out_specs=P("section", None, ("seq", "mp")),
        check_vma=False,
    )
```

```python
import math

import jax
import jax.numpy as jnp
from jax import lax
from jax.experimental import pallas as pl
from jax.experimental.pallas import tpu as pltpu
from jax.sharding import PartitionSpec as P

HEAD_WIDTH = 128
WINDOW = 512
RING = 4
LEG = 6
MESH = pl.DeviceIdType.MESH
NT = (((1,), (1,)), ((), ()))
TN = (((0,), (0,)), ((), ()))
PIECES = 2
EARLY_EVEN = 4
EARLY_ODD = 2


def signal(semaphore, device):
    pl.semaphore_signal(semaphore, inc=1, device_id=device, device_id_type=MESH)


def cascade_kernel(
    docs_ref,
    query_ref,
    key_ref,
    value_ref,
    grad_ref,
    w_query_ref,
    key_weight_ref,
    value_weight_ref,
    out_ref,
    keys,
    values,
    queries,
    grads,
    bias,
    sums,
    behind,
    behind_in,
    weights,
    weights_in,
    held,
    part,
    part_in,
    ready,
    relayed,
    landed,
    own_sem,
    own_weight_sem,
    swap_send,
    swap_recv,
    halo_send,
    halo_recv,
    line_send,
    line_recv,
    weight_send,
    weight_recv,
    across_send,
    across_recv,
    right_send,
    right_recv,
    left_send,
    left_recv,
    far_right_send,
    far_right_recv,
    far_left_send,
    far_left_recv,
    core_send,
    core_recv,
    section_send,
    section_recv,
    relay_recv,
    forward_send,
):
    seq_place = lax.axis_index("seq")
    core = lax.axis_index("mp")
    section = lax.axis_index("section")
    section_count = lax.axis_size("section")
    run = seq_place // RING
    turn = lax.rem(seq_place, RING)
    column = section // RING
    block = lax.rem(section, RING)
    rows = query_ref.shape[0]
    span = RING * rows
    half = span // 2
    width = w_query_ref.shape[0] // 2
    scaling = 1.0 / math.sqrt(HEAD_WIDTH)
    near = range(1, RING)

    right = run * RING + lax.rem(turn + 1, RING)
    left = run * RING + lax.rem(turn + RING - 1, RING)
    paired_run = run + 1 - 2 * lax.rem(run, 2)
    paired = paired_run * RING + turn
    opposite_run = lax.rem(run + 2, RING)
    opposite = opposite_run * RING + turn
    back_section = lax.rem(section + section_count - 1, section_count)
    next_section = lax.rem(section + 1, section_count)

    depth = RING * RING
    along = block * RING + run
    odd = lax.rem(run, 2) == 1
    ahead = lax.rem(along + LEG, depth)
    before = lax.rem(along + depth - LEG, depth)
    after_relay = lax.rem(along + LEG - 1, depth)
    before_relay = lax.rem(along + depth - LEG + 1, depth)

    def at(col, place):
        return {"section": col * RING + place // RING, "seq": lax.rem(place, RING) * RING + turn}

    first_column = lax.rem(column + RING - (block == 0).astype(jnp.int32), RING)
    source_column = lax.rem(column + (before < RING).astype(jnp.int32), RING)

    barrier = pltpu.get_barrier_semaphore()
    for step in near:
        signal(barrier, {"seq": run * RING + lax.rem(turn + step, RING)})
    signal(barrier, {"seq": opposite})
    signal(barrier, {"mp": 1 - core})
    for place in (seq_place, paired):
        signal(barrier, {"section": back_section, "seq": place})
        signal(barrier, {"section": next_section, "seq": place})

    @pl.when(odd)
    def _():
        signal(barrier, at(first_column, ahead))
        signal(barrier, at(source_column, before))
        signal(barrier, at(column, after_relay))

    @pl.when(jnp.logical_not(odd))
    def _():
        signal(barrier, at(column, before_relay))

    @pl.when(run < RING - 1)
    def _():
        signal(barrier, {"seq": seq_place + RING})

    @pl.when(run > 0)
    def _():
        signal(barrier, {"seq": seq_place - RING})

    peers = RING - 1 + 1 + 1 + 4 + 1 + 2 * odd.astype(jnp.int32)
    peers = peers + (run > 0).astype(jnp.int32) + (run < RING - 1).astype(jnp.int32)

    sources = (key_ref, value_ref, query_ref, grad_ref)
    buffers = (keys, values, queries, grads)

    def block_rows(place, first=0):
        return pl.ds(pl.multiple_of(first + place * rows, rows), rows)

    def head_cols(kind, head):
        wide = buffers[kind].shape[1]
        return sources[kind].at[:, pl.ds(pl.multiple_of(head * wide, HEAD_WIDTH), wide)]

    def home(kind):
        return span if kind < 2 else 0

    def own_copy(kind):
        return pltpu.make_async_copy(
            head_cols(kind, turn), buffers[kind].at[block_rows(turn, home(kind))], own_sem.at[kind]
        )

    def swap_copy(kind, step):
        to = lax.rem(turn + step, RING)
        return pltpu.make_async_remote_copy(
            src_ref=head_cols(kind, to),
            dst_ref=buffers[kind].at[block_rows(turn, home(kind))],
            send_sem=swap_send.at[kind, step - 1],
            recv_sem=swap_recv.at[kind, step - 1],
            device_id={"seq": run * RING + to},
            device_id_type=MESH,
        )

    def halo_copy(kind, step):
        place = lax.rem(turn + RING - step, RING)
        return pltpu.make_async_remote_copy(
            src_ref=buffers[kind].at[block_rows(place, span)] if step else head_cols(kind, turn),
            dst_ref=buffers[kind].at[block_rows(place)],
            send_sem=halo_send.at[kind, step],
            recv_sem=halo_recv.at[kind, step],
            device_id={"seq": seq_place + RING},
            device_id_type=MESH,
        )

    def line_copy(place):
        return pltpu.make_async_remote_copy(
            src_ref=behind.at[place],
            dst_ref=behind_in.at[place],
            send_sem=line_send.at[place],
            recv_sem=line_recv.at[place],
            device_id={"seq": seq_place - RING},
            device_id_type=MESH,
        )

    def own_weight_copies(head):
        wide = 2 * HEAD_WIDTH
        query_cols = pl.ds(head * wide, wide)
        kv_span = pl.ds(head * HEAD_WIDTH, HEAD_WIDTH)
        return [
            pltpu.make_async_copy(source, target, own_weight_sem.at[head, index])
            for index, (source, target) in enumerate(
                (
                    (w_query_ref.at[:, query_cols], weights.at[head, :, pl.ds(0, wide)]),
                    (key_weight_ref.at[:, kv_span], weights.at[head, :, pl.ds(wide, HEAD_WIDTH)]),
                    (
                        value_weight_ref.at[:, kv_span],
                        weights.at[head, :, pl.ds(wide + HEAD_WIDTH, HEAD_WIDTH)],
                    ),
                )
            )
        ]

    def weight_copy(head):
        return pltpu.make_async_remote_copy(
            src_ref=weights.at[head],
            dst_ref=weights_in.at[head],
            send_sem=weight_send.at[head],
            recv_sem=weight_recv.at[head],
            device_id={"seq": paired},
            device_id_type=MESH,
        )

    def both(ref, place):
        block = ref[place * rows : (place + 1) * rows]
        return jnp.concatenate([block[:, :HEAD_WIDTH], block[:, HEAD_WIDTH:]], axis=0)

    def attend(place):
        query = both(queries, place)
        grad = both(grads, place)
        reach = slice(place * rows, place * rows + span + rows)
        key = keys[reach]
        value = values[reach]
        scores = lax.dot_general(query, key, NT, preferred_element_type=jnp.float32)
        mask = jnp.concatenate([bias[place], bias[place]], axis=0)
        scores = scores * scaling + mask
        raised = jnp.exp(scores - jnp.max(scores, axis=1, keepdims=True))
        weights_full = raised * (1.0 / jnp.sum(raised, axis=1, keepdims=True))
        weights_half = weights_full.astype(jnp.bfloat16)
        attended = jnp.dot(weights_half, value, preferred_element_type=jnp.float32)
        delta = jnp.sum(grad.astype(jnp.float32) * attended, axis=1, keepdims=True)
        grad_weights = lax.dot_general(grad, value, NT, preferred_element_type=jnp.float32)
        grad_scores = (weights_full * (grad_weights - delta)).astype(jnp.bfloat16)
        grad_query = jnp.dot(grad_scores, key, preferred_element_type=jnp.float32) * scaling
        grad_query = grad_query.astype(jnp.bfloat16)
        here = slice(place * rows, (place + 1) * rows)
        held[0, 0, turn, here, :HEAD_WIDTH] = grad_query[:rows]
        held[0, 0, turn, here, HEAD_WIDTH:] = grad_query[rows:]
        terms = (
            lax.dot_general(grad_scores, query, TN, preferred_element_type=jnp.float32) * scaling,
            lax.dot_general(weights_half, grad, TN, preferred_element_type=jnp.float32),
        )
        for kind in (0, 1):
            if place == 0:
                sums[kind, reach] = terms[kind]
            else:
                sums[kind, place * rows : place * rows + span] += terms[kind][:span]
                sums[kind, place * rows + span : place * rows + span + rows] = terms[kind][span:]

        @pl.when(run > 0)
        def _():
            behind[place] = sums[:, here].astype(jnp.bfloat16)
            line_copy(place).start()

    def collect(place):
        @pl.when(run < RING - 1)
        def _():
            line_copy(place).wait_recv()
            there = slice(span + place * rows, span + (place + 1) * rows)
            sums[:, there] += behind_in[place].astype(jnp.float32)

    def across_copy(piece):
        return pltpu.make_async_remote_copy(
            src_ref=held.at[piece, 0, turn],
            dst_ref=held.at[piece, 1, turn],
            send_sem=across_send.at[piece],
            recv_sem=across_recv.at[piece],
            device_id={"seq": opposite},
            device_id_type=MESH,
        )

    def ring_copy(shard, to, send, recv):
        return pltpu.make_async_remote_copy(
            src_ref=shard,
            dst_ref=shard,
            send_sem=send,
            recv_sem=recv,
            device_id={"seq": to},
            device_id_type=MESH,
        )

    def shard_of(piece, line, step):
        return held.at[piece, line, lax.rem(turn + step + RING, RING)]

    def half_of(piece, line, step, start):
        return held.at[piece, line, lax.rem(turn + step + RING, RING), pl.ds(start, half)]

    def right_copy(piece, line, step=0):
        return ring_copy(
            shard_of(piece, line, step), right, right_send.at[piece, line], right_recv.at[piece, line]
        )

    def left_copy(piece, line, step=0):
        return ring_copy(
            shard_of(piece, line, step), left, left_send.at[piece, line], left_recv.at[piece, line]
        )

    def far_right_copy(piece, line, step=-1):
        return ring_copy(
            half_of(piece, line, step, 0),
            right,
            far_right_send.at[piece, line],
            far_right_recv.at[piece, line],
        )

    def far_left_copy(piece, line, step=1):
        return ring_copy(
            half_of(piece, line, step, half),
            left,
            far_left_send.at[piece, line],
            far_left_recv.at[piece, line],
        )

    def along_ring(piece, line):
        right_copy(piece, line).start()
        left_copy(piece, line).start()

    def spread(piece):
        across_copy(piece).start()
        along_ring(piece, 0)

    def from_across(piece):
        across_copy(piece).wait_recv()
        along_ring(piece, 1)

    def farther(piece, line):
        right_copy(piece, line, -1).wait_recv()
        far_right_copy(piece, line).start()
        left_copy(piece, line, 1).wait_recv()
        far_left_copy(piece, line).start()

    def last_of(piece, line):
        far_right_copy(piece, line, -2).wait_recv()
        far_left_copy(piece, line, 2).wait_recv()

    def core_copy(unit):
        return pltpu.make_async_remote_copy(
            src_ref=part.at[unit, 1 - core],
            dst_ref=part_in.at[unit],
            send_sem=core_send.at[unit],
            recv_sem=core_recv.at[unit],
            device_id={"mp": 1 - core},
            device_id_type=MESH,
        )

    def section_copy(unit):
        line, owner = divmod(unit, 2)
        row = opposite_run if line else run
        return pltpu.make_async_remote_copy(
            src_ref=ready.at[unit],
            dst_ref=landed.at[row],
            send_sem=section_send.at[unit],
            recv_sem=section_recv.at[row],
            device_id={"section": back_section, "seq": paired if owner else seq_place},
            device_id_type=MESH,
        )

    def goes_up(unit, origin):
        return (origin == 3) | ((origin == 1) & (unit == 1))

    def relay_copy(unit):
        return pltpu.make_async_remote_copy(
            src_ref=ready.at[unit],
            dst_ref=relayed.at[unit // 2],
            send_sem=section_send.at[unit],
            recv_sem=relay_recv.at[unit // 2],
            device_id=at(first_column, ahead),
            device_id_type=MESH,
        )

    def forward_copy(unit):
        row = run if unit // 2 else opposite_run
        return pltpu.make_async_remote_copy(
            src_ref=relayed.at[unit // 2],
            dst_ref=landed.at[row],
            send_sem=forward_send.at[unit // 2],
            recv_sem=section_recv.at[row],
            device_id=at(column, after_relay),
            device_id_type=MESH,
        )

    def forward(unit):
        @pl.when(goes_up(unit, opposite_run))
        def _():
            relay_copy(unit).wait_recv()
            forward_copy(unit).start()

    def land(row):
        pltpu.make_async_remote_copy(
            src_ref=landed.at[row],
            dst_ref=landed.at[row],
            send_sem=forward_send.at[0],
            recv_sem=section_recv.at[row],
            device_id={"section": back_section},
            device_id_type=MESH,
        ).wait_recv()
        out_ref[pl.ds(pl.multiple_of(row * span, span), span), :] = jnp.transpose(landed[row])

    def project(unit):
        line, owner = divmod(unit, 2)
        source = weights_in if owner else weights
        product = None
        for head in range(RING):
            for piece in range(PIECES):
                weight = source[head, :, piece * 2 * HEAD_WIDTH : (piece + 1) * 2 * HEAD_WIDTH]
                term = lax.dot_general(
                    weight, held[piece, line, head], NT, preferred_element_type=jnp.float32
                )
                product = term if product is None else product + term
        part[unit, 0] = product[:width]
        part[unit, 1] = product[width:]
        core_copy(unit).start()

    def hand_over(unit):
        core_copy(unit).wait_recv()
        ready[unit] = (part[unit, core] + part_in[unit]).astype(jnp.bfloat16)
        if unit % 2 == 0:
            section_copy(unit).start()
        else:

            @pl.when(goes_up(unit, run))
            def _():
                relay_copy(unit).start()

            @pl.when(jnp.logical_not(goes_up(unit, run)))
            def _():
                section_copy(unit).start()

    for head in range(RING):
        for copy in own_weight_copies(head):
            copy.start()
    for kind in range(4):
        own_copy(kind).start()
    pl.semaphore_wait(barrier, peers)
    order = (1, 3, 2)
    for step in order:
        for kind in (0, 1):
            swap_copy(kind, step).start()

    @pl.when(run < RING - 1)
    def _():
        for kind in (0, 1):
            halo_copy(kind, 0).start()

    for step in order:
        for kind in (2, 3):
            swap_copy(kind, step).start()

    @pl.when(odd)
    def _():
        for head in range(EARLY_ODD):
            for copy in own_weight_copies(head):
                copy.wait()
            weight_copy(head).start()

    query_row = lax.broadcasted_iota(jnp.int32, (rows, rows), 0)
    key_row = lax.broadcasted_iota(jnp.int32, (rows, rows), 1)

    def block_docs(place):
        start = pl.multiple_of(jnp.maximum(place, 0) * rows, rows)
        return docs_ref[:, pl.ds(start, rows)].astype(jnp.float32)

    for place in range(RING):
        query_place = run * RING + place
        query_docs = jnp.transpose(jnp.broadcast_to(block_docs(query_place), (rows, rows)))
        for step in range(RING + 1):
            offset = query_row - key_row + step * rows
            allowed = (query_docs == block_docs(query_place - step)) & (offset >= 0)
            allowed = allowed & (offset < WINDOW)
            allowed = allowed & (jnp.full((rows, rows), query_place, jnp.int32) >= step)
            first = (RING - step) * rows
            bias[place, :, first : first + rows] = jnp.where(allowed, 0.0, -jnp.inf)

    @pl.when(run == 0)
    def _():
        for buffer in (keys, values):
            buffer[:span] = jnp.zeros((span, HEAD_WIDTH), jnp.bfloat16)

    for step in order:
        for kind in (0, 1):
            swap_copy(kind, step).wait_recv()

        @pl.when(run < RING - 1)
        def _():
            for kind in (0, 1):
                halo_copy(kind, step).start()

    @pl.when(jnp.logical_not(odd))
    def _():
        for head in range(EARLY_EVEN):
            for copy in own_weight_copies(head):
                copy.wait()
            weight_copy(head).start()

    for kind in range(4):
        own_copy(kind).wait()
    for step in order:
        for kind in (2, 3):
            swap_copy(kind, step).wait_recv()

    @pl.when(run > 0)
    def _():
        for step in range(RING):
            for kind in (0, 1):
                halo_copy(kind, step).wait_recv()

    for place in range(RING):
        attend(place)
    spread(0)
    for place in range(RING):
        collect(place)
    for kind in (0, 1):
        first = kind * HEAD_WIDTH
        held[1, 0, turn, :, first : first + HEAD_WIDTH] = sums[kind, span:].astype(jnp.bfloat16)
    spread(1)

    @pl.when(odd)
    def _():
        for head in range(EARLY_ODD, RING):
            for copy in own_weight_copies(head):
                copy.wait()
            weight_copy(head).start()

    @pl.when(jnp.logical_not(odd))
    def _():
        for head in range(EARLY_EVEN, RING):
            for copy in own_weight_copies(head):
                copy.wait()
            weight_copy(head).start()


    farther(0, 0)
    from_across(0)
    farther(1, 0)
    for piece in range(PIECES):
        last_of(piece, 0)
    project(0)
    farther(0, 1)
    hand_over(0)
    from_across(1)
    for head in range(RING):
        weight_copy(head).wait_recv()
    project(1)
    farther(1, 1)
    hand_over(1)
    for piece in range(PIECES):
        last_of(piece, 1)
    project(2)
    hand_over(2)
    project(3)
    hand_over(3)
    forward(1)
    forward(3)
    for row in (run, opposite_run, paired_run, lax.rem(paired_run + 2, RING)):
        land(row)

    for unit in range(4):
        core_copy(unit).wait_send()
        section_copy(unit).wait_send()

    for unit in (1, 3):

        @pl.when(goes_up(unit, opposite_run))
        def _():
            forward_copy(unit).wait_send()

    for piece in range(PIECES):
        across_copy(piece).wait_send()
        for line in (0, 1):
            right_copy(piece, line).wait_send()
            left_copy(piece, line).wait_send()
            far_right_copy(piece, line).wait_send()
            far_left_copy(piece, line).wait_send()
    for head in range(RING):
        weight_copy(head).wait_send()
    for kind in range(4):
        for step in near:
            swap_copy(kind, step).wait_send()

    @pl.when(run < RING - 1)
    def _():
        for kind in (0, 1):
            for step in range(RING):
                halo_copy(kind, step).wait_send()

    @pl.when(run > 0)
    def _():
        for place in range(RING):
            line_copy(place).wait_send()


def cascade(docs, query, key, value, grad, w_query, key_weight, value_weight):
    rows = query.shape[0]
    seq_count = lax.axis_size("seq")
    width = w_query.shape[0] // 2
    span = RING * rows
    wide = 2 * HEAD_WIDTH
    dma = pltpu.SemaphoreType.DMA
    whole = pl.BlockSpec(memory_space=pltpu.VMEM)
    stay = pl.BlockSpec(memory_space=pl.ANY)
    return pl.pallas_call(
        cascade_kernel,
        out_shape=jax.ShapeDtypeStruct((seq_count * rows, width), jnp.bfloat16),
        in_specs=[whole] + [stay] * 7,
        out_specs=whole,
        scratch_shapes=[
            pltpu.VMEM((2 * span, HEAD_WIDTH), jnp.bfloat16),
            pltpu.VMEM((2 * span, HEAD_WIDTH), jnp.bfloat16),
            pltpu.VMEM((span, wide), jnp.bfloat16),
            pltpu.VMEM((span, wide), jnp.bfloat16),
            pltpu.VMEM((RING, rows, span + rows), jnp.float32),
            pltpu.VMEM((2, 2 * span, HEAD_WIDTH), jnp.float32),
            pltpu.VMEM((RING, 2, rows, HEAD_WIDTH), jnp.bfloat16),
            pltpu.VMEM((RING, 2, rows, HEAD_WIDTH), jnp.bfloat16),
            pltpu.VMEM((RING, 2 * width, 2 * wide), jnp.bfloat16),
            pltpu.VMEM((RING, 2 * width, 2 * wide), jnp.bfloat16),
            pltpu.VMEM((PIECES, 2, RING, span, wide), jnp.bfloat16),
            pltpu.VMEM((4, 2, width, span), jnp.float32),
            pltpu.VMEM((4, width, span), jnp.float32),
            pltpu.VMEM((4, width, span), jnp.bfloat16),
            pltpu.VMEM((2, width, span), jnp.bfloat16),
            pltpu.VMEM((RING, width, span), jnp.bfloat16),
            dma((4,)),
            dma((RING, 3)),
            dma((4, RING - 1)),
            dma((4, RING - 1)),
            dma((2, RING)),
            dma((2, RING)),
            *([dma((RING,))] * 4),
            *([dma((PIECES,))] * 2),
            *([dma((PIECES, 2))] * 8),
            *([dma((4,))] * 4),
            *([dma((2,))] * 2),
        ],
        compiler_params=pltpu.CompilerParams(collective_id=0, has_side_effects=True),
    )(docs, query, key, value, grad, w_query, key_weight, value_weight)


def per_device(
    query_rows,
    key_row_matrix,
    value_row_matrix,
    out_grad,
    w_query,
    key_weight,
    value_weight,
    doc_ids,
):
    upstream = cascade(
        doc_ids,
        query_rows[0],
        key_row_matrix[0],
        value_row_matrix[0],
        out_grad[0],
        w_query[0],
        key_weight[0],
        value_weight[0],
    )
    return upstream[None]


def solution(mesh):
    placed = (
        P("section", "seq", "mp"),
        P("section", "seq", "mp"),
        P("section", "seq", "mp"),
        P("section", "seq", "mp"),
        P("section", "seq", "mp"),
        P("section", "seq", "mp"),
        P("section", "seq", "mp"),
        P("section", None),
    )
    return jax.shard_map(
        per_device,
        mesh=mesh,
        in_specs=placed,
        out_specs=P("section", None, ("seq", "mp")),
        check_vma=False,
    )
```
